32 devices in a mesh: parts: 2 (over y), src: 4 (over z), tile: 2 (over x), row: 2 (over core).
Axes of the slice: x: 2, y: 2, z: 4, core: 2. Of those that a mesh axis runs over, the one named last changes fastest.
Arguments:
- mask_windows: float32 [4, 256, 256], P(('parts', 'tile'), ('src', 'row')), parts along dimension 0, may hold values from -4 to 4
- target_windows: float32 [4, 256, 256], P(('parts', 'tile'), ('src', 'row')), parts along dimension 0, may hold values from 0 to 1
- pupil_bands: int32 [24, 128, 2], P(('parts', 'src')), parts along dimension 0, may hold values from 0 to 128, as said below
- pupil_phase: float32 [24, 128, 128], P(('parts', 'src')), parts along dimension 0, may hold values from -3.140625 to 3.140625
- source_weight: float32 [24], P(('parts', 'src')), parts along dimension 0, may hold values from 0.2 to 1
Outputs:
- mask_grad: float32 [4, 256, 256], P(('parts', 'tile'), ('src', 'row')), parts along dimension 0
- source_grad: float32 [24], P(('parts', 'src')), parts along dimension 0
The draws below stay inside these ranges and needn't reach their ends.
There are 2 independent parts, one for each index of `parts`. The reference program is written for one: setup_inputs(seed, part) draws one part's arguments, and reference() takes and returns one part's arrays. A program takes and returns all parts, laid end to end along the dimension named above; each array names one. Nothing has to cross between parts.
Inputs may be any that keep to these rules, and one draw needn't show every extreme that they name: For every source point and frequency row, pupil_bands[s, kx, 0] <= pupil_bands[s, kx, 1]; a row that passes nothing holds (0, 0).
All inputs are finite; a program needn't handle non-finite values.
Results may differ from the reference program's by a relative error of at most 0.00019.
Values sent between devices are 32-bit elements; how exact they have to be, the bound alone decides.
A program may use at most 64 MiB of HBM per device.

```python
import math
import jax
import jax.numpy as jnp
from jax import lax

M = 256
K = 128
OV = 32
S = 12
W = 2


def draw_pupil_bands(key, part):
    reach_max = 3 * K // 16
    radius = 5 * K // 16
    centre = K // 2
    key_rows, key_cols = jax.random.split(jax.random.fold_in(key, 11))
    shift_rows = jax.random.randint(key_rows, (S,), -reach_max, reach_max + 1)
    shift_cols = jax.random.randint(key_cols, (S,), -reach_max, reach_max + 1)
    shift_cols = shift_cols.at[0].set(reach_max)
    freq_index = jnp.arange(K, dtype=jnp.int32)
    dist_rows = freq_index[None, :] - centre - shift_rows[:, None]
    dist_cols = freq_index[None, :] - centre - shift_cols[:, None]
    inside = dist_rows[:, :, None] * dist_rows[:, :, None] + dist_cols[:, None, :] * dist_cols[:, None, :] <= radius * radius
    inside = inside.astype(jnp.int32)
    band_hi = jnp.max(inside * (freq_index[None, None, :] + 1), axis=2)
    band_lo = jnp.where(band_hi > 0, K - jnp.max(inside * (K - freq_index[None, None, :]), axis=2), 0)
    return jnp.stack([band_lo, band_hi], axis=2).astype(jnp.int32)


def levels(rng, shape, shards, low, high):
    def one(dim, shards_of):
        heights = jax.random.uniform(jax.random.fold_in(jax.random.fold_in(rng, 6), dim), (shards_of,), jnp.float32, low / len(shards), high / len(shards))
        return jnp.repeat(jnp.exp(heights), shape[dim] // shards_of).reshape((-1,) + (1,) * (len(shape) - dim - 1))

    factor_of = one(*shards[0])
    for cut in shards[1:]:
        factor_of = factor_of * one(*cut)
    return factor_of


def scatter_about(own_key, extent, deviation, most, cuts=(), kind=jnp.bfloat16):
    drawn = jax.random.normal(own_key, extent, jnp.float32) * deviation
    if len(cuts) > 0:
        drawn = levels(own_key, extent, cuts, -0.22, 0.18) * drawn
    return jnp.clip(drawn, min=-most, max=most).astype(kind)


def setup_inputs(seed: int = 0, part: int = 0) -> dict:
    keys = jax.random.split(jax.random.key(seed), 6)
    part_keys = jax.random.split(jax.random.fold_in(keys[5], part), 6)
    return {
        "mask_windows": scatter_about(part_keys[0], (W, M, M), 1.0, 4.0, ((0, 2), (1, 8)), jnp.float32),
        "target_windows": jnp.clip(1.0 * jax.random.uniform(part_keys[1], (W, M, M), jnp.float32) ** levels(part_keys[1], (W, M, M), ((0, 2), (1, 8)), -0.2, 0.2), 0.0, 1.0),
        "pupil_bands": draw_pupil_bands(jax.random.fold_in(jax.random.fold_in(keys[5], part), 71), part),
        "pupil_phase": jnp.clip(jax.random.uniform(part_keys[3], (S, K, K), jnp.float32, -3.140625, 3.140625), -3.140625, 3.140625),
        "source_weight": jnp.clip(jnp.exp(math.log(1.0) - 1.609438 * jax.random.uniform(part_keys[4], (S,), jnp.float32) ** levels(part_keys[4], (S,), ((0, 4),), -0.2, 0.2)), 0.2, 1.0),
    }


STEEPNESS = 20.0
THRESHOLD = 0.15
LOSS_SCALE = 32.0


def matmul(left_op, right_op):
    return jnp.dot(left_op, right_op, precision=lax.Precision.HIGHEST, preferred_element_type=jnp.float32)


def wave_tables(positions):
    freq_index = jnp.arange(K, dtype=jnp.int32) - K // 2
    phase_index = (freq_index[:, None] * positions[None, :]) % M
    angles = (2.0 * math.pi / M) * phase_index.astype(jnp.float32)
    return jnp.cos(angles), jnp.sin(angles)


def pupil_gate(pupil_bands, pupil_phase):
    freq_cols = jnp.arange(K, dtype=jnp.int32)
    inside = (freq_cols[None, None, :] >= pupil_bands[:, :, 0:1]) & (freq_cols[None, None, :] < pupil_bands[:, :, 1:2])
    passing = inside.astype(jnp.float32)
    return passing * jnp.cos(pupil_phase), passing * jnp.sin(pupil_phase)


def reference(mask_windows, target_windows, pupil_bands, pupil_phase, source_weight):
    cos_tab, sin_tab = wave_tables(jnp.arange(M, dtype=jnp.int32))
    field_scale = 1.0 / (M * K)
    pupil_real, pupil_imag = pupil_gate(pupil_bands, pupil_phase)
    weights = source_weight / S

    def fields(spec_real, spec_imag, pass_real, pass_imag):
        amp_real = pass_real * spec_real - pass_imag * spec_imag
        amp_imag = pass_imag * spec_real + pass_real * spec_imag
        half_real = matmul(amp_real, cos_tab) - matmul(amp_imag, sin_tab)
        half_imag = matmul(amp_real, sin_tab) + matmul(amp_imag, cos_tab)
        field_real = field_scale * (matmul(cos_tab.T, half_real) - matmul(sin_tab.T, half_imag))
        field_imag = field_scale * (matmul(cos_tab.T, half_imag) + matmul(sin_tab.T, half_real))
        return field_real, field_imag

    def one_window(inputs):
        window, goal_window = inputs
        part_real = matmul(window, cos_tab.T)
        part_imag = -matmul(window, sin_tab.T)
        spec_real = matmul(cos_tab, part_real) + matmul(sin_tab, part_imag)
        spec_imag = matmul(cos_tab, part_imag) - matmul(sin_tab, part_real)

        def add_light(totals, source_in):
            pass_real, pass_imag, weight = source_in
            field_real, field_imag = fields(spec_real, spec_imag, pass_real, pass_imag)
            return totals + weight * (field_real * field_real + field_imag * field_imag), None

        intensity = lax.scan(add_light, jnp.zeros((M, M), jnp.float32), (pupil_real, pupil_imag, weights))[0]
        resist = jax.nn.sigmoid(STEEPNESS * (intensity - THRESHOLD))
        cotangent = LOSS_SCALE * (resist - goal_window) * STEEPNESS * resist * (1.0 - resist)

        def add_back(totals, source_in):
            grad_real, grad_imag = totals
            pass_real, pass_imag, weight = source_in
            field_real, field_imag = fields(spec_real, spec_imag, pass_real, pass_imag)
            back_scale = (2.0 * weight) * cotangent
            back_real = back_scale * field_real
            back_imag = back_scale * field_imag
            adj_real = matmul(cos_tab, back_real) + matmul(sin_tab, back_imag)
            adj_imag = matmul(cos_tab, back_imag) - matmul(sin_tab, back_real)
            amp_grad_real = field_scale * (matmul(adj_real, cos_tab.T) + matmul(adj_imag, sin_tab.T))
            amp_grad_imag = field_scale * (matmul(adj_imag, cos_tab.T) - matmul(adj_real, sin_tab.T))
            grad_real = grad_real + pass_real * amp_grad_real + pass_imag * amp_grad_imag
            grad_imag = grad_imag + pass_real * amp_grad_imag - pass_imag * amp_grad_real
            term_value = jnp.sum(cotangent * (field_real * field_real + field_imag * field_imag))
            return (grad_real, grad_imag), term_value

        zero_spec = jnp.zeros((K, K), jnp.float32)
        grads_pair, source_terms = lax.scan(add_back, (zero_spec, zero_spec), (pupil_real, pupil_imag, weights))
        grad_real, grad_imag = grads_pair
        q_one = matmul(grad_real, cos_tab) - matmul(grad_imag, sin_tab)
        q_two = matmul(grad_real, sin_tab) + matmul(grad_imag, cos_tab)
        grad_window = matmul(cos_tab.T, q_one) - matmul(sin_tab.T, q_two)
        return grad_window, source_terms

    grads, source_terms = lax.map(one_window, (mask_windows, target_windows))
    zero_strip = jnp.zeros((1, M, OV), jnp.float32)
    from_below = jnp.concatenate([zero_strip, grads[:-1, :, M - OV:]], axis=0)
    from_above = jnp.concatenate([grads[1:, :, :OV], zero_strip], axis=0)
    middle = jnp.zeros((W, M, M - 2 * OV), jnp.float32)
    mask_grad = grads + jnp.concatenate([from_below, middle, from_above], axis=2)
    source_grad = jnp.sum(source_terms, axis=0) / (S * M * W)
    return mask_grad, source_grad
```

```python
import functools
import math

import jax
import jax.numpy as jnp
import numpy as np
from jax import lax
from jax.experimental import pallas as pl
from jax.experimental.pallas import tpu as pltpu
from jax.sharding import PartitionSpec as P

M = 256
K = 128
OV = 32


STEEPNESS = 20.0
THRESHOLD = 0.15
LOSS_SCALE = 32.0


def with_halo(block, sides, width):
    for axis, dim in sides:
        count = lax.axis_size(axis)
        forward = [(i, i + 1) for i in range(count - 1)]
        backward = [(target, source) for source, target in forward]
        low = lax.ppermute(
            lax.slice_in_dim(block, block.shape[dim] - width, None, axis=dim), axis, forward
        )
        high = lax.ppermute(lax.slice_in_dim(block, 0, width, axis=dim), axis, backward)
        block = jnp.concatenate([low, block, high], axis=dim)
    return block


def matmul(left_op, right_op):
    return lax.dot_general(
        left_op,
        right_op,
        (((1,), (0,)), ((), ())),
        precision=lax.Precision.HIGHEST,
        preferred_element_type=jnp.float32,
    )


def matmul_tn(left_op, right_op):
    return lax.dot_general(
        left_op,
        right_op,
        (((0,), (0,)), ((), ())),
        precision=lax.Precision.HIGHEST,
        preferred_element_type=jnp.float32,
    )


def matmul_nt(left_op, right_op):
    return lax.dot_general(
        left_op,
        right_op,
        (((1,), (1,)), ((), ())),
        precision=lax.Precision.HIGHEST,
        preferred_element_type=jnp.float32,
    )


def wave_tables(positions):
    freq_index = jnp.arange(K, dtype=jnp.int32) - K // 2
    phase_index = freq_index[:, None] * positions[None, :] % M
    angles = 2.0 * math.pi / M * phase_index.astype(jnp.float32)
    return (jnp.cos(angles), jnp.sin(angles))


def shards_plain(mask_windows, target_windows, pupil_bands, pupil_phase, source_weight):
    src_count = lax.axis_size("src")
    tile_count = lax.axis_size("tile")
    row_count = lax.axis_size("row")
    local_x = mask_windows.shape[1]
    per_device = pupil_phase.shape[0]
    sources = per_device * src_count
    field_scale = 1.0 / (M * K)
    src_id = lax.axis_index("src")
    row_id = lax.axis_index("row")
    x_start = (src_id * row_count + row_id) * local_x
    block_starts = (jnp.arange(src_count, dtype=jnp.int32) * row_count + row_id) * local_x
    row_set = (block_starts[:, None] + jnp.arange(local_x, dtype=jnp.int32)[None, :]).reshape(
        src_count * local_x
    )
    cos_all, sin_all = wave_tables(jnp.arange(M, dtype=jnp.int32))
    cos_set, sin_set = wave_tables(row_set)
    cos_own, sin_own = wave_tables(x_start + jnp.arange(local_x, dtype=jnp.int32))
    window = mask_windows[0]
    goal_block = target_windows[0]
    zero_spec = jnp.zeros((K, K), jnp.float32)
    shard_rows = lax.all_gather(window, ("src", "row"), axis=0, tiled=True)
    part_real = matmul_nt(shard_rows, cos_all)
    part_imag = -matmul_nt(shard_rows, sin_all)
    spec_real = matmul(cos_all, part_real) + matmul(sin_all, part_imag)
    spec_imag = matmul(cos_all, part_imag) - matmul(sin_all, part_real)
    freq_cols = jnp.arange(K, dtype=jnp.int32)
    inside = (freq_cols[None, None, :] >= pupil_bands[:, :, 0:1]) & (
        freq_cols[None, None, :] < pupil_bands[:, :, 1:2]
    )
    passing = inside.astype(jnp.float32)
    pupil_real = passing * jnp.cos(pupil_phase)
    pupil_imag = passing * jnp.sin(pupil_phase)
    amp_real = (pupil_real * spec_real - pupil_imag * spec_imag).reshape(per_device * K, K)
    amp_imag = (pupil_imag * spec_real + pupil_real * spec_imag).reshape(per_device * K, K)
    half_real = (matmul(amp_real, cos_all) - matmul(amp_imag, sin_all)).reshape(per_device, K, M)
    half_imag = (matmul(amp_real, sin_all) + matmul(amp_imag, cos_all)).reshape(per_device, K, M)
    weights = source_weight / sources

    def fields(pair_in):
        one_real, one_imag = pair_in
        field_real = field_scale * (matmul_tn(cos_set, one_real) - matmul_tn(sin_set, one_imag))
        field_imag = field_scale * (matmul_tn(cos_set, one_imag) + matmul_tn(sin_set, one_real))
        return (field_real, field_imag)

    stack_real, stack_imag = lax.map(fields, (half_real, half_imag))
    part_real = stack_real
    part_imag = stack_imag
    intensity = lax.psum_scatter(
        jnp.sum(weights[:, None, None] * (part_real * part_real + part_imag * part_imag), axis=0),
        "src",
        scatter_dimension=0,
        tiled=True,
    )
    resist = jax.nn.sigmoid(STEEPNESS * (intensity - THRESHOLD))
    cotangent = LOSS_SCALE * (resist - goal_block) * STEEPNESS * resist * (1.0 - resist)
    cotangent_all = lax.all_gather(cotangent, "src", axis=0, tiled=True)
    source_ids = jnp.arange(per_device, dtype=jnp.int32)

    def add_back(source_id, totals):
        grad_real, grad_imag, source_terms = totals
        field_real = stack_real[source_id]
        field_imag = stack_imag[source_id]
        back_scale = 2.0 * weights[source_id] * cotangent_all
        back_real = back_scale * field_real
        back_imag = back_scale * field_imag
        adj_real = matmul(cos_set, back_real) + matmul(sin_set, back_imag)
        adj_imag = matmul(cos_set, back_imag) - matmul(sin_set, back_real)
        amp_grad_real = field_scale * (matmul_nt(adj_real, cos_all) + matmul_nt(adj_imag, sin_all))
        amp_grad_imag = field_scale * (matmul_nt(adj_imag, cos_all) - matmul_nt(adj_real, sin_all))
        pass_real = pupil_real[source_id]
        pass_imag = pupil_imag[source_id]
        grad_real = grad_real + pass_real * amp_grad_real + pass_imag * amp_grad_imag
        grad_imag = grad_imag + pass_real * amp_grad_imag - pass_imag * amp_grad_real
        term_value = jnp.sum(cotangent_all * (field_real * field_real + field_imag * field_imag))
        source_terms = source_terms + jnp.where(source_ids == source_id, term_value, 0.0)
        return (grad_real, grad_imag, source_terms)

    grad_real, grad_imag, source_terms = lax.fori_loop(
        0, per_device, add_back, (zero_spec, zero_spec, jnp.zeros((per_device,), jnp.float32))
    )
    grad_real, grad_imag = lax.psum((grad_real, grad_imag), ("src", "row"))
    source_sum = lax.psum(source_terms, ("tile", "row"))
    source_grad = source_sum / (sources * M * tile_count)
    q_one = matmul(grad_real, cos_all) - matmul(grad_imag, sin_all)
    q_two = matmul(grad_real, sin_all) + matmul(grad_imag, cos_all)
    grad_block = matmul_tn(cos_own, q_one) - matmul_tn(sin_own, q_two)
    padded = with_halo(grad_block, (("tile", 1),), OV)
    from_below = padded[:, :OV]
    from_above = padded[:, M + OV :]
    middle = jnp.zeros((local_x, M - 2 * OV), jnp.float32)
    grad_block = grad_block + jnp.concatenate([from_below, middle, from_above], axis=1)
    return (grad_block[None], source_grad)


MESH = pl.DeviceIdType.MESH


def pair(values):
    high = values.astype(jnp.bfloat16)
    return high, (values - high.astype(jnp.float32)).astype(jnp.bfloat16)


def dot_pair(left_op, right_op, contract_right=0):
    dims = (((1,), (contract_right,)), ((), ()))

    def one(a, b):
        return lax.dot_general(a, b, dims, preferred_element_type=jnp.float32)

    (left_high, left_low), (right_high, right_low) = left_op, right_op
    return one(left_high, right_high) + (
        one(left_high, right_low) + one(left_low, right_high)
    )


def frequency_order(freqs):
    half = freqs // 2
    return np.concatenate([np.arange(half), [-half], -np.arange(1, half)])


def wave_constants(pixels, freqs, blocks, src_count, local_x, fold):
    half = freqs // 2
    spots = np.arange(pixels)

    def waves(index):
        angles = 2.0 * np.pi / pixels * (np.outer(index, spots) % pixels)
        return np.cos(angles), np.sin(angles)

    cos_x, sin_x = waves(np.arange(freqs) - half)
    order = frequency_order(freqs)
    cos_y, sin_y = waves(order)
    spectrum = np.concatenate([cos_x, -sin_x], axis=0)
    wave_y = np.block([[cos_y, sin_y], [-sin_y, cos_y]])
    real_rows = np.concatenate([cos_x.T, -sin_x.T], axis=1)
    imag_rows = np.concatenate([sin_x.T, cos_x.T], axis=1)
    wave_rows = np.stack(
        [one.reshape(blocks, local_x, 2 * freqs) for one in (real_rows, imag_rows)], axis=1
    )
    sets = []
    for own in range(blocks):
        src, row = own // 2, own % 2
        mate = (src + src_count // 2) % src_count * 2 + 1 - row
        rows = np.concatenate([np.arange(local_x) + one * local_x for one in (own, mate)])
        c, s = cos_x[:, rows], sin_x[:, rows]
        sets.append(np.block([[c, s], [-s, c]]))
    packed = np.concatenate([cos_y[:half], -sin_y[half:]], axis=0).T
    edges = []
    for start in (pixels - OV, 0):
        table = np.zeros((fold, 2 * freqs, fold, OV))
        for group in range(fold):
            table[group, :freqs, group] = packed[start : start + OV].T
            table[group, freqs + half, group] = cos_y[half, start : start + OV]
        edges.append(table.reshape(fold * 2 * freqs, freqs))
    move = np.zeros((freqs, freqs))
    move[order + half, np.arange(freqs)] = 1.0
    return (
        split_constant(packed),
        split_constant(spectrum),
        split_constant(wave_y),
        split_constant(wave_rows),
        split_constant(np.stack(sets), 1),
        split_constant(np.stack(edges), 1),
        move.astype(jnp.bfloat16),
    )


def split_constant(values, axis=0):
    values = values.astype(np.float32)
    high = values.astype(jnp.bfloat16)
    low = (values - high.astype(np.float32)).astype(jnp.bfloat16)
    return np.stack([high, low], axis=axis)


def sine_cosine(phase):
    quarter = 0.25 * phase
    square = quarter * quarter
    sine = 1.0 / 362880.0
    for term in (-1.0 / 5040.0, 1.0 / 120.0, -1.0 / 6.0, 1.0):
        sine = sine * square + term
    sine = sine * quarter
    fall = -1.0 / 40320.0
    for term in (1.0 / 720.0, -1.0 / 24.0, 0.5):
        fall = fall * square + term
    cosine = 1.0 - fall * square
    twice = 2.0 * sine
    sine, cosine = twice * cosine, 1.0 - twice * sine
    twice = 2.0 * sine
    return twice * cosine, 1.0 - twice * sine


def dot_exact(left_op, right_op, dims=(((1,), (0,)), ((), ()))):
    high, low = pair(left_op)

    def one(a):
        return lax.dot_general(a, right_op, dims, preferred_element_type=jnp.float32)

    return one(high) + one(low)


def kernel(
    src_count,
    tile_count,
    wm_hbm,
    wf_hbm,
    wy_hbm,
    wb_hbm,
    wx_hbm,
    we_hbm,
    move_hbm,
    mask_hbm,
    goal_hbm,
    band_hbm,
    phase_hbm,
    weight_hbm,
    out_ref,
    terms_ref,
    wm_ref,
    wf_ref,
    wy_ref,
    wb_ref,
    wx_ref,
    we_ref,
    move_ref,
    mask_ref,
    goal_ref,
    band_ref,
    phase_ref,
    weight_ref,
    load_sems,
    mbuf,
    pupil_ref,
    fbuf,
    ubuf,
    meta_ref,
    goals_ref,
    part_send,
    part_recv,
    tsend,
    trecv,
    csend,
    crecv,
    gsend,
    grecv,
    hsend,
    hrecv,
    mask_ss,
    mask_rs,
    fwd_ss,
    fwd_rs,
    meta_ss,
    meta_rs,
    phase_ss,
    phase_rs,
    pfwd_ss,
    pfwd_rs,
    goal_ss,
    goal_rs,
    part_ss,
    part_rs,
    core_ss,
    core_rs,
    grad_ss,
    grad_rs,
    halo_ss,
    halo_rs,
):
    part = lax.axis_index("parts")
    src = lax.axis_index("src")
    tile = lax.axis_index("tile")
    row = lax.axis_index("row")
    local_x, pixels = mask_ref.shape[1:]
    per_device, half, freqs = phase_ref.shape[1], phase_ref.shape[3], phase_ref.shape[4]
    sources = per_device * src_count
    field_scale = 1.0 / (pixels * freqs)
    fold = freqs // OV
    depth = local_x // fold
    other_row = 1 - row
    other_tile = 1 - tile
    last = src_count - 1
    own_slot = src * 2 + row
    mate_src = lax.rem(src + src_count // 2, src_count)
    mate_slot = mate_src * 2 + other_row
    pool_src = src + 1 - 2 * lax.rem(src, 2)

    def far(step):
        up = last - src
        side = lax.div(up + last - step, src_count)
        return side * (last - step) + (1 - side) * (step - up)

    far_first = [far(step) for step in range(last)]
    near_first = far_first[::-1]

    def to(src_ref, dst_ref, ss, rs, src_at=src, tile_at=tile, row_at=other_row):
        return pltpu.make_async_remote_copy(
            src_ref=src_ref,
            dst_ref=dst_ref,
            send_sem=ss,
            recv_sem=rs,
            device_id=(part, src_at, tile_at, row_at),
            device_id_type=MESH,
        )

    barrier = pltpu.get_barrier_semaphore()
    peers = [(peer, tile, other_row) for peer in far_first]
    peers += [(peer, other_tile, other_row) for peer in far_first]
    peers += [(src, tile, other_row), (src, other_tile, row)]
    for src_at, tile_at, row_at in peers:
        pl.semaphore_signal(
            barrier, inc=1, device_id=(part, src_at, tile_at, row_at), device_id_type=MESH
        )

    loads = {}
    for index, (name, source, target) in enumerate(
        [
            ("mask", mask_hbm, mask_ref),
            ("wm", wm_hbm, wm_ref),
            ("weight", weight_hbm, weight_ref),
            ("band", band_hbm, band_ref),
            ("phase", phase_hbm, phase_ref.at[0]),
            ("goal", goal_hbm, goal_ref),
            ("move", move_hbm, move_ref),
            ("wf", wf_hbm, wf_ref),
            ("wb", wb_hbm, wb_ref),
            ("wy", wy_hbm, wy_ref),
            ("wx", wx_hbm.at[own_slot], wx_ref),
            ("we", we_hbm.at[tile], we_ref),
        ]
    ):
        loads[name] = pltpu.make_async_copy(source, target, load_sems.at[index])
        loads[name].start()

    lanes = lax.broadcasted_iota(jnp.int32, (local_x, freqs), 1)
    spots = lax.broadcasted_iota(jnp.int32, (8, pixels), 1)
    turn = spots - 4 * lax.div(spots, 4)
    quarter_wave = jnp.where(turn == 0, 1.0, jnp.where(turn == 2, -1.0, 0.0))
    first_row = lax.broadcasted_iota(jnp.int32, (8, pixels), 0) == 0

    loads["mask"].wait()
    loads["wm"].wait()
    wm = (wm_ref[0], wm_ref[1])
    mask = mask_ref[0]
    mbuf[own_slot, :local_x] = dot_pair(pair(mask), wm)
    quarter_row = jnp.where(first_row, quarter_wave, 0.0).astype(jnp.bfloat16)
    padded = jnp.concatenate([mask, jnp.zeros((freqs - local_x, pixels), jnp.float32)], axis=0)
    high, low = pair(padded)
    nt = (((1,), (1,)), ((), ()))
    mbuf[own_slot, local_x:] = lax.dot_general(
        quarter_row, high, nt, preferred_element_type=jnp.float32
    ) + lax.dot_general(quarter_row, low, nt, preferred_element_type=jnp.float32)
    loads["weight"].wait()
    loads["band"].wait()
    for one in range(per_device):
        meta_ref[0, one : one + 1, :] = jnp.full((1, freqs), weight_ref[one] / sources)
    meta_ref[0, 8:, :] = jnp.concatenate(
        [band_ref[one] for one in range(per_device)]
        + [jnp.zeros((8 - 2 * per_device, freqs), jnp.int32)],
        axis=0,
    ).astype(jnp.float32)
    loads["phase"].wait()
    loads["goal"].wait()
    pl.semaphore_wait(barrier, len(peers))

    copies = []

    def send(*args, **keys):
        copy = to(*args, **keys)
        copy.start()
        copies.append(copy)
        return copy

    own_block = mbuf.at[own_slot]
    for peer in far_first:
        send(own_block, own_block, mask_ss.at[peer], mask_rs.at[src], src_at=peer)
    send(own_block, own_block, fwd_ss.at[src], fwd_rs.at[src])
    meta_copy = send(meta_ref.at[0], meta_ref.at[1], meta_ss, meta_rs, src_at=pool_src)
    phase_copies = [
        send(
            phase_ref.at[0, one, row],
            phase_ref.at[1, one, row],
            phase_ss.at[one],
            phase_rs.at[one],
            src_at=pool_src,
        )
        for one in range(per_device)
    ]
    goal_copy = send(goal_ref.at[0], goals_ref, goal_ss, goal_rs, src_at=mate_src)

    loads["move"].wait()
    move = move_ref[...]
    columns = lax.broadcasted_iota(jnp.int32, (freqs, freqs), 1).astype(jnp.float32)

    def make_pupils(group):
        bands = meta_ref[group, 8:, :].T
        parts = []
        for one in range(per_device):
            lower, upper = bands[:, 2 * one : 2 * one + 1], bands[:, 2 * one + 1 : 2 * one + 2]
            passing = (columns >= lower) & (columns < upper)
            sine, cosine = sine_cosine(phase_ref[group, one].reshape(freqs, freqs))
            parts += [jnp.where(passing, cosine, 0.0), jnp.where(passing, sine, 0.0)]
        moved = dot_exact(jnp.concatenate(parts, axis=0), move)
        pupil_ref[group] = moved.reshape(2 * per_device, freqs, freqs)

    make_pupils(0)
    for name in ("wf", "wb", "wy", "wx", "we"):
        loads[name].wait()

    for index, peer in enumerate(near_first):
        if index == last - 1:
            for one in range(per_device):
                half_block = phase_ref.at[1, one, other_row]
                to(
                    half_block, half_block, phase_ss.at[one], phase_rs.at[one], src_at=pool_src
                ).wait_recv()
                send(half_block, half_block, pfwd_ss.at[one], pfwd_rs.at[one])
        block = mbuf.at[peer * 2 + other_row]
        to(block, block, mask_ss.at[peer], mask_rs.at[peer], src_at=peer).wait_recv()
        send(block, block, fwd_ss.at[peer], fwd_rs.at[peer])
    for peer in near_first:
        block = mbuf.at[peer * 2 + row]
        to(block, block, fwd_ss.at[peer], fwd_rs.at[peer]).wait_recv()
    block = mbuf.at[src * 2 + other_row]
    to(block, block, fwd_ss.at[src], fwd_rs.at[src]).wait_recv()

    blocks = pixels // local_x
    extra = jnp.concatenate([mbuf[one, local_x : local_x + 1] for one in range(blocks)], axis=0).T
    rows = []
    for one in range(blocks):
        straight = mbuf[one, :local_x]
        turned = pltpu.roll(straight, half, axis=1)
        real = jnp.where(lanes < half, straight, turned)
        real = jnp.where(lanes == half, extra[:local_x, one : one + 1], real)
        imag = jnp.where(lanes < half, -turned, straight)
        imag = jnp.where(lanes == 0, 0.0, imag)
        rows.append(jnp.concatenate([real, imag], axis=1))
    spectrum = dot_pair((wf_ref[0], wf_ref[1]), pair(jnp.concatenate(rows, axis=0)))
    spec_real = spectrum[:freqs, :freqs] - spectrum[freqs:, freqs:]
    spec_imag = spectrum[:freqs, freqs:] + spectrum[freqs:, :freqs]

    wxt = tuple(
        jnp.concatenate(
            [wb_ref[index, slot, side] for side in range(2) for slot in (own_slot, mate_slot)],
            axis=0,
        )
        for index in range(2)
    )
    wy = (wy_ref[0], wy_ref[1])
    to(
        meta_ref.at[0], meta_ref.at[1], meta_ss, meta_rs, src_at=pool_src
    ).wait_recv()
    for one in range(per_device):
        half_block = phase_ref.at[1, one, row]
        to(half_block, half_block, pfwd_ss.at[one], pfwd_rs.at[one]).wait_recv()

    def swept_rows(group):
        reals, imags = [], []
        for one in range(per_device):
            pr, pi = pupil_ref[group, 2 * one], pupil_ref[group, 2 * one + 1]
            reals.append(pr * spec_real - pi * spec_imag)
            imags.append(pi * spec_real + pr * spec_imag)
        amps = jnp.concatenate(
            [jnp.concatenate(reals, axis=1), jnp.concatenate(imags, axis=1)], axis=0
        )
        return dot_pair(wxt, pair(amps)) * field_scale

    weights = [
        jnp.concatenate([meta_ref[group, one : one + 1, :]] * 2, axis=1)
        for group in range(2)
        for one in range(per_device)
    ]

    def light_of(group, swept, block):
        tops = swept[block * local_x : (block + 1) * local_x]
        ends = swept[(2 + block) * local_x : (3 + block) * local_x]
        rows = jnp.concatenate(
            [
                jnp.concatenate(
                    [
                        tops[:, one * freqs : (one + 1) * freqs],
                        ends[:, one * freqs : (one + 1) * freqs],
                    ],
                    axis=1,
                )
                for one in range(per_device)
            ],
            axis=0,
        )
        field = dot_pair(pair(rows), wy)
        fbuf[group, block] = field
        squares = field[:, :pixels] * field[:, :pixels] + field[:, pixels:] * field[:, pixels:]
        total = weights[group * per_device] * squares[:local_x]
        for one in range(1, per_device):
            total = total + (
                weights[group * per_device + one]
                * squares[one * local_x : (one + 1) * local_x]
            )
        return total

    make_pupils(1)
    swept = swept_rows(0)
    lights = [light_of(0, swept, block) for block in range(2)]
    swept = swept_rows(1)
    for block in (1, 0):
        lights[block] = lights[block] + light_of(1, swept, block)
        part_send[block] = lights[block]
        send(
            part_send.at[block],
            part_recv.at[1 - block],
            part_ss.at[block],
            part_rs.at[1 - block],
            src_at=mate_src,
        )
    to(goal_ref.at[0], goals_ref, goal_ss, goal_rs, src_at=mate_src).wait_recv()

    terms = [jnp.zeros((1, pixels), jnp.float32)] * (2 * per_device)
    for block in (0, 1):
        to(
            part_send.at[1 - block],
            part_recv.at[block],
            part_ss.at[1 - block],
            part_rs.at[block],
            src_at=mate_src,
        ).wait_recv()
        intensity = lights[block] + part_recv[block]
        goal = goal_ref[0] if block == 0 else goals_ref[...]
        resist = 1.0 / (1.0 + jnp.exp(-STEEPNESS * (intensity - THRESHOLD)))
        cotangent = LOSS_SCALE * (resist - goal) * STEEPNESS * resist * (1.0 - resist)
        for group in range(2):
            backs = []
            for one in range(per_device):
                at = group * per_device + one
                field = fbuf[group, block, one * local_x : (one + 1) * local_x]
                real, imag = field[:, :pixels], field[:, pixels:]
                lit_real, lit_imag = cotangent * real, cotangent * imag
                scale = 2.0 * weights[at]
                backs.append(jnp.concatenate([scale * lit_real, scale * lit_imag], axis=1))
                terms[at] = terms[at] + jnp.sum(
                    lit_real * real + lit_imag * imag, axis=0, keepdims=True
                )
            adjoint = dot_pair(pair(jnp.concatenate(backs, axis=0)), wy, 1)
            for one in range(per_device):
                rows = slice(one * local_x, (one + 1) * local_x)
                at = group * per_device + one
                cols = slice(at * freqs, (at + 1) * freqs)
                ubuf[block, :, cols] = adjoint[rows, :freqs]
                ubuf[2 + block, :, cols] = adjoint[rows, freqs:]

    blank = jnp.zeros((1, freqs), jnp.float32)
    for group in range(2):
        tsend[group] = jnp.concatenate(
            [blank]
            + [
                terms[group * per_device + one][:, :freqs]
                + terms[group * per_device + one][:, freqs:]
                for one in range(per_device)
            ]
            + [blank] * (7 - per_device),
            axis=0,
        )
    term_copy = send(tsend, trecv, core_ss.at[1], core_rs.at[1])

    wx = (wx_ref[0], wx_ref[1])
    swept = ubuf[...].reshape(4 * local_x, 2 * per_device * freqs)
    swept = dot_pair(wx, pair(swept)) * field_scale
    grad_real = jnp.zeros((freqs, freqs), jnp.float32)
    grad_imag = grad_real
    for at in range(2 * per_device):
        group, one = at // per_device, at % per_device
        pr, pi = pupil_ref[group, 2 * one], pupil_ref[group, 2 * one + 1]
        cols = slice(at * freqs, (at + 1) * freqs)
        real, imag = swept[:freqs, cols], swept[freqs:, cols]
        grad_real = grad_real + pr * real + pi * imag
        grad_imag = grad_imag + pr * imag - pi * real

    lane = lax.broadcasted_iota(jnp.int32, (freqs, freqs), 1)
    turn_real = pltpu.roll(grad_real, half, axis=1)
    turn_imag = pltpu.roll(grad_imag, half, axis=1)
    sum_real = grad_real + jnp.where(lane == 0, 0.0, turn_real)
    sum_imag = grad_imag + jnp.where(lane == 0, 0.0, turn_imag)
    gap_real = jnp.where(lane == half, 0.0, turn_real) - grad_real
    gap_imag = jnp.where(lane == half, 0.0, turn_imag) - grad_imag
    upper = jnp.where(lane < half, sum_real, -gap_imag)
    lower = jnp.where(lane < half, sum_imag, gap_real)
    grads = pair(
        jnp.concatenate(
            [
                jnp.concatenate([upper, grad_real], axis=1),
                jnp.concatenate([lower, grad_imag], axis=1),
            ],
            axis=0,
        )
    )

    def rows_of(far_row, own_row):
        slots = [peer * 2 + far_row for peer in far_first] + [src * 2 + own_row]
        waves = tuple(
            jnp.concatenate([wb_ref[index, slot, 0] for slot in slots], axis=0)
            for index in range(2)
        )
        return dot_pair(waves, grads)

    csend[...] = rows_of(row, other_row)
    core_copy = send(csend, crecv, core_ss.at[0], core_rs.at[0])
    mine = rows_of(other_row, row)
    term_copy.wait_recv()
    own_terms = tsend[0] + trecv[0]
    pool_terms = tsend[1] + trecv[1]
    core_copy.wait_recv()
    mine = mine + crecv[...]
    pick = jnp.where(
        (lax.broadcasted_iota(jnp.int32, (8, freqs), 0) == 0)
        & (lax.broadcasted_iota(jnp.int32, (8, freqs), 1) == half),
        1.0,
        0.0,
    ).astype(jnp.bfloat16)
    high, low = pair(mine[:, freqs:])
    tail = lax.dot_general(pick, high, nt, preferred_element_type=jnp.float32)
    tail = tail + lax.dot_general(pick, low, nt, preferred_element_type=jnp.float32)
    for index, peer in enumerate(far_first + [src]):
        gsend[index, :local_x] = mine[index * local_x : (index + 1) * local_x, :freqs]
        moved = tail if index == 0 else pltpu.roll(tail, freqs - index * local_x, axis=1)
        gsend[index, local_x:] = moved + (pool_terms if index < last else own_terms)
        if index < last:
            send(
                gsend.at[index], grecv.at[src], grad_ss.at[index], grad_rs.at[src], src_at=peer
            )
    strips = jnp.concatenate(
        [
            jnp.concatenate(
                [
                    mine[index * local_x + one * depth : index * local_x + (one + 1) * depth]
                    for one in range(fold)
                ],
                axis=1,
            )
            for index in range(src_count)
        ],
        axis=0,
    )
    strips = dot_pair(pair(strips), (we_ref[0], we_ref[1]))
    for index, peer in enumerate(far_first + [src]):
        hsend[index, :depth] = strips[index * depth : (index + 1) * depth]
        hsend[index, depth:] = pool_terms if index < last else own_terms
        send(
            hsend.at[index],
            hrecv.at[src],
            halo_ss.at[index],
            halo_rs.at[src],
            src_at=peer,
            tile_at=other_tile,
            row_at=other_row if index < last else row,
        )

    total = gsend[last]
    for peer in near_first:
        to(
            gsend.at[0], grecv.at[peer], grad_ss.at[0], grad_rs.at[peer], src_at=peer
        ).wait_recv()
        total = total + grecv[peer]
    grad_block = dot_pair(pair(total[:local_x]), wm, 1)
    grad_block = grad_block + total[local_x:].T[:local_x, :1] * quarter_wave[:1]
    low, high = grad_block[:, :freqs], grad_block[:, pixels - freqs :]

    packed = jnp.zeros((depth, freqs), jnp.float32)
    for peer in [src] + near_first:
        to(
            hsend.at[0],
            hrecv.at[peer],
            halo_ss.at[0],
            halo_rs.at[peer],
            src_at=peer,
            tile_at=other_tile,
            row_at=row if peer is src else other_row,
        ).wait_recv()
        packed = packed + hrecv[peer, :depth]
    strip = jnp.concatenate(
        [packed]
        + [pltpu.roll(packed, freqs - one * OV, axis=1) for one in range(1, fold)],
        axis=0,
    )
    from_below = jnp.where((lanes < OV) & (tile == 1), strip, 0.0)
    from_above = jnp.where(
        (lanes >= freqs - OV) & (tile == 0), pltpu.roll(strip, freqs - OV, axis=1), 0.0
    )
    out_ref[0, :, :freqs] = low + from_below
    out_ref[0, :, pixels - freqs :] = high + from_above
    terms = own_terms + grecv[pool_src, local_x:]
    terms = terms + (hrecv[src, depth:] + hrecv[pool_src, depth:])
    terms = terms / (sources * pixels * tile_count)
    for one in range(per_device):
        terms_ref[one] = jnp.sum(terms[one + 1 : one + 2, :])
    for copy in copies:
        copy.wait_send()


def shards(mask_windows, target_windows, pupil_bands, pupil_phase, source_weight):
    src_count = lax.axis_size("src")
    tile_count = lax.axis_size("tile")
    row_count = lax.axis_size("row")
    local_x, pixels = mask_windows.shape[1:]
    per_device, freqs = pupil_phase.shape[:2]
    blocks = src_count * row_count
    fits = row_count == 2 and tile_count == 2 and src_count == 4 and 2 * per_device <= 8
    fits = fits and freqs == 128 and pixels == 2 * freqs and local_x == OV
    if not fits or local_x * blocks != pixels or OV * 4 != freqs:
        return shards_plain(
            mask_windows, target_windows, pupil_bands, pupil_phase, source_weight
        )
    half, fold = freqs // 2, freqs // OV
    tables = wave_constants(pixels, freqs, blocks, src_count, local_x, fold)
    bands = jnp.transpose(pupil_bands, (0, 2, 1))
    phases = pupil_phase.reshape(per_device, 2, half, freqs)
    in_vmem = pl.BlockSpec(memory_space=pltpu.VMEM)
    in_smem = pl.BlockSpec(memory_space=pltpu.SMEM)
    f32 = jnp.float32
    block = (local_x, pixels)
    dma = pltpu.SemaphoreType.DMA
    like = [pltpu.VMEM(one.shape, one.dtype) for one in tables]
    like[4] = pltpu.VMEM(tables[4].shape[1:], tables[4].dtype)
    like[5] = pltpu.VMEM(tables[5].shape[1:], tables[5].dtype)
    four = dma((src_count,))
    return pl.pallas_call(
        functools.partial(kernel, src_count, tile_count),
        out_shape=(
            jax.ShapeDtypeStruct(mask_windows.shape, f32),
            jax.ShapeDtypeStruct(source_weight.shape, f32),
        ),
        in_specs=[pl.BlockSpec(memory_space=pltpu.HBM)] * 12,
        out_specs=(in_vmem, in_smem),
        scratch_shapes=like
        + [
            pltpu.VMEM(mask_windows.shape, f32),
            pltpu.VMEM(target_windows.shape, f32),
            pltpu.VMEM(bands.shape, bands.dtype),
            pltpu.VMEM((2,) + phases.shape, f32),
            pltpu.SMEM(source_weight.shape, f32),
            dma((12,)),
            pltpu.VMEM((blocks, local_x + 8, freqs), f32),
            pltpu.VMEM((2, 2 * per_device, freqs, freqs), f32),
            pltpu.VMEM((2, 2, per_device * local_x, 2 * pixels), f32),
            pltpu.VMEM((4, local_x, 2 * per_device * freqs), f32),
            pltpu.VMEM((2, 16, freqs), f32),
            pltpu.VMEM(block, f32),
            pltpu.VMEM((2,) + block, f32),
            pltpu.VMEM((2,) + block, f32),
            pltpu.VMEM((2, 8, freqs), f32),
            pltpu.VMEM((2, 8, freqs), f32),
            pltpu.VMEM((src_count * local_x, pixels), f32),
            pltpu.VMEM((src_count * local_x, pixels), f32),
            pltpu.VMEM((src_count, local_x + 8, freqs), f32),
            pltpu.VMEM((src_count, local_x + 8, freqs), f32),
            pltpu.VMEM((src_count, 16, freqs), f32),
            pltpu.VMEM((src_count, 16, freqs), f32),
        ]
        + [four] * 4
        + [dma(())] * 2
        + [dma((per_device,))] * 4
        + [dma(())] * 2
        + [dma((2,))] * 4
        + [four] * 4,
        compiler_params=pltpu.CompilerParams(
            collective_id=0, has_side_effects=True, vmem_limit_bytes=63 * 1024 * 1024
        ),
    )(*tables, mask_windows, target_windows, bands, phases, source_weight)


def solution(mesh):
    return jax.shard_map(
        shards,
        mesh=mesh,
        in_specs=(
            P(("parts", "tile"), ("src", "row"), None),
            P(("parts", "tile"), ("src", "row"), None),
            P(("parts", "src"), None, None),
            P(("parts", "src"), None, None),
            P(("parts", "src")),
        ),
        out_specs=(P(("parts", "tile"), ("src", "row"), None), P(("parts", "src"))),
        check_vma=False,
    )
```

```python
import functools
import math

import jax
import jax.numpy as jnp
import numpy as np
from jax import lax
from jax.experimental import pallas as pl
from jax.experimental.pallas import tpu as pltpu
from jax.sharding import PartitionSpec as P

M = 256
K = 128
OV = 32


STEEPNESS = 20.0
THRESHOLD = 0.15
LOSS_SCALE = 32.0


def with_halo(block, sides, width):
    for axis, dim in sides:
        count = lax.axis_size(axis)
        forward = [(i, i + 1) for i in range(count - 1)]
        backward = [(target, source) for source, target in forward]
        low = lax.ppermute(
            lax.slice_in_dim(block, block.shape[dim] - width, None, axis=dim), axis, forward
        )
        high = lax.ppermute(lax.slice_in_dim(block, 0, width, axis=dim), axis, backward)
        block = jnp.concatenate([low, block, high], axis=dim)
    return block


def matmul(left_op, right_op):
    return lax.dot_general(
        left_op,
        right_op,
        (((1,), (0,)), ((), ())),
        precision=lax.Precision.HIGHEST,
        preferred_element_type=jnp.float32,
    )


def matmul_tn(left_op, right_op):
    return lax.dot_general(
        left_op,
        right_op,
        (((0,), (0,)), ((), ())),
        precision=lax.Precision.HIGHEST,
        preferred_element_type=jnp.float32,
    )


def matmul_nt(left_op, right_op):
    return lax.dot_general(
        left_op,
        right_op,
        (((1,), (1,)), ((), ())),
        precision=lax.Precision.HIGHEST,
        preferred_element_type=jnp.float32,
    )


def wave_tables(positions):
    freq_index = jnp.arange(K, dtype=jnp.int32) - K // 2
    phase_index = freq_index[:, None] * positions[None, :] % M
    angles = 2.0 * math.pi / M * phase_index.astype(jnp.float32)
    return (jnp.cos(angles), jnp.sin(angles))


def shards_plain(mask_windows, target_windows, pupil_bands, pupil_phase, source_weight):
    src_count = lax.axis_size("src")
    tile_count = lax.axis_size("tile")
    row_count = lax.axis_size("row")
    local_x = mask_windows.shape[1]
    per_device = pupil_phase.shape[0]
    sources = per_device * src_count
    field_scale = 1.0 / (M * K)
    src_id = lax.axis_index("src")
    row_id = lax.axis_index("row")
    x_start = (src_id * row_count + row_id) * local_x
    block_starts = (jnp.arange(src_count, dtype=jnp.int32) * row_count + row_id) * local_x
    row_set = (block_starts[:, None] + jnp.arange(local_x, dtype=jnp.int32)[None, :]).reshape(
        src_count * local_x
    )
    cos_all, sin_all = wave_tables(jnp.arange(M, dtype=jnp.int32))
    cos_set, sin_set = wave_tables(row_set)
    cos_own, sin_own = wave_tables(x_start + jnp.arange(local_x, dtype=jnp.int32))
    window = mask_windows[0]
    goal_block = target_windows[0]
    zero_spec = jnp.zeros((K, K), jnp.float32)
    shard_rows = lax.all_gather(window, ("src", "row"), axis=0, tiled=True)
    part_real = matmul_nt(shard_rows, cos_all)
    part_imag = -matmul_nt(shard_rows, sin_all)
    spec_real = matmul(cos_all, part_real) + matmul(sin_all, part_imag)
    spec_imag = matmul(cos_all, part_imag) - matmul(sin_all, part_real)
    freq_cols = jnp.arange(K, dtype=jnp.int32)
    inside = (freq_cols[None, None, :] >= pupil_bands[:, :, 0:1]) & (
        freq_cols[None, None, :] < pupil_bands[:, :, 1:2]
    )
    passing = inside.astype(jnp.float32)
    pupil_real = passing * jnp.cos(pupil_phase)
    pupil_imag = passing * jnp.sin(pupil_phase)
    amp_real = (pupil_real * spec_real - pupil_imag * spec_imag).reshape(per_device * K, K)
    amp_imag = (pupil_imag * spec_real + pupil_real * spec_imag).reshape(per_device * K, K)
    half_real = (matmul(amp_real, cos_all) - matmul(amp_imag, sin_all)).reshape(per_device, K, M)
    half_imag = (matmul(amp_real, sin_all) + matmul(amp_imag, cos_all)).reshape(per_device, K, M)
    weights = source_weight / sources

    def fields(pair_in):
        one_real, one_imag = pair_in
        field_real = field_scale * (matmul_tn(cos_set, one_real) - matmul_tn(sin_set, one_imag))
        field_imag = field_scale * (matmul_tn(cos_set, one_imag) + matmul_tn(sin_set, one_real))
        return (field_real, field_imag)

    stack_real, stack_imag = lax.map(fields, (half_real, half_imag))
    part_real = stack_real
    part_imag = stack_imag
    intensity = lax.psum_scatter(
        jnp.sum(weights[:, None, None] * (part_real * part_real + part_imag * part_imag), axis=0),
        "src",
        scatter_dimension=0,
        tiled=True,
    )
    resist = jax.nn.sigmoid(STEEPNESS * (intensity - THRESHOLD))
    cotangent = LOSS_SCALE * (resist - goal_block) * STEEPNESS * resist * (1.0 - resist)
    cotangent_all = lax.all_gather(cotangent, "src", axis=0, tiled=True)
    source_ids = jnp.arange(per_device, dtype=jnp.int32)

    def add_back(source_id, totals):
        grad_real, grad_imag, source_terms = totals
        field_real = stack_real[source_id]
        field_imag = stack_imag[source_id]
        back_scale = 2.0 * weights[source_id] * cotangent_all
        back_real = back_scale * field_real
        back_imag = back_scale * field_imag
        adj_real = matmul(cos_set, back_real) + matmul(sin_set, back_imag)
        adj_imag = matmul(cos_set, back_imag) - matmul(sin_set, back_real)
        amp_grad_real = field_scale * (matmul_nt(adj_real, cos_all) + matmul_nt(adj_imag, sin_all))
        amp_grad_imag = field_scale * (matmul_nt(adj_imag, cos_all) - matmul_nt(adj_real, sin_all))
        pass_real = pupil_real[source_id]
        pass_imag = pupil_imag[source_id]
        grad_real = grad_real + pass_real * amp_grad_real + pass_imag * amp_grad_imag
        grad_imag = grad_imag + pass_real * amp_grad_imag - pass_imag * amp_grad_real
        term_value = jnp.sum(cotangent_all * (field_real * field_real + field_imag * field_imag))
        source_terms = source_terms + jnp.where(source_ids == source_id, term_value, 0.0)
        return (grad_real, grad_imag, source_terms)

    grad_real, grad_imag, source_terms = lax.fori_loop(
        0, per_device, add_back, (zero_spec, zero_spec, jnp.zeros((per_device,), jnp.float32))
    )
    grad_real, grad_imag = lax.psum((grad_real, grad_imag), ("src", "row"))
    source_sum = lax.psum(source_terms, ("tile", "row"))
    source_grad = source_sum / (sources * M * tile_count)
    q_one = matmul(grad_real, cos_all) - matmul(grad_imag, sin_all)
    q_two = matmul(grad_real, sin_all) + matmul(grad_imag, cos_all)
    grad_block = matmul_tn(cos_own, q_one) - matmul_tn(sin_own, q_two)
    padded = with_halo(grad_block, (("tile", 1),), OV)
    from_below = padded[:, :OV]
    from_above = padded[:, M + OV :]
    middle = jnp.zeros((local_x, M - 2 * OV), jnp.float32)
    grad_block = grad_block + jnp.concatenate([from_below, middle, from_above], axis=1)
    return (grad_block[None], source_grad)


MESH = pl.DeviceIdType.MESH


def pair(values):
    high = values.astype(jnp.bfloat16)
    return high, (values - high.astype(jnp.float32)).astype(jnp.bfloat16)


def dot_pair(left_op, right_op, contract_right=0):
    dims = (((1,), (contract_right,)), ((), ()))

    def one(a, b):
        return lax.dot_general(a, b, dims, preferred_element_type=jnp.float32)

    (left_high, left_low), (right_high, right_low) = left_op, right_op
    return one(left_high, right_high) + (
        one(left_high, right_low) + one(left_low, right_high)
    )


def frequency_order(freqs):
    half = freqs // 2
    return np.concatenate([np.arange(half), [-half], -np.arange(1, half)])


def wave_constants(pixels, freqs, blocks, src_count, local_x, fold):
    half = freqs // 2
    spots = np.arange(pixels)

    def waves(index):
        angles = 2.0 * np.pi / pixels * (np.outer(index, spots) % pixels)
        return np.cos(angles), np.sin(angles)

    cos_x, sin_x = waves(np.arange(freqs) - half)
    order = frequency_order(freqs)
    cos_y, sin_y = waves(order)
    spectrum = np.concatenate([cos_x, -sin_x], axis=0)
    wave_y = np.block([[cos_y, sin_y], [-sin_y, cos_y]])
    real_rows = np.concatenate([cos_x.T, -sin_x.T], axis=1)
    imag_rows = np.concatenate([sin_x.T, cos_x.T], axis=1)
    wave_rows = np.stack(
        [one.reshape(blocks, local_x, 2 * freqs) for one in (real_rows, imag_rows)], axis=1
    )
    sets = []
    for own in range(blocks):
        src, row = own // 2, own % 2
        mate = (src + src_count // 2) % src_count * 2 + 1 - row
        rows = np.concatenate([np.arange(local_x) + one * local_x for one in (own, mate)])
        c, s = cos_x[:, rows], sin_x[:, rows]
        sets.append(np.block([[c, s], [-s, c]]))
    packed = np.concatenate([cos_y[:half], -sin_y[half:]], axis=0).T
    edges = []
    for start in (pixels - OV, 0):
        table = np.zeros((fold, 2 * freqs, fold, OV))
        for group in range(fold):
            table[group, :freqs, group] = packed[start : start + OV].T
            table[group, freqs + half, group] = cos_y[half, start : start + OV]
        edges.append(table.reshape(fold * 2 * freqs, freqs))
    move = np.zeros((freqs, freqs))
    move[order + half, np.arange(freqs)] = 1.0
    return (
        split_constant(packed),
        split_constant(spectrum),
        split_constant(wave_y),
        split_constant(wave_rows),
        split_constant(np.stack(sets), 1),
        split_constant(np.stack(edges), 1),
        move.astype(jnp.bfloat16),
    )


def split_constant(values, axis=0):
    values = values.astype(np.float32)
    high = values.astype(jnp.bfloat16)
    low = (values - high.astype(np.float32)).astype(jnp.bfloat16)
    return np.stack([high, low], axis=axis)


def sine_cosine(phase):
    quarter = 0.25 * phase
    square = quarter * quarter
    sine = 1.0 / 362880.0
    for term in (-1.0 / 5040.0, 1.0 / 120.0, -1.0 / 6.0, 1.0):
        sine = sine * square + term
    sine = sine * quarter
    fall = -1.0 / 40320.0
    for term in (1.0 / 720.0, -1.0 / 24.0, 0.5):
        fall = fall * square + term
    cosine = 1.0 - fall * square
    twice = 2.0 * sine
    sine, cosine = twice * cosine, 1.0 - twice * sine
    twice = 2.0 * sine
    return twice * cosine, 1.0 - twice * sine


def dot_exact(left_op, right_op, dims=(((1,), (0,)), ((), ()))):
    high, low = pair(left_op)

    def one(a):
        return lax.dot_general(a, right_op, dims, preferred_element_type=jnp.float32)

    return one(high) + one(low)


def kernel(
    src_count,
    tile_count,
    wm_hbm,
    wf_hbm,
    wy_hbm,
    wb_hbm,
    wx_hbm,
    we_hbm,
    move_hbm,
    mask_hbm,
    goal_hbm,
    band_hbm,
    phase_hbm,
    weight_hbm,
    out_ref,
    terms_ref,
    wm_ref,
    wf_ref,
    wy_ref,
    wb_ref,
    wx_ref,
    we_ref,
    move_ref,
    mask_ref,
    goal_ref,
    band_ref,
    phase_ref,
    weight_ref,
    load_sems,
    mbuf,
    pupil_ref,
    fbuf,
    ubuf,
    meta_ref,
    goals_ref,
    part_send,
    part_recv,
    tsend,
    trecv,
    csend,
    crecv,
    gsend,
    grecv,
    hsend,
    hrecv,
    mask_ss,
    mask_rs,
    fwd_ss,
    fwd_rs,
    meta_ss,
    meta_rs,
    phase_ss,
    phase_rs,
    pfwd_ss,
    pfwd_rs,
    goal_ss,
    goal_rs,
    part_ss,
    part_rs,
    core_ss,
    core_rs,
    grad_ss,
    grad_rs,
    halo_ss,
    halo_rs,
):
    part = lax.axis_index("parts")
    src = lax.axis_index("src")
    tile = lax.axis_index("tile")
    row = lax.axis_index("row")
    local_x, pixels = mask_ref.shape[1:]
    per_device, half, freqs = phase_ref.shape[1], phase_ref.shape[3], phase_ref.shape[4]
    sources = per_device * src_count
    field_scale = 1.0 / (pixels * freqs)
    fold = freqs // OV
    depth = local_x // fold
    other_row = 1 - row
    other_tile = 1 - tile
    last = src_count - 1
    own_slot = src * 2 + row
    mate_src = lax.rem(src + src_count // 2, src_count)
    mate_slot = mate_src * 2 + other_row
    pool_src = src + 1 - 2 * lax.rem(src, 2)

    def far(step):
        up = last - src
        side = lax.div(up + last - step, src_count)
        return side * (last - step) + (1 - side) * (step - up)

    far_first = [far(step) for step in range(last)]
    near_first = far_first[::-1]

    def to(src_ref, dst_ref, ss, rs, src_at=src, tile_at=tile, row_at=other_row):
        return pltpu.make_async_remote_copy(
            src_ref=src_ref,
            dst_ref=dst_ref,
            send_sem=ss,
            recv_sem=rs,
            device_id=(part, src_at, tile_at, row_at),
            device_id_type=MESH,
        )

    barrier = pltpu.get_barrier_semaphore()
    peers = [(peer, tile, other_row) for peer in far_first]
    peers += [(peer, other_tile, other_row) for peer in far_first]
    peers += [(src, tile, other_row), (src, other_tile, row)]
    for src_at, tile_at, row_at in peers:
        pl.semaphore_signal(
            barrier, inc=1, device_id=(part, src_at, tile_at, row_at), device_id_type=MESH
        )

    loads = {}
    for index, (name, source, target) in enumerate(
        [
            ("mask", mask_hbm, mask_ref),
            ("wm", wm_hbm, wm_ref),
            ("weight", weight_hbm, weight_ref),
            ("band", band_hbm, band_ref),
            ("phase", phase_hbm, phase_ref.at[0]),
            ("goal", goal_hbm, goal_ref),
            ("move", move_hbm, move_ref),
            ("wf", wf_hbm, wf_ref),
            ("wb", wb_hbm, wb_ref),
            ("wy", wy_hbm, wy_ref),
            ("wx", wx_hbm.at[own_slot], wx_ref),
            ("we", we_hbm.at[tile], we_ref),
        ]
    ):
        loads[name] = pltpu.make_async_copy(source, target, load_sems.at[index])
        loads[name].start()

    lanes = lax.broadcasted_iota(jnp.int32, (local_x, freqs), 1)
    spots = lax.broadcasted_iota(jnp.int32, (8, pixels), 1)
    turn = spots - 4 * lax.div(spots, 4)
    quarter_wave = jnp.where(turn == 0, 1.0, jnp.where(turn == 2, -1.0, 0.0))
    first_row = lax.broadcasted_iota(jnp.int32, (8, pixels), 0) == 0

    loads["mask"].wait()
    loads["wm"].wait()
    wm = (wm_ref[0], wm_ref[1])
    mask = mask_ref[0]
    mbuf[own_slot, :local_x] = dot_pair(pair(mask), wm)
    quarter_row = jnp.where(first_row, quarter_wave, 0.0).astype(jnp.bfloat16)
    padded = jnp.concatenate([mask, jnp.zeros((freqs - local_x, pixels), jnp.float32)], axis=0)
    high, low = pair(padded)
    nt = (((1,), (1,)), ((), ()))
    mbuf[own_slot, local_x:] = lax.dot_general(
        quarter_row, high, nt, preferred_element_type=jnp.float32
    ) + lax.dot_general(quarter_row, low, nt, preferred_element_type=jnp.float32)
    loads["weight"].wait()
    loads["band"].wait()
    for one in range(per_device):
        meta_ref[0, one : one + 1, :] = jnp.full((1, freqs), weight_ref[one] / sources)
    meta_ref[0, 8:, :] = jnp.concatenate(
        [band_ref[one] for one in range(per_device)]
        + [jnp.zeros((8 - 2 * per_device, freqs), jnp.int32)],
        axis=0,
    ).astype(jnp.float32)
    loads["phase"].wait()
    loads["goal"].wait()
    pl.semaphore_wait(barrier, len(peers))

    copies = []

    def send(*args, **keys):
        copy = to(*args, **keys)
        copy.start()
        copies.append(copy)
        return copy

    own_block = mbuf.at[own_slot]
    for peer in far_first:
        send(own_block, own_block, mask_ss.at[peer], mask_rs.at[src], src_at=peer)
    send(own_block, own_block, fwd_ss.at[src], fwd_rs.at[src])
    send(meta_ref.at[0], meta_ref.at[1], meta_ss, meta_rs, src_at=pool_src)
    for one in range(per_device):
        half_block = phase_ref.at[1, one, row]
        send(
            phase_ref.at[0, one, row],
            half_block,
            phase_ss.at[one],
            phase_rs.at[one],
            src_at=pool_src,
        )

    loads["move"].wait()
    move = move_ref[...]
    columns = lax.broadcasted_iota(jnp.int32, (freqs, freqs), 1).astype(jnp.float32)

    def make_pupils(group):
        bands = meta_ref[group, 8:, :].T
        parts = []
        for one in range(per_device):
            lower, upper = bands[:, 2 * one : 2 * one + 1], bands[:, 2 * one + 1 : 2 * one + 2]
            passing = (columns >= lower) & (columns < upper)
            sine, cosine = sine_cosine(phase_ref[group, one].reshape(freqs, freqs))
            parts += [jnp.where(passing, cosine, 0.0), jnp.where(passing, sine, 0.0)]
        moved = dot_exact(jnp.concatenate(parts, axis=0), move)
        pupil_ref[group] = moved.reshape(2 * per_device, freqs, freqs)

    make_pupils(0)
    for name in ("wf", "wb", "wy", "wx", "we"):
        loads[name].wait()

    for peer in near_first:
        block = mbuf.at[peer * 2 + other_row]
        to(block, block, mask_ss.at[peer], mask_rs.at[peer], src_at=peer).wait_recv()
        send(block, block, fwd_ss.at[peer], fwd_rs.at[peer])
    for peer in near_first:
        block = mbuf.at[peer * 2 + row]
        to(block, block, fwd_ss.at[peer], fwd_rs.at[peer]).wait_recv()
    block = mbuf.at[src * 2 + other_row]
    to(block, block, fwd_ss.at[src], fwd_rs.at[src]).wait_recv()

    blocks = pixels // local_x
    extra = jnp.concatenate([mbuf[one, local_x : local_x + 1] for one in range(blocks)], axis=0).T
    rows = []
    for one in range(blocks):
        straight = mbuf[one, :local_x]
        turned = pltpu.roll(straight, half, axis=1)
        real = jnp.where(lanes < half, straight, turned)
        real = jnp.where(lanes == half, extra[:local_x, one : one + 1], real)
        imag = jnp.where(lanes < half, -turned, straight)
        imag = jnp.where(lanes == 0, 0.0, imag)
        rows.append(jnp.concatenate([real, imag], axis=1))
    spectrum = dot_pair((wf_ref[0], wf_ref[1]), pair(jnp.concatenate(rows, axis=0)))
    spec_real = spectrum[:freqs, :freqs] - spectrum[freqs:, freqs:]
    spec_imag = spectrum[:freqs, freqs:] + spectrum[freqs:, :freqs]

    wxt = tuple(
        jnp.concatenate(
            [wb_ref[index, slot, side] for side in range(2) for slot in (own_slot, mate_slot)],
            axis=0,
        )
        for index in range(2)
    )
    wy = (wy_ref[0], wy_ref[1])
    for one in range(per_device):
        half_block = phase_ref.at[1, one, other_row]
        to(
            half_block, half_block, phase_ss.at[one], phase_rs.at[one], src_at=pool_src
        ).wait_recv()
        send(half_block, half_block, pfwd_ss.at[one], pfwd_rs.at[one])
    send(goal_ref.at[0], goals_ref, goal_ss, goal_rs, src_at=mate_src)

    def swept_rows(group):
        reals, imags = [], []
        for one in range(per_device):
            pr, pi = pupil_ref[group, 2 * one], pupil_ref[group, 2 * one + 1]
            reals.append(pr * spec_real - pi * spec_imag)
            imags.append(pi * spec_real + pr * spec_imag)
        amps = jnp.concatenate(
            [jnp.concatenate(reals, axis=1), jnp.concatenate(imags, axis=1)], axis=0
        )
        return dot_pair(wxt, pair(amps)) * field_scale

    to(meta_ref.at[0], meta_ref.at[1], meta_ss, meta_rs, src_at=pool_src).wait_recv()
    weights = [
        jnp.concatenate([meta_ref[group, one : one + 1, :]] * 2, axis=1)
        for group in range(2)
        for one in range(per_device)
    ]

    def light_of(group, swept, block):
        tops = swept[block * local_x : (block + 1) * local_x]
        ends = swept[(2 + block) * local_x : (3 + block) * local_x]
        rows = jnp.concatenate(
            [
                jnp.concatenate(
                    [
                        tops[:, one * freqs : (one + 1) * freqs],
                        ends[:, one * freqs : (one + 1) * freqs],
                    ],
                    axis=1,
                )
                for one in range(per_device)
            ],
            axis=0,
        )
        field = dot_pair(pair(rows), wy)
        fbuf[group, block] = field
        squares = field[:, :pixels] * field[:, :pixels] + field[:, pixels:] * field[:, pixels:]
        total = weights[group * per_device] * squares[:local_x]
        for one in range(1, per_device):
            total = total + (
                weights[group * per_device + one]
                * squares[one * local_x : (one + 1) * local_x]
            )
        return total

    swept = swept_rows(0)
    lights = [light_of(0, swept, block) for block in range(2)]
    for one in range(per_device):
        half_block = phase_ref.at[1, one, row]
        to(half_block, half_block, pfwd_ss.at[one], pfwd_rs.at[one]).wait_recv()
    make_pupils(1)
    swept = swept_rows(1)
    for block in (1, 0):
        lights[block] = lights[block] + light_of(1, swept, block)
        part_send[block] = lights[block]
        send(
            part_send.at[block],
            part_recv.at[1 - block],
            part_ss.at[block],
            part_rs.at[1 - block],
            src_at=mate_src,
        )
    to(goal_ref.at[0], goals_ref, goal_ss, goal_rs, src_at=mate_src).wait_recv()

    terms = [jnp.zeros((1, pixels), jnp.float32)] * (2 * per_device)
    for block in (0, 1):
        to(
            part_send.at[1 - block],
            part_recv.at[block],
            part_ss.at[1 - block],
            part_rs.at[block],
            src_at=mate_src,
        ).wait_recv()
        intensity = lights[block] + part_recv[block]
        goal = goal_ref[0] if block == 0 else goals_ref[...]
        resist = 1.0 / (1.0 + jnp.exp(-STEEPNESS * (intensity - THRESHOLD)))
        cotangent = LOSS_SCALE * (resist - goal) * STEEPNESS * resist * (1.0 - resist)
        for group in range(2):
            backs = []
            for one in range(per_device):
                at = group * per_device + one
                field = fbuf[group, block, one * local_x : (one + 1) * local_x]
                real, imag = field[:, :pixels], field[:, pixels:]
                lit_real, lit_imag = cotangent * real, cotangent * imag
                scale = 2.0 * weights[at]
                backs.append(jnp.concatenate([scale * lit_real, scale * lit_imag], axis=1))
                terms[at] = terms[at] + jnp.sum(
                    lit_real * real + lit_imag * imag, axis=0, keepdims=True
                )
            adjoint = dot_pair(pair(jnp.concatenate(backs, axis=0)), wy, 1)
            for one in range(per_device):
                rows = slice(one * local_x, (one + 1) * local_x)
                at = group * per_device + one
                cols = slice(at * freqs, (at + 1) * freqs)
                ubuf[block, :, cols] = adjoint[rows, :freqs]
                ubuf[2 + block, :, cols] = adjoint[rows, freqs:]

    blank = jnp.zeros((1, freqs), jnp.float32)
    for group in range(2):
        tsend[group] = jnp.concatenate(
            [blank]
            + [
                terms[group * per_device + one][:, :freqs]
                + terms[group * per_device + one][:, freqs:]
                for one in range(per_device)
            ]
            + [blank] * (7 - per_device),
            axis=0,
        )
    term_copy = send(tsend, trecv, core_ss.at[1], core_rs.at[1])

    wx = (wx_ref[0], wx_ref[1])
    swept = ubuf[...].reshape(4 * local_x, 2 * per_device * freqs)
    swept = dot_pair(wx, pair(swept)) * field_scale
    grad_real = jnp.zeros((freqs, freqs), jnp.float32)
    grad_imag = grad_real
    for at in range(2 * per_device):
        group, one = at // per_device, at % per_device
        pr, pi = pupil_ref[group, 2 * one], pupil_ref[group, 2 * one + 1]
        cols = slice(at * freqs, (at + 1) * freqs)
        real, imag = swept[:freqs, cols], swept[freqs:, cols]
        grad_real = grad_real + pr * real + pi * imag
        grad_imag = grad_imag + pr * imag - pi * real

    lane = lax.broadcasted_iota(jnp.int32, (freqs, freqs), 1)
    turn_real = pltpu.roll(grad_real, half, axis=1)
    turn_imag = pltpu.roll(grad_imag, half, axis=1)
    sum_real = grad_real + jnp.where(lane == 0, 0.0, turn_real)
    sum_imag = grad_imag + jnp.where(lane == 0, 0.0, turn_imag)
    gap_real = jnp.where(lane == half, 0.0, turn_real) - grad_real
    gap_imag = jnp.where(lane == half, 0.0, turn_imag) - grad_imag
    upper = jnp.where(lane < half, sum_real, -gap_imag)
    lower = jnp.where(lane < half, sum_imag, gap_real)
    grads = pair(
        jnp.concatenate(
            [
                jnp.concatenate([upper, grad_real], axis=1),
                jnp.concatenate([lower, grad_imag], axis=1),
            ],
            axis=0,
        )
    )

    def rows_of(far_row, own_row):
        slots = [peer * 2 + far_row for peer in far_first] + [src * 2 + own_row]
        waves = tuple(
            jnp.concatenate([wb_ref[index, slot, 0] for slot in slots], axis=0)
            for index in range(2)
        )
        return dot_pair(waves, grads)

    csend[...] = rows_of(row, other_row)
    core_copy = send(csend, crecv, core_ss.at[0], core_rs.at[0])
    mine = rows_of(other_row, row)
    term_copy.wait_recv()
    own_terms = tsend[0] + trecv[0]
    pool_terms = tsend[1] + trecv[1]
    core_copy.wait_recv()
    mine = mine + crecv[...]
    pick = jnp.where(
        (lax.broadcasted_iota(jnp.int32, (8, freqs), 0) == 0)
        & (lax.broadcasted_iota(jnp.int32, (8, freqs), 1) == half),
        1.0,
        0.0,
    ).astype(jnp.bfloat16)
    high, low = pair(mine[:, freqs:])
    tail = lax.dot_general(pick, high, nt, preferred_element_type=jnp.float32)
    tail = tail + lax.dot_general(pick, low, nt, preferred_element_type=jnp.float32)
    for index, peer in enumerate(far_first + [src]):
        gsend[index, :local_x] = mine[index * local_x : (index + 1) * local_x, :freqs]
        moved = tail if index == 0 else pltpu.roll(tail, freqs - index * local_x, axis=1)
        gsend[index, local_x:] = moved + (pool_terms if index < last else own_terms)
        if index < last:
            send(
                gsend.at[index], grecv.at[src], grad_ss.at[index], grad_rs.at[src], src_at=peer
            )
    strips = jnp.concatenate(
        [
            jnp.concatenate(
                [
                    mine[index * local_x + one * depth : index * local_x + (one + 1) * depth]
                    for one in range(fold)
                ],
                axis=1,
            )
            for index in range(src_count)
        ],
        axis=0,
    )
    strips = dot_pair(pair(strips), (we_ref[0], we_ref[1]))
    for index, peer in enumerate(far_first + [src]):
        hsend[index, :depth] = strips[index * depth : (index + 1) * depth]
        hsend[index, depth:] = pool_terms if index < last else own_terms
        send(
            hsend.at[index],
            hrecv.at[src],
            halo_ss.at[index],
            halo_rs.at[src],
            src_at=peer,
            tile_at=other_tile,
            row_at=other_row if index < last else row,
        )

    total = gsend[last]
    for peer in near_first:
        to(
            gsend.at[0], grecv.at[peer], grad_ss.at[0], grad_rs.at[peer], src_at=peer
        ).wait_recv()
        total = total + grecv[peer]
    grad_block = dot_pair(pair(total[:local_x]), wm, 1)
    grad_block = grad_block + total[local_x:].T[:local_x, :1] * quarter_wave[:1]
    low, high = grad_block[:, :freqs], grad_block[:, pixels - freqs :]

    packed = jnp.zeros((depth, freqs), jnp.float32)
    for peer in [src] + near_first:
        to(
            hsend.at[0],
            hrecv.at[peer],
            halo_ss.at[0],
            halo_rs.at[peer],
            src_at=peer,
            tile_at=other_tile,
            row_at=row if peer is src else other_row,
        ).wait_recv()
        packed = packed + hrecv[peer, :depth]
    strip = jnp.concatenate(
        [packed]
        + [pltpu.roll(packed, freqs - one * OV, axis=1) for one in range(1, fold)],
        axis=0,
    )
    from_below = jnp.where((lanes < OV) & (tile == 1), strip, 0.0)
    from_above = jnp.where(
        (lanes >= freqs - OV) & (tile == 0), pltpu.roll(strip, freqs - OV, axis=1), 0.0
    )
    out_ref[0, :, :freqs] = low + from_below
    out_ref[0, :, pixels - freqs :] = high + from_above
    terms = own_terms + grecv[pool_src, local_x:]
    terms = terms + (hrecv[src, depth:] + hrecv[pool_src, depth:])
    terms = terms / (sources * pixels * tile_count)
    terms_ref[...] = terms
    for copy in copies:
        copy.wait_send()


def finish_kernel(grads_ref, terms_ref, out_ref, sums_ref, sem):
    copy = pltpu.make_async_copy(grads_ref, out_ref, sem)
    copy.start()
    for one in range(sums_ref.shape[0]):
        sums_ref[one] = jnp.sum(terms_ref[one + 1 : one + 2, :])
    copy.wait()


def finish(grads, terms, shape):
    in_vmem = pl.BlockSpec(memory_space=pltpu.VMEM)
    return pl.pallas_call(
        finish_kernel,
        out_shape=(
            jax.ShapeDtypeStruct(grads.shape, grads.dtype),
            jax.ShapeDtypeStruct(shape, terms.dtype),
        ),
        in_specs=[in_vmem, in_vmem],
        out_specs=(
            pl.BlockSpec(memory_space=pltpu.HBM),
            pl.BlockSpec(memory_space=pltpu.SMEM),
        ),
        scratch_shapes=[pltpu.SemaphoreType.DMA(())],
    )(*(pltpu.with_memory_space_constraint(one, pltpu.VMEM) for one in (grads, terms)))


def shards(mask_windows, target_windows, pupil_bands, pupil_phase, source_weight):
    src_count = lax.axis_size("src")
    tile_count = lax.axis_size("tile")
    row_count = lax.axis_size("row")
    local_x, pixels = mask_windows.shape[1:]
    per_device, freqs = pupil_phase.shape[:2]
    blocks = src_count * row_count
    fits = row_count == 2 and tile_count == 2 and src_count == 4 and 2 * per_device <= 8
    fits = fits and freqs == 128 and pixels == 2 * freqs and local_x == OV
    if not fits or local_x * blocks != pixels or OV * 4 != freqs:
        return shards_plain(
            mask_windows, target_windows, pupil_bands, pupil_phase, source_weight
        )
    half, fold = freqs // 2, freqs // OV
    tables = wave_constants(pixels, freqs, blocks, src_count, local_x, fold)
    bands = jnp.transpose(pupil_bands, (0, 2, 1))
    phases = pupil_phase.reshape(per_device, 2, half, freqs)
    in_vmem = pl.BlockSpec(memory_space=pltpu.VMEM)
    in_smem = pl.BlockSpec(memory_space=pltpu.SMEM)
    f32 = jnp.float32
    block = (local_x, pixels)
    dma = pltpu.SemaphoreType.DMA
    like = [pltpu.VMEM(one.shape, one.dtype) for one in tables]
    like[4] = pltpu.VMEM(tables[4].shape[1:], tables[4].dtype)
    like[5] = pltpu.VMEM(tables[5].shape[1:], tables[5].dtype)
    four = dma((src_count,))
    grads, terms = pl.pallas_call(
        functools.partial(kernel, src_count, tile_count),
        out_shape=(
            pltpu.VMEM(mask_windows.shape, f32),
            pltpu.VMEM((8, freqs), f32),
        ),
        in_specs=[pl.BlockSpec(memory_space=pltpu.HBM)] * 12,
        out_specs=(in_vmem, in_vmem),
        scratch_shapes=like
        + [
            pltpu.VMEM(mask_windows.shape, f32),
            pltpu.VMEM(target_windows.shape, f32),
            pltpu.VMEM(bands.shape, bands.dtype),
            pltpu.VMEM((2,) + phases.shape, f32),
            pltpu.SMEM(source_weight.shape, f32),
            dma((12,)),
            pltpu.VMEM((blocks, local_x + 8, freqs), f32),
            pltpu.VMEM((2, 2 * per_device, freqs, freqs), f32),
            pltpu.VMEM((2, 2, per_device * local_x, 2 * pixels), f32),
            pltpu.VMEM((4, local_x, 2 * per_device * freqs), f32),
            pltpu.VMEM((2, 16, freqs), f32),
            pltpu.VMEM(block, f32),
            pltpu.VMEM((2,) + block, f32),
            pltpu.VMEM((2,) + block, f32),
            pltpu.VMEM((2, 8, freqs), f32),
            pltpu.VMEM((2, 8, freqs), f32),
            pltpu.VMEM((src_count * local_x, pixels), f32),
            pltpu.VMEM((src_count * local_x, pixels), f32),
            pltpu.VMEM((src_count, local_x + 8, freqs), f32),
            pltpu.VMEM((src_count, local_x + 8, freqs), f32),
            pltpu.VMEM((src_count, 16, freqs), f32),
            pltpu.VMEM((src_count, 16, freqs), f32),
        ]
        + [four] * 4
        + [dma(())] * 2
        + [dma((per_device,))] * 4
        + [dma(())] * 2
        + [dma((2,))] * 4
        + [four] * 4,
        compiler_params=pltpu.CompilerParams(
            collective_id=0, has_side_effects=True, vmem_limit_bytes=63 * 1024 * 1024
        ),
    )(*tables, mask_windows, target_windows, bands, phases, source_weight)
    return finish(grads, terms, source_weight.shape)


def solution(mesh):
    return jax.shard_map(
        shards,
        mesh=mesh,
        in_specs=(
            P(("parts", "tile"), ("src", "row"), None),
            P(("parts", "tile"), ("src", "row"), None),
            P(("parts", "src"), None, None),
            P(("parts", "src"), None, None),
            P(("parts", "src")),
        ),
        out_specs=(P(("parts", "tile"), ("src", "row"), None), P(("parts", "src"))),
        check_vma=False,
    )
```

```python
import functools
import math

import jax
import jax.numpy as jnp
import numpy as np
from jax import lax
from jax.experimental import pallas as pl
from jax.experimental.pallas import tpu as pltpu
from jax.sharding import PartitionSpec as P

M = 256
K = 128
OV = 32


STEEPNESS = 20.0
THRESHOLD = 0.15
LOSS_SCALE = 32.0


def with_halo(block, sides, width):
    for axis, dim in sides:
        count = lax.axis_size(axis)
        forward = [(i, i + 1) for i in range(count - 1)]
        backward = [(target, source) for source, target in forward]
        low = lax.ppermute(
            lax.slice_in_dim(block, block.shape[dim] - width, None, axis=dim), axis, forward
        )
        high = lax.ppermute(lax.slice_in_dim(block, 0, width, axis=dim), axis, backward)
        block = jnp.concatenate([low, block, high], axis=dim)
    return block


def matmul(left_op, right_op):
    return lax.dot_general(
        left_op,
        right_op,
        (((1,), (0,)), ((), ())),
        precision=lax.Precision.HIGHEST,
        preferred_element_type=jnp.float32,
    )


def matmul_tn(left_op, right_op):
    return lax.dot_general(
        left_op,
        right_op,
        (((0,), (0,)), ((), ())),
        precision=lax.Precision.HIGHEST,
        preferred_element_type=jnp.float32,
    )


def matmul_nt(left_op, right_op):
    return lax.dot_general(
        left_op,
        right_op,
        (((1,), (1,)), ((), ())),
        precision=lax.Precision.HIGHEST,
        preferred_element_type=jnp.float32,
    )


def wave_tables(positions):
    freq_index = jnp.arange(K, dtype=jnp.int32) - K // 2
    phase_index = freq_index[:, None] * positions[None, :] % M
    angles = 2.0 * math.pi / M * phase_index.astype(jnp.float32)
    return (jnp.cos(angles), jnp.sin(angles))


def shards_plain(mask_windows, target_windows, pupil_bands, pupil_phase, source_weight):
    src_count = lax.axis_size("src")
    tile_count = lax.axis_size("tile")
    row_count = lax.axis_size("row")
    local_x = mask_windows.shape[1]
    per_device = pupil_phase.shape[0]
    sources = per_device * src_count
    field_scale = 1.0 / (M * K)
    src_id = lax.axis_index("src")
    row_id = lax.axis_index("row")
    x_start = (src_id * row_count + row_id) * local_x
    block_starts = (jnp.arange(src_count, dtype=jnp.int32) * row_count + row_id) * local_x
    row_set = (block_starts[:, None] + jnp.arange(local_x, dtype=jnp.int32)[None, :]).reshape(
        src_count * local_x
    )
    cos_all, sin_all = wave_tables(jnp.arange(M, dtype=jnp.int32))
    cos_set, sin_set = wave_tables(row_set)
    cos_own, sin_own = wave_tables(x_start + jnp.arange(local_x, dtype=jnp.int32))
    window = mask_windows[0]
    goal_block = target_windows[0]
    zero_spec = jnp.zeros((K, K), jnp.float32)
    shard_rows = lax.all_gather(window, ("src", "row"), axis=0, tiled=True)
    part_real = matmul_nt(shard_rows, cos_all)
    part_imag = -matmul_nt(shard_rows, sin_all)
    spec_real = matmul(cos_all, part_real) + matmul(sin_all, part_imag)
    spec_imag = matmul(cos_all, part_imag) - matmul(sin_all, part_real)
    freq_cols = jnp.arange(K, dtype=jnp.int32)
    inside = (freq_cols[None, None, :] >= pupil_bands[:, :, 0:1]) & (
        freq_cols[None, None, :] < pupil_bands[:, :, 1:2]
    )
    passing = inside.astype(jnp.float32)
    pupil_real = passing * jnp.cos(pupil_phase)
    pupil_imag = passing * jnp.sin(pupil_phase)
    amp_real = (pupil_real * spec_real - pupil_imag * spec_imag).reshape(per_device * K, K)
    amp_imag = (pupil_imag * spec_real + pupil_real * spec_imag).reshape(per_device * K, K)
    half_real = (matmul(amp_real, cos_all) - matmul(amp_imag, sin_all)).reshape(per_device, K, M)
    half_imag = (matmul(amp_real, sin_all) + matmul(amp_imag, cos_all)).reshape(per_device, K, M)
    weights = source_weight / sources

    def fields(pair_in):
        one_real, one_imag = pair_in
        field_real = field_scale * (matmul_tn(cos_set, one_real) - matmul_tn(sin_set, one_imag))
        field_imag = field_scale * (matmul_tn(cos_set, one_imag) + matmul_tn(sin_set, one_real))
        return (field_real, field_imag)

    stack_real, stack_imag = lax.map(fields, (half_real, half_imag))
    part_real = stack_real
    part_imag = stack_imag
    intensity = lax.psum_scatter(
        jnp.sum(weights[:, None, None] * (part_real * part_real + part_imag * part_imag), axis=0),
        "src",
        scatter_dimension=0,
        tiled=True,
    )
    resist = jax.nn.sigmoid(STEEPNESS * (intensity - THRESHOLD))
    cotangent = LOSS_SCALE * (resist - goal_block) * STEEPNESS * resist * (1.0 - resist)
    cotangent_all = lax.all_gather(cotangent, "src", axis=0, tiled=True)
    source_ids = jnp.arange(per_device, dtype=jnp.int32)

    def add_back(source_id, totals):
        grad_real, grad_imag, source_terms = totals
        field_real = stack_real[source_id]
        field_imag = stack_imag[source_id]
        back_scale = 2.0 * weights[source_id] * cotangent_all
        back_real = back_scale * field_real
        back_imag = back_scale * field_imag
        adj_real = matmul(cos_set, back_real) + matmul(sin_set, back_imag)
        adj_imag = matmul(cos_set, back_imag) - matmul(sin_set, back_real)
        amp_grad_real = field_scale * (matmul_nt(adj_real, cos_all) + matmul_nt(adj_imag, sin_all))
        amp_grad_imag = field_scale * (matmul_nt(adj_imag, cos_all) - matmul_nt(adj_real, sin_all))
        pass_real = pupil_real[source_id]
        pass_imag = pupil_imag[source_id]
        grad_real = grad_real + pass_real * amp_grad_real + pass_imag * amp_grad_imag
        grad_imag = grad_imag + pass_real * amp_grad_imag - pass_imag * amp_grad_real
        term_value = jnp.sum(cotangent_all * (field_real * field_real + field_imag * field_imag))
        source_terms = source_terms + jnp.where(source_ids == source_id, term_value, 0.0)
        return (grad_real, grad_imag, source_terms)

    grad_real, grad_imag, source_terms = lax.fori_loop(
        0, per_device, add_back, (zero_spec, zero_spec, jnp.zeros((per_device,), jnp.float32))
    )
    grad_real, grad_imag = lax.psum((grad_real, grad_imag), ("src", "row"))
    source_sum = lax.psum(source_terms, ("tile", "row"))
    source_grad = source_sum / (sources * M * tile_count)
    q_one = matmul(grad_real, cos_all) - matmul(grad_imag, sin_all)
    q_two = matmul(grad_real, sin_all) + matmul(grad_imag, cos_all)
    grad_block = matmul_tn(cos_own, q_one) - matmul_tn(sin_own, q_two)
    padded = with_halo(grad_block, (("tile", 1),), OV)
    from_below = padded[:, :OV]
    from_above = padded[:, M + OV :]
    middle = jnp.zeros((local_x, M - 2 * OV), jnp.float32)
    grad_block = grad_block + jnp.concatenate([from_below, middle, from_above], axis=1)
    return (grad_block[None], source_grad)


MESH = pl.DeviceIdType.MESH


def pair(values):
    high = values.astype(jnp.bfloat16)
    return high, (values - high.astype(jnp.float32)).astype(jnp.bfloat16)


def dot_pair(left_op, right_op, contract_right=0):
    dims = (((1,), (contract_right,)), ((), ()))

    def one(a, b):
        return lax.dot_general(a, b, dims, preferred_element_type=jnp.float32)

    (left_high, left_low), (right_high, right_low) = left_op, right_op
    return one(left_high, right_high) + (
        one(left_high, right_low) + one(left_low, right_high)
    )


def frequency_order(freqs):
    half = freqs // 2
    return np.concatenate([np.arange(half), [-half], -np.arange(1, half)])


def wave_constants(pixels, freqs, blocks, src_count, local_x, fold):
    half = freqs // 2
    spots = np.arange(pixels)

    def waves(index):
        angles = 2.0 * np.pi / pixels * (np.outer(index, spots) % pixels)
        return np.cos(angles), np.sin(angles)

    cos_x, sin_x = waves(np.arange(freqs) - half)
    order = frequency_order(freqs)
    cos_y, sin_y = waves(order)
    spectrum = np.concatenate([cos_x, -sin_x], axis=0)
    wave_y = np.block([[cos_y, sin_y], [-sin_y, cos_y]])
    real_rows = np.concatenate([cos_x.T, -sin_x.T], axis=1)
    imag_rows = np.concatenate([sin_x.T, cos_x.T], axis=1)
    wave_rows = np.stack(
        [one.reshape(blocks, local_x, 2 * freqs) for one in (real_rows, imag_rows)], axis=1
    )
    sets = []
    for own in range(blocks):
        src, row = own // 2, own % 2
        mate = (src + src_count // 2) % src_count * 2 + 1 - row
        rows = np.concatenate([np.arange(local_x) + one * local_x for one in (own, mate)])
        c, s = cos_x[:, rows], sin_x[:, rows]
        sets.append(np.block([[c, s], [-s, c]]))
    packed = np.concatenate([cos_y[:half], -sin_y[half:]], axis=0).T
    edges = []
    for start in (pixels - OV, 0):
        table = np.zeros((fold, 2 * freqs, fold, OV))
        for group in range(fold):
            table[group, :freqs, group] = packed[start : start + OV].T
            table[group, freqs + half, group] = cos_y[half, start : start + OV]
        edges.append(table.reshape(fold * 2 * freqs, freqs))
    move = np.zeros((freqs, freqs))
    move[order + half, np.arange(freqs)] = 1.0
    return (
        split_constant(packed),
        split_constant(spectrum),
        split_constant(wave_y),
        split_constant(wave_rows),
        split_constant(np.stack(sets), 1),
        split_constant(np.stack(edges), 1),
        move.astype(jnp.bfloat16),
    )


def split_constant(values, axis=0):
    values = values.astype(np.float32)
    high = values.astype(jnp.bfloat16)
    low = (values - high.astype(np.float32)).astype(jnp.bfloat16)
    return np.stack([high, low], axis=axis)


def sine_cosine(phase):
    quarter = 0.25 * phase
    square = quarter * quarter
    sine = 1.0 / 362880.0
    for term in (-1.0 / 5040.0, 1.0 / 120.0, -1.0 / 6.0, 1.0):
        sine = sine * square + term
    sine = sine * quarter
    fall = -1.0 / 40320.0
    for term in (1.0 / 720.0, -1.0 / 24.0, 0.5):
        fall = fall * square + term
    cosine = 1.0 - fall * square
    twice = 2.0 * sine
    sine, cosine = twice * cosine, 1.0 - twice * sine
    twice = 2.0 * sine
    return twice * cosine, 1.0 - twice * sine


def dot_exact(left_op, right_op, dims=(((1,), (0,)), ((), ()))):
    high, low = pair(left_op)

    def one(a):
        return lax.dot_general(a, right_op, dims, preferred_element_type=jnp.float32)

    return one(high) + one(low)


def kernel(
    src_count,
    tile_count,
    wm_hbm,
    wf_hbm,
    wy_hbm,
    wb_hbm,
    wx_hbm,
    we_hbm,
    move_hbm,
    mask_hbm,
    goal_hbm,
    band_hbm,
    phase_hbm,
    weight_hbm,
    out_ref,
    terms_ref,
    wm_ref,
    wf_ref,
    wy_ref,
    wb_ref,
    wx_ref,
    we_ref,
    move_ref,
    mask_ref,
    goal_ref,
    band_ref,
    phase_ref,
    weight_ref,
    load_sems,
    mbuf,
    pupil_ref,
    fbuf,
    ubuf,
    meta_ref,
    goals_ref,
    part_send,
    part_recv,
    tsend,
    trecv,
    csend,
    crecv,
    gsend,
    grecv,
    hsend,
    hrecv,
    mask_ss,
    mask_rs,
    fwd_ss,
    fwd_rs,
    meta_ss,
    meta_rs,
    phase_ss,
    phase_rs,
    pfwd_ss,
    pfwd_rs,
    goal_ss,
    goal_rs,
    part_ss,
    part_rs,
    core_ss,
    core_rs,
    grad_ss,
    grad_rs,
    halo_ss,
    halo_rs,
):
    part = lax.axis_index("parts")
    src = lax.axis_index("src")
    tile = lax.axis_index("tile")
    row = lax.axis_index("row")
    local_x, pixels = mask_ref.shape[1:]
    per_device, half, freqs = phase_ref.shape[1], phase_ref.shape[3], phase_ref.shape[4]
    sources = per_device * src_count
    field_scale = 1.0 / (pixels * freqs)
    fold = freqs // OV
    depth = local_x // fold
    other_row = 1 - row
    other_tile = 1 - tile
    last = src_count - 1
    own_slot = src * 2 + row
    mate_src = lax.rem(src + src_count // 2, src_count)
    mate_slot = mate_src * 2 + other_row
    pool_src = src + 1 - 2 * lax.rem(src, 2)

    side = lax.div(src, 2)
    far_first = [last * (1 - side), 2 - side, pool_src]
    near_first = far_first[::-1]

    def to(src_ref, dst_ref, ss, rs, src_at=src, tile_at=tile, row_at=other_row):
        return pltpu.make_async_remote_copy(
            src_ref=src_ref,
            dst_ref=dst_ref,
            send_sem=ss,
            recv_sem=rs,
            device_id=(part, src_at, tile_at, row_at),
            device_id_type=MESH,
        )

    barrier = pltpu.get_barrier_semaphore()
    peers = [(peer, tile, other_row) for peer in far_first]
    peers += [(peer, other_tile, other_row) for peer in far_first]
    peers += [(src, tile, other_row), (src, other_tile, row)]
    for src_at, tile_at, row_at in peers:
        pl.semaphore_signal(
            barrier, inc=1, device_id=(part, src_at, tile_at, row_at), device_id_type=MESH
        )

    loads = {}
    for index, (name, source, target) in enumerate(
        [
            ("mask", mask_hbm, mask_ref),
            ("wm", wm_hbm, wm_ref),
            ("weight", weight_hbm, weight_ref),
            ("band", band_hbm, band_ref),
            ("phase", phase_hbm, phase_ref.at[0]),
            ("goal", goal_hbm, goal_ref),
            ("move", move_hbm, move_ref),
            ("wf", wf_hbm, wf_ref),
            ("wb", wb_hbm, wb_ref),
            ("wy", wy_hbm, wy_ref),
            ("wx", wx_hbm.at[own_slot], wx_ref),
            ("we", we_hbm.at[tile], we_ref),
        ]
    ):
        loads[name] = pltpu.make_async_copy(source, target, load_sems.at[index])
        loads[name].start()

    lanes = lax.broadcasted_iota(jnp.int32, (local_x, freqs), 1)
    spots = lax.broadcasted_iota(jnp.int32, (8, pixels), 1)
    turn = spots - 4 * lax.div(spots, 4)
    quarter_wave = jnp.where(turn == 0, 1.0, jnp.where(turn == 2, -1.0, 0.0))
    first_row = lax.broadcasted_iota(jnp.int32, (8, pixels), 0) == 0

    loads["mask"].wait()
    loads["wm"].wait()
    wm = (wm_ref[0], wm_ref[1])
    mask = mask_ref[0]
    mbuf[own_slot, :local_x] = dot_pair(pair(mask), wm)
    quarter_row = jnp.where(first_row, quarter_wave, 0.0).astype(jnp.bfloat16)
    padded = jnp.concatenate([mask, jnp.zeros((freqs - local_x, pixels), jnp.float32)], axis=0)
    high, low = pair(padded)
    nt = (((1,), (1,)), ((), ()))
    mbuf[own_slot, local_x:] = lax.dot_general(
        quarter_row, high, nt, preferred_element_type=jnp.float32
    ) + lax.dot_general(quarter_row, low, nt, preferred_element_type=jnp.float32)
    loads["weight"].wait()
    loads["band"].wait()
    for one in range(per_device):
        meta_ref[0, one : one + 1, :] = jnp.full((1, freqs), weight_ref[one] / sources)
    meta_ref[0, 8:, :] = jnp.concatenate(
        [band_ref[one] for one in range(per_device)]
        + [jnp.zeros((8 - 2 * per_device, freqs), jnp.int32)],
        axis=0,
    ).astype(jnp.float32)
    loads["phase"].wait()
    loads["goal"].wait()
    pl.semaphore_wait(barrier, len(peers))

    copies = []

    def send(*args, **keys):
        copy = to(*args, **keys)
        copy.start()
        copies.append(copy)
        return copy

    own_block = mbuf.at[own_slot]
    for peer in far_first:
        send(own_block, own_block, mask_ss.at[peer], mask_rs.at[src], src_at=peer)
    send(own_block, own_block, fwd_ss.at[src], fwd_rs.at[src])
    send(meta_ref.at[0], meta_ref.at[1], meta_ss, meta_rs, src_at=pool_src)
    for one in range(per_device):
        half_block = phase_ref.at[1, one, row]
        send(
            phase_ref.at[0, one, row],
            half_block,
            phase_ss.at[one],
            phase_rs.at[one],
            src_at=pool_src,
        )

    loads["move"].wait()
    move = move_ref[...]
    columns = lax.broadcasted_iota(jnp.int32, (freqs, freqs), 1).astype(jnp.float32)

    def make_pupil(group, one):
        bands = meta_ref[group, 8:, :].T
        lower, upper = bands[:, 2 * one : 2 * one + 1], bands[:, 2 * one + 1 : 2 * one + 2]
        passing = (columns >= lower) & (columns < upper)
        sine, cosine = sine_cosine(phase_ref[group, one].reshape(freqs, freqs))
        moved = dot_exact(
            jnp.concatenate(
                [jnp.where(passing, cosine, 0.0), jnp.where(passing, sine, 0.0)], axis=0
            ),
            move,
        )
        pupil_ref[group, 2 * one] = moved[:freqs]
        pupil_ref[group, 2 * one + 1] = moved[freqs:]

    for one in range(per_device):
        make_pupil(0, one)
    for name in ("wf", "wb", "wy", "wx", "we"):
        loads[name].wait()

    for index, peer in enumerate(near_first):
        block = mbuf.at[peer * 2 + other_row]
        to(block, block, mask_ss.at[peer], mask_rs.at[peer], src_at=peer).wait_recv()
        send(block, block, fwd_ss.at[peer], fwd_rs.at[peer])
        if index == 0:
            send(goal_ref.at[0], goals_ref, goal_ss, goal_rs, src_at=mate_src)
    for peer in near_first:
        block = mbuf.at[peer * 2 + row]
        to(block, block, fwd_ss.at[peer], fwd_rs.at[peer]).wait_recv()
    block = mbuf.at[src * 2 + other_row]
    to(block, block, fwd_ss.at[src], fwd_rs.at[src]).wait_recv()

    blocks = pixels // local_x
    extra = jnp.concatenate([mbuf[one, local_x : local_x + 1] for one in range(blocks)], axis=0).T
    rows = []
    for one in range(blocks):
        straight = mbuf[one, :local_x]
        turned = pltpu.roll(straight, half, axis=1)
        real = jnp.where(lanes < half, straight, turned)
        real = jnp.where(lanes == half, extra[:local_x, one : one + 1], real)
        imag = jnp.where(lanes < half, -turned, straight)
        imag = jnp.where(lanes == 0, 0.0, imag)
        rows.append(jnp.concatenate([real, imag], axis=1))
    spectrum = dot_pair((wf_ref[0], wf_ref[1]), pair(jnp.concatenate(rows, axis=0)))
    spec_real = spectrum[:freqs, :freqs] - spectrum[freqs:, freqs:]
    spec_imag = spectrum[:freqs, freqs:] + spectrum[freqs:, :freqs]

    wxt = tuple(
        jnp.concatenate(
            [wb_ref[index, slot, side] for side in range(2) for slot in (own_slot, mate_slot)],
            axis=0,
        )
        for index in range(2)
    )
    wy = (wy_ref[0], wy_ref[1])
    for one in range(per_device):
        half_block = phase_ref.at[1, one, other_row]
        to(
            half_block, half_block, phase_ss.at[one], phase_rs.at[one], src_at=pool_src
        ).wait_recv()
        send(half_block, half_block, pfwd_ss.at[one], pfwd_rs.at[one])

    def swept_rows(group):
        reals, imags = [], []
        for one in range(per_device):
            pr, pi = pupil_ref[group, 2 * one], pupil_ref[group, 2 * one + 1]
            reals.append(pr * spec_real - pi * spec_imag)
            imags.append(pi * spec_real + pr * spec_imag)
        amps = jnp.concatenate(
            [jnp.concatenate(reals, axis=1), jnp.concatenate(imags, axis=1)], axis=0
        )
        return dot_pair(wxt, pair(amps)) * field_scale

    to(meta_ref.at[0], meta_ref.at[1], meta_ss, meta_rs, src_at=pool_src).wait_recv()
    weights = [
        jnp.concatenate([meta_ref[group, one : one + 1, :]] * 2, axis=1)
        for group in range(2)
        for one in range(per_device)
    ]

    def light_of(group, swept, block):
        tops = swept[block * local_x : (block + 1) * local_x]
        ends = swept[(2 + block) * local_x : (3 + block) * local_x]
        rows = jnp.concatenate(
            [
                jnp.concatenate(
                    [
                        tops[:, one * freqs : (one + 1) * freqs],
                        ends[:, one * freqs : (one + 1) * freqs],
                    ],
                    axis=1,
                )
                for one in range(per_device)
            ],
            axis=0,
        )
        field = dot_pair(pair(rows), wy)
        fbuf[group, block] = field
        squares = field[:, :pixels] * field[:, :pixels] + field[:, pixels:] * field[:, pixels:]
        total = weights[group * per_device] * squares[:local_x]
        for one in range(1, per_device):
            total = total + (
                weights[group * per_device + one]
                * squares[one * local_x : (one + 1) * local_x]
            )
        return total

    swept = swept_rows(0)
    lights = [light_of(0, swept, block) for block in range(2)]
    for one in range(per_device):
        half_block = phase_ref.at[1, one, row]
        to(half_block, half_block, pfwd_ss.at[one], pfwd_rs.at[one]).wait_recv()
        make_pupil(1, one)
    swept = swept_rows(1)
    for block in (1, 0):
        lights[block] = lights[block] + light_of(1, swept, block)
        part_send[block] = lights[block]
        send(
            part_send.at[block],
            part_recv.at[1 - block],
            part_ss.at[block],
            part_rs.at[1 - block],
            src_at=mate_src,
        )
    to(goal_ref.at[0], goals_ref, goal_ss, goal_rs, src_at=mate_src).wait_recv()

    terms = [jnp.zeros((1, pixels), jnp.float32)] * (2 * per_device)
    for block in (0, 1):
        to(
            part_send.at[1 - block],
            part_recv.at[block],
            part_ss.at[1 - block],
            part_rs.at[block],
            src_at=mate_src,
        ).wait_recv()
        intensity = lights[block] + part_recv[block]
        goal = goal_ref[0] if block == 0 else goals_ref[...]
        resist = 1.0 / (1.0 + jnp.exp(-STEEPNESS * (intensity - THRESHOLD)))
        cotangent = LOSS_SCALE * (resist - goal) * STEEPNESS * resist * (1.0 - resist)
        for group in range(2):
            backs = []
            for one in range(per_device):
                at = group * per_device + one
                field = fbuf[group, block, one * local_x : (one + 1) * local_x]
                real, imag = field[:, :pixels], field[:, pixels:]
                lit_real, lit_imag = cotangent * real, cotangent * imag
                scale = 2.0 * weights[at]
                backs.append(jnp.concatenate([scale * lit_real, scale * lit_imag], axis=1))
                terms[at] = terms[at] + jnp.sum(
                    lit_real * real + lit_imag * imag, axis=0, keepdims=True
                )
            adjoint = dot_pair(pair(jnp.concatenate(backs, axis=0)), wy, 1)
            for one in range(per_device):
                rows = slice(one * local_x, (one + 1) * local_x)
                at = group * per_device + one
                cols = slice(at * freqs, (at + 1) * freqs)
                ubuf[block, :, cols] = adjoint[rows, :freqs]
                ubuf[2 + block, :, cols] = adjoint[rows, freqs:]

    blank = jnp.zeros((1, freqs), jnp.float32)
    for group in range(2):
        tsend[group] = jnp.concatenate(
            [blank]
            + [
                terms[group * per_device + one][:, :freqs]
                + terms[group * per_device + one][:, freqs:]
                for one in range(per_device)
            ]
            + [blank] * (7 - per_device),
            axis=0,
        )
    term_copy = send(tsend, trecv, core_ss.at[src_count], core_rs.at[src_count])

    wx = (wx_ref[0], wx_ref[1])
    swept = ubuf[...].reshape(4 * local_x, 2 * per_device * freqs)
    swept = dot_pair(wx, pair(swept)) * field_scale
    grad_real = jnp.zeros((freqs, freqs), jnp.float32)
    grad_imag = grad_real
    for at in range(2 * per_device):
        group, one = at // per_device, at % per_device
        pr, pi = pupil_ref[group, 2 * one], pupil_ref[group, 2 * one + 1]
        cols = slice(at * freqs, (at + 1) * freqs)
        real, imag = swept[:freqs, cols], swept[freqs:, cols]
        grad_real = grad_real + pr * real + pi * imag
        grad_imag = grad_imag + pr * imag - pi * real

    lane = lax.broadcasted_iota(jnp.int32, (freqs, freqs), 1)
    turn_real = pltpu.roll(grad_real, half, axis=1)
    turn_imag = pltpu.roll(grad_imag, half, axis=1)
    sum_real = grad_real + jnp.where(lane == 0, 0.0, turn_real)
    sum_imag = grad_imag + jnp.where(lane == 0, 0.0, turn_imag)
    gap_real = jnp.where(lane == half, 0.0, turn_real) - grad_real
    gap_imag = jnp.where(lane == half, 0.0, turn_imag) - grad_imag
    upper = jnp.where(lane < half, sum_real, -gap_imag)
    lower = jnp.where(lane < half, sum_imag, gap_real)
    grads = pair(
        jnp.concatenate(
            [
                jnp.concatenate([upper, grad_real], axis=1),
                jnp.concatenate([lower, grad_imag], axis=1),
            ],
            axis=0,
        )
    )

    def rows_of(far_row, own_row):
        slots = [peer * 2 + far_row for peer in far_first] + [src * 2 + own_row]
        waves = tuple(
            jnp.concatenate([wb_ref[index, slot, 0] for slot in slots], axis=0)
            for index in range(2)
        )
        return dot_pair(waves, grads)

    theirs = rows_of(row, other_row)
    for index in range(src_count):
        csend[index] = theirs[index * local_x : (index + 1) * local_x]
        send(csend.at[index], crecv.at[index], core_ss.at[index], core_rs.at[index])
    mine = rows_of(other_row, row)
    term_copy.wait_recv()
    own_terms = tsend[0] + trecv[0]
    pool_terms = tsend[1] + trecv[1]
    for index in range(src_count):
        gsend[index, local_x:] = pool_terms if index < last else own_terms
    sums = []
    for index, peer in enumerate(far_first + [src]):
        to(csend.at[index], crecv.at[index], core_ss.at[index], core_rs.at[index]).wait_recv()
        both = mine[index * local_x : (index + 1) * local_x] + crecv[index]
        gsend[index, :local_x] = both[:, :freqs]
        gsend[index, local_x : local_x + 1, :local_x] = both[:, freqs:].T[half : half + 1]
        if index < last:
            send(
                gsend.at[index], grecv.at[src], grad_ss.at[index], grad_rs.at[src], src_at=peer
            )
        sums.append(both)
    strips = jnp.concatenate(
        [
            jnp.concatenate(
                [
                    sums[index][one * depth : (one + 1) * depth]
                    for one in range(fold)
                ],
                axis=1,
            )
            for index in range(src_count)
        ],
        axis=0,
    )
    strips = dot_pair(pair(strips), (we_ref[0], we_ref[1]))
    for index, peer in enumerate(far_first + [src]):
        hsend[index, :depth] = strips[index * depth : (index + 1) * depth]
        if index >= last - 1:
            hsend[index, depth:] = pool_terms if index < last else own_terms
        tall = depth if index < last - 1 else depth + 8
        send(
            hsend.at[index, :tall],
            hrecv.at[src, :tall],
            halo_ss.at[index],
            halo_rs.at[src],
            src_at=peer,
            tile_at=other_tile,
            row_at=other_row if index < last else row,
        )

    total = gsend[last]
    for peer in near_first:
        to(
            gsend.at[0], grecv.at[peer], grad_ss.at[0], grad_rs.at[peer], src_at=peer
        ).wait_recv()
        total = total + grecv[peer]
    grad_block = dot_pair(pair(total[:local_x]), wm, 1)
    grad_block = grad_block + total[local_x:].T[:local_x, :1] * quarter_wave[:1]
    low, high = grad_block[:, :freqs], grad_block[:, pixels - freqs :]

    packed = jnp.zeros((depth, freqs), jnp.float32)
    for index, peer in enumerate([src] + near_first):
        tall = depth if index > 1 else depth + 8
        to(
            hsend.at[0, :tall],
            hrecv.at[peer, :tall],
            halo_ss.at[0],
            halo_rs.at[peer],
            src_at=peer,
            tile_at=other_tile,
            row_at=row if peer is src else other_row,
        ).wait_recv()
        packed = packed + hrecv[peer, :depth]
    strip = jnp.concatenate(
        [packed]
        + [pltpu.roll(packed, freqs - one * OV, axis=1) for one in range(1, fold)],
        axis=0,
    )
    from_below = jnp.where((lanes < OV) & (tile == 1), strip, 0.0)
    from_above = jnp.where(
        (lanes >= freqs - OV) & (tile == 0), pltpu.roll(strip, freqs - OV, axis=1), 0.0
    )
    out_ref[0, :, :freqs] = low + from_below
    out_ref[0, :, pixels - freqs :] = high + from_above
    terms = own_terms + grecv[pool_src, local_x:]
    terms = terms + (hrecv[src, depth:] + hrecv[pool_src, depth:])
    terms = terms / (sources * pixels * tile_count)
    terms_ref[...] = terms
    for copy in copies:
        copy.wait_send()


def finish_kernel(grads_ref, terms_ref, out_ref, sums_ref, held_ref, sems):
    copy = pltpu.make_async_copy(grads_ref, out_ref, sems.at[0])
    copy.start()
    for one in range(held_ref.shape[0]):
        held_ref[one] = jnp.sum(terms_ref[one + 1 : one + 2, :])
    other = pltpu.make_async_copy(held_ref, sums_ref, sems.at[1])
    other.start()
    copy.wait()
    other.wait()


def finish(grads, terms, shape):
    in_vmem = pl.BlockSpec(memory_space=pltpu.VMEM)
    in_hbm = pl.BlockSpec(memory_space=pltpu.HBM)
    return pl.pallas_call(
        finish_kernel,
        out_shape=(
            jax.ShapeDtypeStruct(grads.shape, grads.dtype),
            jax.ShapeDtypeStruct(shape, terms.dtype),
        ),
        in_specs=[in_vmem, in_vmem],
        out_specs=(in_hbm, in_hbm),
        scratch_shapes=[pltpu.SMEM(shape, terms.dtype), pltpu.SemaphoreType.DMA((2,))],
    )(*(pltpu.with_memory_space_constraint(one, pltpu.VMEM) for one in (grads, terms)))


def shards(mask_windows, target_windows, pupil_bands, pupil_phase, source_weight):
    src_count = lax.axis_size("src")
    tile_count = lax.axis_size("tile")
    row_count = lax.axis_size("row")
    local_x, pixels = mask_windows.shape[1:]
    per_device, freqs = pupil_phase.shape[:2]
    blocks = src_count * row_count
    fits = row_count == 2 and tile_count == 2 and src_count == 4 and 2 * per_device <= 8
    fits = fits and freqs == 128 and pixels == 2 * freqs and local_x == OV
    if not fits or local_x * blocks != pixels or OV * 4 != freqs:
        return shards_plain(
            mask_windows, target_windows, pupil_bands, pupil_phase, source_weight
        )
    half, fold = freqs // 2, freqs // OV
    tables = wave_constants(pixels, freqs, blocks, src_count, local_x, fold)
    bands = jnp.transpose(pupil_bands, (0, 2, 1))
    phases = pupil_phase.reshape(per_device, 2, half, freqs)
    in_vmem = pl.BlockSpec(memory_space=pltpu.VMEM)
    in_smem = pl.BlockSpec(memory_space=pltpu.SMEM)
    f32 = jnp.float32
    block = (local_x, pixels)
    dma = pltpu.SemaphoreType.DMA
    like = [pltpu.VMEM(one.shape, one.dtype) for one in tables]
    like[4] = pltpu.VMEM(tables[4].shape[1:], tables[4].dtype)
    like[5] = pltpu.VMEM(tables[5].shape[1:], tables[5].dtype)
    four = dma((src_count,))
    grads, terms = pl.pallas_call(
        functools.partial(kernel, src_count, tile_count),
        out_shape=(
            pltpu.VMEM(mask_windows.shape, f32),
            pltpu.VMEM((8, freqs), f32),
        ),
        in_specs=[pl.BlockSpec(memory_space=pltpu.HBM)] * 12,
        out_specs=(in_vmem, in_vmem),
        scratch_shapes=like
        + [
            pltpu.VMEM(mask_windows.shape, f32),
            pltpu.VMEM(target_windows.shape, f32),
            pltpu.VMEM(bands.shape, bands.dtype),
            pltpu.VMEM((2,) + phases.shape, f32),
            pltpu.SMEM(source_weight.shape, f32),
            dma((12,)),
            pltpu.VMEM((blocks, local_x + 8, freqs), f32),
            pltpu.VMEM((2, 2 * per_device, freqs, freqs), f32),
            pltpu.VMEM((2, 2, per_device * local_x, 2 * pixels), f32),
            pltpu.VMEM((4, local_x, 2 * per_device * freqs), f32),
            pltpu.VMEM((2, 16, freqs), f32),
            pltpu.VMEM(block, f32),
            pltpu.VMEM((2,) + block, f32),
            pltpu.VMEM((2,) + block, f32),
            pltpu.VMEM((2, 8, freqs), f32),
            pltpu.VMEM((2, 8, freqs), f32),
            pltpu.VMEM((src_count,) + block, f32),
            pltpu.VMEM((src_count,) + block, f32),
            pltpu.VMEM((src_count, local_x + 8, freqs), f32),
            pltpu.VMEM((src_count, local_x + 8, freqs), f32),
            pltpu.VMEM((src_count, 16, freqs), f32),
            pltpu.VMEM((src_count, 16, freqs), f32),
        ]
        + [four] * 4
        + [dma(())] * 2
        + [dma((per_device,))] * 4
        + [dma(())] * 2
        + [dma((2,))] * 2
        + [dma((src_count + 1,))] * 2
        + [four] * 4,
        compiler_params=pltpu.CompilerParams(
            collective_id=0, has_side_effects=True, vmem_limit_bytes=63 * 1024 * 1024
        ),
    )(*tables, mask_windows, target_windows, bands, phases, source_weight)
    return finish(grads, terms, source_weight.shape)


def solution(mesh):
    return jax.shard_map(
        shards,
        mesh=mesh,
        in_specs=(
            P(("parts", "tile"), ("src", "row"), None),
            P(("parts", "tile"), ("src", "row"), None),
            P(("parts", "src"), None, None),
            P(("parts", "src"), None, None),
            P(("parts", "src")),
        ),
        out_specs=(P(("parts", "tile"), ("src", "row"), None), P(("parts", "src"))),
        check_vma=False,
    )
```

```python
import functools
import math

import jax
import jax.numpy as jnp
import numpy as np
from jax import lax
from jax.experimental import pallas as pl
from jax.experimental.pallas import tpu as pltpu
from jax.sharding import PartitionSpec as P

M = 256
K = 128
OV = 32


STEEPNESS = 20.0
THRESHOLD = 0.15
LOSS_SCALE = 32.0


def with_halo(block, sides, width):
    for axis, dim in sides:
        count = lax.axis_size(axis)
        forward = [(i, i + 1) for i in range(count - 1)]
        backward = [(target, source) for source, target in forward]
        low = lax.ppermute(
            lax.slice_in_dim(block, block.shape[dim] - width, None, axis=dim), axis, forward
        )
        high = lax.ppermute(lax.slice_in_dim(block, 0, width, axis=dim), axis, backward)
        block = jnp.concatenate([low, block, high], axis=dim)
    return block


def matmul(left_op, right_op):
    return lax.dot_general(
        left_op,
        right_op,
        (((1,), (0,)), ((), ())),
        precision=lax.Precision.HIGHEST,
        preferred_element_type=jnp.float32,
    )


def matmul_tn(left_op, right_op):
    return lax.dot_general(
        left_op,
        right_op,
        (((0,), (0,)), ((), ())),
        precision=lax.Precision.HIGHEST,
        preferred_element_type=jnp.float32,
    )


def matmul_nt(left_op, right_op):
    return lax.dot_general(
        left_op,
        right_op,
        (((1,), (1,)), ((), ())),
        precision=lax.Precision.HIGHEST,
        preferred_element_type=jnp.float32,
    )


def wave_tables(positions):
    freq_index = jnp.arange(K, dtype=jnp.int32) - K // 2
    phase_index = freq_index[:, None] * positions[None, :] % M
    angles = 2.0 * math.pi / M * phase_index.astype(jnp.float32)
    return (jnp.cos(angles), jnp.sin(angles))


def shards_plain(mask_windows, target_windows, pupil_bands, pupil_phase, source_weight):
    src_count = lax.axis_size("src")
    tile_count = lax.axis_size("tile")
    row_count = lax.axis_size("row")
    local_x = mask_windows.shape[1]
    per_device = pupil_phase.shape[0]
    sources = per_device * src_count
    field_scale = 1.0 / (M * K)
    src_id = lax.axis_index("src")
    row_id = lax.axis_index("row")
    x_start = (src_id * row_count + row_id) * local_x
    block_starts = (jnp.arange(src_count, dtype=jnp.int32) * row_count + row_id) * local_x
    row_set = (block_starts[:, None] + jnp.arange(local_x, dtype=jnp.int32)[None, :]).reshape(
        src_count * local_x
    )
    cos_all, sin_all = wave_tables(jnp.arange(M, dtype=jnp.int32))
    cos_set, sin_set = wave_tables(row_set)
    cos_own, sin_own = wave_tables(x_start + jnp.arange(local_x, dtype=jnp.int32))
    window = mask_windows[0]
    goal_block = target_windows[0]
    zero_spec = jnp.zeros((K, K), jnp.float32)
    shard_rows = lax.all_gather(window, ("src", "row"), axis=0, tiled=True)
    part_real = matmul_nt(shard_rows, cos_all)
    part_imag = -matmul_nt(shard_rows, sin_all)
    spec_real = matmul(cos_all, part_real) + matmul(sin_all, part_imag)
    spec_imag = matmul(cos_all, part_imag) - matmul(sin_all, part_real)
    freq_cols = jnp.arange(K, dtype=jnp.int32)
    inside = (freq_cols[None, None, :] >= pupil_bands[:, :, 0:1]) & (
        freq_cols[None, None, :] < pupil_bands[:, :, 1:2]
    )
    passing = inside.astype(jnp.float32)
    pupil_real = passing * jnp.cos(pupil_phase)
    pupil_imag = passing * jnp.sin(pupil_phase)
    amp_real = (pupil_real * spec_real - pupil_imag * spec_imag).reshape(per_device * K, K)
    amp_imag = (pupil_imag * spec_real + pupil_real * spec_imag).reshape(per_device * K, K)
    half_real = (matmul(amp_real, cos_all) - matmul(amp_imag, sin_all)).reshape(per_device, K, M)
    half_imag = (matmul(amp_real, sin_all) + matmul(amp_imag, cos_all)).reshape(per_device, K, M)
    weights = source_weight / sources

    def fields(pair_in):
        one_real, one_imag = pair_in
        field_real = field_scale * (matmul_tn(cos_set, one_real) - matmul_tn(sin_set, one_imag))
        field_imag = field_scale * (matmul_tn(cos_set, one_imag) + matmul_tn(sin_set, one_real))
        return (field_real, field_imag)

    stack_real, stack_imag = lax.map(fields, (half_real, half_imag))
    part_real = stack_real
    part_imag = stack_imag
    intensity = lax.psum_scatter(
        jnp.sum(weights[:, None, None] * (part_real * part_real + part_imag * part_imag), axis=0),
        "src",
        scatter_dimension=0,
        tiled=True,
    )
    resist = jax.nn.sigmoid(STEEPNESS * (intensity - THRESHOLD))
    cotangent = LOSS_SCALE * (resist - goal_block) * STEEPNESS * resist * (1.0 - resist)
    cotangent_all = lax.all_gather(cotangent, "src", axis=0, tiled=True)
    source_ids = jnp.arange(per_device, dtype=jnp.int32)

    def add_back(source_id, totals):
        grad_real, grad_imag, source_terms = totals
        field_real = stack_real[source_id]
        field_imag = stack_imag[source_id]
        back_scale = 2.0 * weights[source_id] * cotangent_all
        back_real = back_scale * field_real
        back_imag = back_scale * field_imag
        adj_real = matmul(cos_set, back_real) + matmul(sin_set, back_imag)
        adj_imag = matmul(cos_set, back_imag) - matmul(sin_set, back_real)
        amp_grad_real = field_scale * (matmul_nt(adj_real, cos_all) + matmul_nt(adj_imag, sin_all))
        amp_grad_imag = field_scale * (matmul_nt(adj_imag, cos_all) - matmul_nt(adj_real, sin_all))
        pass_real = pupil_real[source_id]
        pass_imag = pupil_imag[source_id]
        grad_real = grad_real + pass_real * amp_grad_real + pass_imag * amp_grad_imag
        grad_imag = grad_imag + pass_real * amp_grad_imag - pass_imag * amp_grad_real
        term_value = jnp.sum(cotangent_all * (field_real * field_real + field_imag * field_imag))
        source_terms = source_terms + jnp.where(source_ids == source_id, term_value, 0.0)
        return (grad_real, grad_imag, source_terms)

    grad_real, grad_imag, source_terms = lax.fori_loop(
        0, per_device, add_back, (zero_spec, zero_spec, jnp.zeros((per_device,), jnp.float32))
    )
    grad_real, grad_imag = lax.psum((grad_real, grad_imag), ("src", "row"))
    source_sum = lax.psum(source_terms, ("tile", "row"))
    source_grad = source_sum / (sources * M * tile_count)
    q_one = matmul(grad_real, cos_all) - matmul(grad_imag, sin_all)
    q_two = matmul(grad_real, sin_all) + matmul(grad_imag, cos_all)
    grad_block = matmul_tn(cos_own, q_one) - matmul_tn(sin_own, q_two)
    padded = with_halo(grad_block, (("tile", 1),), OV)
    from_below = padded[:, :OV]
    from_above = padded[:, M + OV :]
    middle = jnp.zeros((local_x, M - 2 * OV), jnp.float32)
    grad_block = grad_block + jnp.concatenate([from_below, middle, from_above], axis=1)
    return (grad_block[None], source_grad)


MESH = pl.DeviceIdType.MESH


def pair(values):
    high = values.astype(jnp.bfloat16)
    return high, (values - high.astype(jnp.float32)).astype(jnp.bfloat16)


def dot_pair(left_op, right_op, contract_right=0):
    dims = (((1,), (contract_right,)), ((), ()))

    def one(a, b):
        return lax.dot_general(a, b, dims, preferred_element_type=jnp.float32)

    (left_high, left_low), (right_high, right_low) = left_op, right_op
    return one(left_high, right_high) + (
        one(left_high, right_low) + one(left_low, right_high)
    )


def frequency_order(freqs):
    half = freqs // 2
    return np.concatenate([np.arange(half), [-half], -np.arange(1, half)])


def wave_constants(pixels, freqs, blocks, src_count, local_x, fold):
    half = freqs // 2
    spots = np.arange(pixels)

    def waves(index):
        angles = 2.0 * np.pi / pixels * (np.outer(index, spots) % pixels)
        return np.cos(angles), np.sin(angles)

    cos_x, sin_x = waves(np.arange(freqs) - half)
    order = frequency_order(freqs)
    cos_y, sin_y = waves(order)
    spectrum = np.concatenate([cos_x, -sin_x], axis=0)
    wave_y = np.block([[cos_y, sin_y], [-sin_y, cos_y]])
    real_rows = np.concatenate([cos_x.T, -sin_x.T], axis=1)
    imag_rows = np.concatenate([sin_x.T, cos_x.T], axis=1)
    wave_rows = np.stack(
        [one.reshape(blocks, local_x, 2 * freqs) for one in (real_rows, imag_rows)], axis=1
    )
    sets = []
    for own in range(blocks):
        src, row = own // 2, own % 2
        mate = (src + src_count // 2) % src_count * 2 + 1 - row
        rows = np.concatenate([np.arange(local_x) + one * local_x for one in (own, mate)])
        c, s = cos_x[:, rows], sin_x[:, rows]
        sets.append(np.block([[c, s], [-s, c]]))
    packed = np.concatenate([cos_y[:half], -sin_y[half:]], axis=0).T
    edges = []
    for start in (pixels - OV, 0):
        table = np.zeros((fold, 2 * freqs, fold, OV))
        for group in range(fold):
            table[group, :freqs, group] = packed[start : start + OV].T
            table[group, freqs + half, group] = cos_y[half, start : start + OV]
        edges.append(table.reshape(fold * 2 * freqs, freqs))
    move = np.zeros((freqs, freqs))
    move[order + half, np.arange(freqs)] = 1.0
    return (
        split_constant(packed),
        split_constant(spectrum),
        split_constant(wave_y),
        split_constant(wave_rows),
        split_constant(np.stack(sets), 1),
        split_constant(np.stack(edges), 1),
        move.astype(jnp.bfloat16),
    )


def split_constant(values, axis=0):
    values = values.astype(np.float32)
    high = values.astype(jnp.bfloat16)
    low = (values - high.astype(np.float32)).astype(jnp.bfloat16)
    return np.stack([high, low], axis=axis)


def sine_cosine(phase):
    quarter = 0.25 * phase
    square = quarter * quarter
    sine = 1.0 / 362880.0
    for term in (-1.0 / 5040.0, 1.0 / 120.0, -1.0 / 6.0, 1.0):
        sine = sine * square + term
    sine = sine * quarter
    fall = -1.0 / 40320.0
    for term in (1.0 / 720.0, -1.0 / 24.0, 0.5):
        fall = fall * square + term
    cosine = 1.0 - fall * square
    twice = 2.0 * sine
    sine, cosine = twice * cosine, 1.0 - twice * sine
    twice = 2.0 * sine
    return twice * cosine, 1.0 - twice * sine


def dot_exact(left_op, right_op, dims=(((1,), (0,)), ((), ()))):
    high, low = pair(left_op)

    def one(a):
        return lax.dot_general(a, right_op, dims, preferred_element_type=jnp.float32)

    return one(high) + one(low)


def kernel(
    src_count,
    tile_count,
    wm_hbm,
    wf_hbm,
    wy_hbm,
    wb_hbm,
    wx_hbm,
    we_hbm,
    move_hbm,
    mask_hbm,
    goal_hbm,
    band_hbm,
    phase_hbm,
    weight_hbm,
    out_ref,
    terms_ref,
    wm_ref,
    wf_ref,
    wy_ref,
    wb_ref,
    wx_ref,
    we_ref,
    move_ref,
    mask_ref,
    goal_ref,
    band_ref,
    phase_ref,
    weight_ref,
    load_sems,
    mbuf,
    pupil_ref,
    fbuf,
    ubuf,
    meta_ref,
    goals_ref,
    part_send,
    part_recv,
    tsend,
    trecv,
    csend,
    crecv,
    gsend,
    grecv,
    hsend,
    hrecv,
    mask_ss,
    mask_rs,
    fwd_ss,
    fwd_rs,
    meta_ss,
    meta_rs,
    phase_ss,
    phase_rs,
    pfwd_ss,
    pfwd_rs,
    goal_ss,
    goal_rs,
    part_ss,
    part_rs,
    core_ss,
    core_rs,
    grad_ss,
    grad_rs,
    halo_ss,
    halo_rs,
):
    part = lax.axis_index("parts")
    src = lax.axis_index("src")
    tile = lax.axis_index("tile")
    row = lax.axis_index("row")
    local_x, pixels = mask_ref.shape[1:]
    per_device, half, freqs = phase_ref.shape[1], phase_ref.shape[3], phase_ref.shape[4]
    sources = per_device * src_count
    field_scale = 1.0 / (pixels * freqs)
    fold = freqs // OV
    depth = local_x // fold
    other_row = 1 - row
    other_tile = 1 - tile
    last = src_count - 1
    own_slot = src * 2 + row
    mate_src = lax.rem(src + src_count // 2, src_count)
    mate_slot = mate_src * 2 + other_row
    pool_src = src + 1 - 2 * lax.rem(src, 2)

    side = lax.div(src, 2)
    far_first = [last * (1 - side), 2 - side, pool_src]
    near_first = far_first[::-1]

    def to(src_ref, dst_ref, ss, rs, src_at=src, tile_at=tile, row_at=other_row):
        return pltpu.make_async_remote_copy(
            src_ref=src_ref,
            dst_ref=dst_ref,
            send_sem=ss,
            recv_sem=rs,
            device_id=(part, src_at, tile_at, row_at),
            device_id_type=MESH,
        )

    barrier = pltpu.get_barrier_semaphore()
    peers = [(peer, tile, other_row) for peer in far_first]
    peers += [(src, tile, other_row), (src, other_tile, other_row)]
    for src_at, tile_at, row_at in peers:
        pl.semaphore_signal(
            barrier, inc=1, device_id=(part, src_at, tile_at, row_at), device_id_type=MESH
        )

    loads = {}
    for index, (name, source, target) in enumerate(
        [
            ("mask", mask_hbm, mask_ref),
            ("wm", wm_hbm, wm_ref),
            ("weight", weight_hbm, weight_ref),
            ("band", band_hbm, band_ref),
            ("phase", phase_hbm, phase_ref.at[0]),
            ("goal", goal_hbm, goal_ref),
            ("move", move_hbm, move_ref),
            ("wf", wf_hbm, wf_ref),
            ("wb", wb_hbm, wb_ref),
            ("wy", wy_hbm, wy_ref),
            ("wx", wx_hbm.at[own_slot], wx_ref),
            ("we", we_hbm.at[tile], we_ref),
        ]
    ):
        loads[name] = pltpu.make_async_copy(source, target, load_sems.at[index])
        loads[name].start()

    lanes = lax.broadcasted_iota(jnp.int32, (local_x, freqs), 1)
    spots = lax.broadcasted_iota(jnp.int32, (8, pixels), 1)
    turn = spots - 4 * lax.div(spots, 4)
    quarter_wave = jnp.where(turn == 0, 1.0, jnp.where(turn == 2, -1.0, 0.0))
    first_row = lax.broadcasted_iota(jnp.int32, (8, pixels), 0) == 0

    loads["mask"].wait()
    loads["wm"].wait()
    wm = (wm_ref[0], wm_ref[1])
    mask = mask_ref[0]
    mbuf[own_slot, :local_x] = dot_pair(pair(mask), wm)
    quarter_row = jnp.where(first_row, quarter_wave, 0.0).astype(jnp.bfloat16)
    padded = jnp.concatenate([mask, jnp.zeros((freqs - local_x, pixels), jnp.float32)], axis=0)
    high, low = pair(padded)
    nt = (((1,), (1,)), ((), ()))
    mbuf[own_slot, local_x:] = lax.dot_general(
        quarter_row, high, nt, preferred_element_type=jnp.float32
    ) + lax.dot_general(quarter_row, low, nt, preferred_element_type=jnp.float32)
    loads["weight"].wait()
    loads["band"].wait()
    for one in range(per_device):
        meta_ref[0, one : one + 1, :] = jnp.full((1, freqs), weight_ref[one] / sources)
    meta_ref[0, 8:, :] = jnp.concatenate(
        [band_ref[one] for one in range(per_device)]
        + [jnp.zeros((8 - 2 * per_device, freqs), jnp.int32)],
        axis=0,
    ).astype(jnp.float32)
    loads["phase"].wait()
    loads["goal"].wait()
    pl.semaphore_wait(barrier, len(peers))

    copies = []

    def send(*args, **keys):
        copy = to(*args, **keys)
        copy.start()
        copies.append(copy)
        return copy

    own_block = mbuf.at[own_slot]
    for peer in far_first:
        send(own_block, own_block, mask_ss.at[peer], mask_rs.at[src], src_at=peer)
    send(own_block, own_block, fwd_ss.at[src], fwd_rs.at[src])
    send(meta_ref.at[0], meta_ref.at[1], meta_ss, meta_rs, src_at=pool_src)
    for one in range(per_device):
        half_block = phase_ref.at[1, one, row]
        send(
            phase_ref.at[0, one, row],
            half_block,
            phase_ss.at[one],
            phase_rs.at[one],
            src_at=pool_src,
        )

    loads["move"].wait()
    move = move_ref[...]
    columns = lax.broadcasted_iota(jnp.int32, (freqs, freqs), 1).astype(jnp.float32)

    def make_pupil(group, one):
        bands = meta_ref[group, 8:, :].T
        lower, upper = bands[:, 2 * one : 2 * one + 1], bands[:, 2 * one + 1 : 2 * one + 2]
        passing = (columns >= lower) & (columns < upper)
        sine, cosine = sine_cosine(phase_ref[group, one].reshape(freqs, freqs))
        moved = dot_exact(
            jnp.concatenate(
                [jnp.where(passing, cosine, 0.0), jnp.where(passing, sine, 0.0)], axis=0
            ),
            move,
        )
        pupil_ref[group, 2 * one] = moved[:freqs]
        pupil_ref[group, 2 * one + 1] = moved[freqs:]

    for one in range(per_device):
        make_pupil(0, one)
    for name in ("wf", "wb", "wy", "wx", "we"):
        loads[name].wait()

    for index, peer in enumerate(near_first):
        block = mbuf.at[peer * 2 + other_row]
        to(block, block, mask_ss.at[peer], mask_rs.at[peer], src_at=peer).wait_recv()
        send(block, block, fwd_ss.at[peer], fwd_rs.at[peer])
        if index == 0:
            send(goal_ref.at[0], goals_ref, goal_ss, goal_rs, src_at=mate_src)
    for peer in near_first:
        block = mbuf.at[peer * 2 + row]
        to(block, block, fwd_ss.at[peer], fwd_rs.at[peer]).wait_recv()
    block = mbuf.at[src * 2 + other_row]
    to(block, block, fwd_ss.at[src], fwd_rs.at[src]).wait_recv()

    blocks = pixels // local_x
    extra = jnp.concatenate([mbuf[one, local_x : local_x + 1] for one in range(blocks)], axis=0).T
    rows = []
    for one in range(blocks):
        straight = mbuf[one, :local_x]
        turned = pltpu.roll(straight, half, axis=1)
        real = jnp.where(lanes < half, straight, turned)
        real = jnp.where(lanes == half, extra[:local_x, one : one + 1], real)
        imag = jnp.where(lanes < half, -turned, straight)
        imag = jnp.where(lanes == 0, 0.0, imag)
        rows.append(jnp.concatenate([real, imag], axis=1))
    spectrum = dot_pair((wf_ref[0], wf_ref[1]), pair(jnp.concatenate(rows, axis=0)))
    spec_real = spectrum[:freqs, :freqs] - spectrum[freqs:, freqs:]
    spec_imag = spectrum[:freqs, freqs:] + spectrum[freqs:, :freqs]

    wxt = tuple(
        jnp.concatenate(
            [wb_ref[index, slot, side] for side in range(2) for slot in (own_slot, mate_slot)],
            axis=0,
        )
        for index in range(2)
    )
    wy = (wy_ref[0], wy_ref[1])
    for one in range(per_device):
        half_block = phase_ref.at[1, one, other_row]
        to(
            half_block, half_block, phase_ss.at[one], phase_rs.at[one], src_at=pool_src
        ).wait_recv()
        send(half_block, half_block, pfwd_ss.at[one], pfwd_rs.at[one])

    def swept_rows(group):
        reals, imags = [], []
        for one in range(per_device):
            pr, pi = pupil_ref[group, 2 * one], pupil_ref[group, 2 * one + 1]
            reals.append(pr * spec_real - pi * spec_imag)
            imags.append(pi * spec_real + pr * spec_imag)
        amps = jnp.concatenate(
            [jnp.concatenate(reals, axis=1), jnp.concatenate(imags, axis=1)], axis=0
        )
        return dot_pair(wxt, pair(amps)) * field_scale

    to(meta_ref.at[0], meta_ref.at[1], meta_ss, meta_rs, src_at=pool_src).wait_recv()
    weights = [
        jnp.concatenate([meta_ref[group, one : one + 1, :]] * 2, axis=1)
        for group in range(2)
        for one in range(per_device)
    ]

    def light_of(group, swept, block):
        tops = swept[block * local_x : (block + 1) * local_x]
        ends = swept[(2 + block) * local_x : (3 + block) * local_x]
        rows = jnp.concatenate(
            [
                jnp.concatenate(
                    [
                        tops[:, one * freqs : (one + 1) * freqs],
                        ends[:, one * freqs : (one + 1) * freqs],
                    ],
                    axis=1,
                )
                for one in range(per_device)
            ],
            axis=0,
        )
        field = dot_pair(pair(rows), wy)
        fbuf[group, block] = field
        squares = field[:, :pixels] * field[:, :pixels] + field[:, pixels:] * field[:, pixels:]
        total = weights[group * per_device] * squares[:local_x]
        for one in range(1, per_device):
            total = total + (
                weights[group * per_device + one]
                * squares[one * local_x : (one + 1) * local_x]
            )
        return total

    swept = swept_rows(0)
    lights = [light_of(0, swept, block) for block in range(2)]
    for one in range(per_device):
        half_block = phase_ref.at[1, one, row]
        to(half_block, half_block, pfwd_ss.at[one], pfwd_rs.at[one]).wait_recv()
        make_pupil(1, one)
    swept = swept_rows(1)
    for block in (1, 0):
        lights[block] = lights[block] + light_of(1, swept, block)
        part_send[block] = lights[block]
        send(
            part_send.at[block],
            part_recv.at[1 - block],
            part_ss.at[block],
            part_rs.at[1 - block],
            src_at=mate_src,
        )
    to(goal_ref.at[0], goals_ref, goal_ss, goal_rs, src_at=mate_src).wait_recv()

    terms = [jnp.zeros((1, pixels), jnp.float32)] * (2 * per_device)
    for block in (0, 1):
        to(
            part_send.at[1 - block],
            part_recv.at[block],
            part_ss.at[1 - block],
            part_rs.at[block],
            src_at=mate_src,
        ).wait_recv()
        intensity = lights[block] + part_recv[block]
        goal = goal_ref[0] if block == 0 else goals_ref[...]
        resist = 1.0 / (1.0 + jnp.exp(-STEEPNESS * (intensity - THRESHOLD)))
        cotangent = LOSS_SCALE * (resist - goal) * STEEPNESS * resist * (1.0 - resist)
        for group in range(2):
            backs = []
            for one in range(per_device):
                at = group * per_device + one
                field = fbuf[group, block, one * local_x : (one + 1) * local_x]
                real, imag = field[:, :pixels], field[:, pixels:]
                lit_real, lit_imag = cotangent * real, cotangent * imag
                scale = 2.0 * weights[at]
                backs.append(jnp.concatenate([scale * lit_real, scale * lit_imag], axis=1))
                terms[at] = terms[at] + jnp.sum(
                    lit_real * real + lit_imag * imag, axis=0, keepdims=True
                )
            adjoint = dot_pair(pair(jnp.concatenate(backs, axis=0)), wy, 1)
            for one in range(per_device):
                rows = slice(one * local_x, (one + 1) * local_x)
                at = group * per_device + one
                cols = slice(at * freqs, (at + 1) * freqs)
                ubuf[block, :, cols] = adjoint[rows, :freqs]
                ubuf[2 + block, :, cols] = adjoint[rows, freqs:]

    blank = jnp.zeros((1, freqs), jnp.float32)
    for group in range(2):
        tsend[group] = jnp.concatenate(
            [blank]
            + [
                terms[group * per_device + one][:, :freqs]
                + terms[group * per_device + one][:, freqs:]
                for one in range(per_device)
            ]
            + [blank] * (7 - per_device),
            axis=0,
        )
    term_copy = send(tsend, trecv, core_ss.at[src_count], core_rs.at[src_count])

    wx = (wx_ref[0], wx_ref[1])
    swept = ubuf[...].reshape(4 * local_x, 2 * per_device * freqs)
    swept = dot_pair(wx, pair(swept)) * field_scale
    grad_real = jnp.zeros((freqs, freqs), jnp.float32)
    grad_imag = grad_real
    for at in range(2 * per_device):
        group, one = at // per_device, at % per_device
        pr, pi = pupil_ref[group, 2 * one], pupil_ref[group, 2 * one + 1]
        cols = slice(at * freqs, (at + 1) * freqs)
        real, imag = swept[:freqs, cols], swept[freqs:, cols]
        grad_real = grad_real + pr * real + pi * imag
        grad_imag = grad_imag + pr * imag - pi * real

    lane = lax.broadcasted_iota(jnp.int32, (freqs, freqs), 1)
    turn_real = pltpu.roll(grad_real, half, axis=1)
    turn_imag = pltpu.roll(grad_imag, half, axis=1)
    sum_real = grad_real + jnp.where(lane == 0, 0.0, turn_real)
    sum_imag = grad_imag + jnp.where(lane == 0, 0.0, turn_imag)
    gap_real = jnp.where(lane == half, 0.0, turn_real) - grad_real
    gap_imag = jnp.where(lane == half, 0.0, turn_imag) - grad_imag
    upper = jnp.where(lane < half, sum_real, -gap_imag)
    lower = jnp.where(lane < half, sum_imag, gap_real)
    grads = pair(
        jnp.concatenate(
            [
                jnp.concatenate([upper, grad_real], axis=1),
                jnp.concatenate([lower, grad_imag], axis=1),
            ],
            axis=0,
        )
    )

    def rows_of(far_row, own_row):
        slots = [peer * 2 + far_row for peer in far_first] + [src * 2 + own_row]
        waves = tuple(
            jnp.concatenate([wb_ref[index, slot, 0] for slot in slots], axis=0)
            for index in range(2)
        )
        return dot_pair(waves, grads)

    theirs = rows_of(row, other_row)
    for index in range(src_count):
        csend[index] = theirs[index * local_x : (index + 1) * local_x]
        send(csend.at[index], crecv.at[index], core_ss.at[index], core_rs.at[index])
    mine = rows_of(other_row, row)
    strips = jnp.concatenate(
        [
            jnp.concatenate(
                [
                    blocks_of[
                        index * local_x + one * depth : index * local_x + (one + 1) * depth
                    ]
                    for one in range(fold)
                ],
                axis=1,
            )
            for blocks_of in (theirs, mine)
            for index in range(src_count)
        ],
        axis=0,
    )
    strips = dot_pair(pair(strips), (we_ref[0], we_ref[1]))
    for side, near_row, far_row in ((0, other_row, row), (1, row, other_row)):
        for index, peer in enumerate(far_first + [src]):
            at = side * src_count + index
            hsend[at, :depth] = strips[at * depth : (at + 1) * depth]
            tall = depth if index < last - 1 else depth + 8
            if index >= last - 1:
                hsend[at, depth:] = tsend[last - index]
            send(
                hsend.at[at, :tall],
                hrecv.at[own_slot, :tall],
                halo_ss.at[at],
                halo_rs.at[own_slot],
                src_at=peer,
                tile_at=other_tile,
                row_at=far_row if index < last else near_row,
            )
    term_copy.wait_recv()
    own_terms = tsend[0] + trecv[0]
    pool_terms = tsend[1] + trecv[1]
    for index in range(src_count):
        gsend[index, local_x:] = pool_terms if index < last else own_terms
    for index, peer in enumerate(far_first + [src]):
        to(csend.at[index], crecv.at[index], core_ss.at[index], core_rs.at[index]).wait_recv()
        both = mine[index * local_x : (index + 1) * local_x] + crecv[index]
        gsend[index, :local_x] = both[:, :freqs]
        gsend[index, local_x : local_x + 1, :local_x] = both[:, freqs:].T[half : half + 1]
        if index < last:
            send(
                gsend.at[index], grecv.at[src], grad_ss.at[index], grad_rs.at[src], src_at=peer
            )

    total = gsend[last]
    for peer in near_first:
        to(
            gsend.at[0], grecv.at[peer], grad_ss.at[0], grad_rs.at[peer], src_at=peer
        ).wait_recv()
        total = total + grecv[peer]
    grad_block = dot_pair(pair(total[:local_x]), wm, 1)
    grad_block = grad_block + total[local_x:].T[:local_x, :1] * quarter_wave[:1]
    low, high = grad_block[:, :freqs], grad_block[:, pixels - freqs :]

    packed = jnp.zeros((depth, freqs), jnp.float32)
    for index, peer in enumerate([src] + near_first):
        tall = depth if index > 1 else depth + 8
        for core in range(2):
            slot = peer * 2 + core
            to(
                hsend.at[0, :tall],
                hrecv.at[slot, :tall],
                halo_ss.at[0],
                halo_rs.at[slot],
                src_at=peer,
                tile_at=other_tile,
                row_at=core,
            ).wait_recv()
            packed = packed + hrecv[slot, :depth]
    strip = jnp.concatenate(
        [packed]
        + [pltpu.roll(packed, freqs - one * OV, axis=1) for one in range(1, fold)],
        axis=0,
    )
    from_below = jnp.where((lanes < OV) & (tile == 1), strip, 0.0)
    from_above = jnp.where(
        (lanes >= freqs - OV) & (tile == 0), pltpu.roll(strip, freqs - OV, axis=1), 0.0
    )
    out_ref[0, :, :freqs] = low + from_below
    out_ref[0, :, pixels - freqs :] = high + from_above
    terms = own_terms + grecv[pool_src, local_x:]
    for slot in (src * 2, src * 2 + 1, pool_src * 2, pool_src * 2 + 1):
        terms = terms + hrecv[slot, depth:]
    terms = terms / (sources * pixels * tile_count)
    terms_ref[...] = terms
    for copy in copies:
        copy.wait_send()


def finish_kernel(grads_ref, terms_ref, out_ref, sums_ref, held_ref, sems):
    copy = pltpu.make_async_copy(grads_ref, out_ref, sems.at[0])
    copy.start()
    for one in range(held_ref.shape[0]):
        held_ref[one] = jnp.sum(terms_ref[one + 1 : one + 2, :])
    other = pltpu.make_async_copy(held_ref, sums_ref, sems.at[1])
    other.start()
    copy.wait()
    other.wait()


def finish(grads, terms, shape):
    in_vmem = pl.BlockSpec(memory_space=pltpu.VMEM)
    in_hbm = pl.BlockSpec(memory_space=pltpu.HBM)
    return pl.pallas_call(
        finish_kernel,
        out_shape=(
            jax.ShapeDtypeStruct(grads.shape, grads.dtype),
            jax.ShapeDtypeStruct(shape, terms.dtype),
        ),
        in_specs=[in_vmem, in_vmem],
        out_specs=(in_hbm, in_hbm),
        scratch_shapes=[pltpu.SMEM(shape, terms.dtype), pltpu.SemaphoreType.DMA((2,))],
    )(*(pltpu.with_memory_space_constraint(one, pltpu.VMEM) for one in (grads, terms)))


def shards(mask_windows, target_windows, pupil_bands, pupil_phase, source_weight):
    src_count = lax.axis_size("src")
    tile_count = lax.axis_size("tile")
    row_count = lax.axis_size("row")
    local_x, pixels = mask_windows.shape[1:]
    per_device, freqs = pupil_phase.shape[:2]
    blocks = src_count * row_count
    fits = row_count == 2 and tile_count == 2 and src_count == 4 and 2 * per_device <= 8
    fits = fits and freqs == 128 and pixels == 2 * freqs and local_x == OV
    if not fits or local_x * blocks != pixels or OV * 4 != freqs:
        return shards_plain(
            mask_windows, target_windows, pupil_bands, pupil_phase, source_weight
        )
    half, fold = freqs // 2, freqs // OV
    tables = wave_constants(pixels, freqs, blocks, src_count, local_x, fold)
    bands = jnp.transpose(pupil_bands, (0, 2, 1))
    phases = pupil_phase.reshape(per_device, 2, half, freqs)
    in_vmem = pl.BlockSpec(memory_space=pltpu.VMEM)
    in_smem = pl.BlockSpec(memory_space=pltpu.SMEM)
    f32 = jnp.float32
    block = (local_x, pixels)
    dma = pltpu.SemaphoreType.DMA
    like = [pltpu.VMEM(one.shape, one.dtype) for one in tables]
    like[4] = pltpu.VMEM(tables[4].shape[1:], tables[4].dtype)
    like[5] = pltpu.VMEM(tables[5].shape[1:], tables[5].dtype)
    four = dma((src_count,))
    grads, terms = pl.pallas_call(
        functools.partial(kernel, src_count, tile_count),
        out_shape=(
            pltpu.VMEM(mask_windows.shape, f32),
            pltpu.VMEM((8, freqs), f32),
        ),
        in_specs=[pl.BlockSpec(memory_space=pltpu.HBM)] * 12,
        out_specs=(in_vmem, in_vmem),
        scratch_shapes=like
        + [
            pltpu.VMEM(mask_windows.shape, f32),
            pltpu.VMEM(target_windows.shape, f32),
            pltpu.VMEM(bands.shape, bands.dtype),
            pltpu.VMEM((2,) + phases.shape, f32),
            pltpu.SMEM(source_weight.shape, f32),
            dma((12,)),
            pltpu.VMEM((blocks, local_x + 8, freqs), f32),
            pltpu.VMEM((2, 2 * per_device, freqs, freqs), f32),
            pltpu.VMEM((2, 2, per_device * local_x, 2 * pixels), f32),
            pltpu.VMEM((4, local_x, 2 * per_device * freqs), f32),
            pltpu.VMEM((2, 16, freqs), f32),
            pltpu.VMEM(block, f32),
            pltpu.VMEM((2,) + block, f32),
            pltpu.VMEM((2,) + block, f32),
            pltpu.VMEM((2, 8, freqs), f32),
            pltpu.VMEM((2, 8, freqs), f32),
            pltpu.VMEM((src_count,) + block, f32),
            pltpu.VMEM((src_count,) + block, f32),
            pltpu.VMEM((src_count, local_x + 8, freqs), f32),
            pltpu.VMEM((src_count, local_x + 8, freqs), f32),
            pltpu.VMEM((blocks, 16, freqs), f32),
            pltpu.VMEM((blocks, 16, freqs), f32),
        ]
        + [four] * 4
        + [dma(())] * 2
        + [dma((per_device,))] * 4
        + [dma(())] * 2
        + [dma((2,))] * 2
        + [dma((src_count + 1,))] * 2
        + [four] * 2
        + [dma((blocks,))] * 2,
        compiler_params=pltpu.CompilerParams(
            collective_id=0, has_side_effects=True, vmem_limit_bytes=63 * 1024 * 1024
        ),
    )(*tables, mask_windows, target_windows, bands, phases, source_weight)
    return finish(grads, terms, source_weight.shape)


def solution(mesh):
    return jax.shard_map(
        shards,
        mesh=mesh,
        in_specs=(
            P(("parts", "tile"), ("src", "row"), None),
            P(("parts", "tile"), ("src", "row"), None),
            P(("parts", "src"), None, None),
            P(("parts", "src"), None, None),
            P(("parts", "src")),
        ),
        out_specs=(P(("parts", "tile"), ("src", "row"), None), P(("parts", "src"))),
        check_vma=False,
    )
```

```python
import functools
import math

import jax
import jax.numpy as jnp
import numpy as np
from jax import lax
from jax.experimental import pallas as pl
from jax.experimental.pallas import tpu as pltpu
from jax.sharding import PartitionSpec as P

M = 256
K = 128
OV = 32


STEEPNESS = 20.0
THRESHOLD = 0.15
LOSS_SCALE = 32.0


def with_halo(block, sides, width):
    for axis, dim in sides:
        count = lax.axis_size(axis)
        forward = [(i, i + 1) for i in range(count - 1)]
        backward = [(target, source) for source, target in forward]
        low = lax.ppermute(
            lax.slice_in_dim(block, block.shape[dim] - width, None, axis=dim), axis, forward
        )
        high = lax.ppermute(lax.slice_in_dim(block, 0, width, axis=dim), axis, backward)
        block = jnp.concatenate([low, block, high], axis=dim)
    return block


def matmul(left_op, right_op):
    return lax.dot_general(
        left_op,
        right_op,
        (((1,), (0,)), ((), ())),
        precision=lax.Precision.HIGHEST,
        preferred_element_type=jnp.float32,
    )


def matmul_tn(left_op, right_op):
    return lax.dot_general(
        left_op,
        right_op,
        (((0,), (0,)), ((), ())),
        precision=lax.Precision.HIGHEST,
        preferred_element_type=jnp.float32,
    )


def matmul_nt(left_op, right_op):
    return lax.dot_general(
        left_op,
        right_op,
        (((1,), (1,)), ((), ())),
        precision=lax.Precision.HIGHEST,
        preferred_element_type=jnp.float32,
    )


def wave_tables(positions):
    freq_index = jnp.arange(K, dtype=jnp.int32) - K // 2
    phase_index = freq_index[:, None] * positions[None, :] % M
    angles = 2.0 * math.pi / M * phase_index.astype(jnp.float32)
    return (jnp.cos(angles), jnp.sin(angles))


def shards_plain(mask_windows, target_windows, pupil_bands, pupil_phase, source_weight):
    src_count = lax.axis_size("src")
    tile_count = lax.axis_size("tile")
    row_count = lax.axis_size("row")
    local_x = mask_windows.shape[1]
    per_device = pupil_phase.shape[0]
    sources = per_device * src_count
    field_scale = 1.0 / (M * K)
    src_id = lax.axis_index("src")
    row_id = lax.axis_index("row")
    x_start = (src_id * row_count + row_id) * local_x
    block_starts = (jnp.arange(src_count, dtype=jnp.int32) * row_count + row_id) * local_x
    row_set = (block_starts[:, None] + jnp.arange(local_x, dtype=jnp.int32)[None, :]).reshape(
        src_count * local_x
    )
    cos_all, sin_all = wave_tables(jnp.arange(M, dtype=jnp.int32))
    cos_set, sin_set = wave_tables(row_set)
    cos_own, sin_own = wave_tables(x_start + jnp.arange(local_x, dtype=jnp.int32))
    window = mask_windows[0]
    goal_block = target_windows[0]
    zero_spec = jnp.zeros((K, K), jnp.float32)
    shard_rows = lax.all_gather(window, ("src", "row"), axis=0, tiled=True)
    part_real = matmul_nt(shard_rows, cos_all)
    part_imag = -matmul_nt(shard_rows, sin_all)
    spec_real = matmul(cos_all, part_real) + matmul(sin_all, part_imag)
    spec_imag = matmul(cos_all, part_imag) - matmul(sin_all, part_real)
    freq_cols = jnp.arange(K, dtype=jnp.int32)
    inside = (freq_cols[None, None, :] >= pupil_bands[:, :, 0:1]) & (
        freq_cols[None, None, :] < pupil_bands[:, :, 1:2]
    )
    passing = inside.astype(jnp.float32)
    pupil_real = passing * jnp.cos(pupil_phase)
    pupil_imag = passing * jnp.sin(pupil_phase)
    amp_real = (pupil_real * spec_real - pupil_imag * spec_imag).reshape(per_device * K, K)
    amp_imag = (pupil_imag * spec_real + pupil_real * spec_imag).reshape(per_device * K, K)
    half_real = (matmul(amp_real, cos_all) - matmul(amp_imag, sin_all)).reshape(per_device, K, M)
    half_imag = (matmul(amp_real, sin_all) + matmul(amp_imag, cos_all)).reshape(per_device, K, M)
    weights = source_weight / sources

    def fields(pair_in):
        one_real, one_imag = pair_in
        field_real = field_scale * (matmul_tn(cos_set, one_real) - matmul_tn(sin_set, one_imag))
        field_imag = field_scale * (matmul_tn(cos_set, one_imag) + matmul_tn(sin_set, one_real))
        return (field_real, field_imag)

    stack_real, stack_imag = lax.map(fields, (half_real, half_imag))
    part_real = stack_real
    part_imag = stack_imag
    intensity = lax.psum_scatter(
        jnp.sum(weights[:, None, None] * (part_real * part_real + part_imag * part_imag), axis=0),
        "src",
        scatter_dimension=0,
        tiled=True,
    )
    resist = jax.nn.sigmoid(STEEPNESS * (intensity - THRESHOLD))
    cotangent = LOSS_SCALE * (resist - goal_block) * STEEPNESS * resist * (1.0 - resist)
    cotangent_all = lax.all_gather(cotangent, "src", axis=0, tiled=True)
    source_ids = jnp.arange(per_device, dtype=jnp.int32)

    def add_back(source_id, totals):
        grad_real, grad_imag, source_terms = totals
        field_real = stack_real[source_id]
        field_imag = stack_imag[source_id]
        back_scale = 2.0 * weights[source_id] * cotangent_all
        back_real = back_scale * field_real
        back_imag = back_scale * field_imag
        adj_real = matmul(cos_set, back_real) + matmul(sin_set, back_imag)
        adj_imag = matmul(cos_set, back_imag) - matmul(sin_set, back_real)
        amp_grad_real = field_scale * (matmul_nt(adj_real, cos_all) + matmul_nt(adj_imag, sin_all))
        amp_grad_imag = field_scale * (matmul_nt(adj_imag, cos_all) - matmul_nt(adj_real, sin_all))
        pass_real = pupil_real[source_id]
        pass_imag = pupil_imag[source_id]
        grad_real = grad_real + pass_real * amp_grad_real + pass_imag * amp_grad_imag
        grad_imag = grad_imag + pass_real * amp_grad_imag - pass_imag * amp_grad_real
        term_value = jnp.sum(cotangent_all * (field_real * field_real + field_imag * field_imag))
        source_terms = source_terms + jnp.where(source_ids == source_id, term_value, 0.0)
        return (grad_real, grad_imag, source_terms)

    grad_real, grad_imag, source_terms = lax.fori_loop(
        0, per_device, add_back, (zero_spec, zero_spec, jnp.zeros((per_device,), jnp.float32))
    )
    grad_real, grad_imag = lax.psum((grad_real, grad_imag), ("src", "row"))
    source_sum = lax.psum(source_terms, ("tile", "row"))
    source_grad = source_sum / (sources * M * tile_count)
    q_one = matmul(grad_real, cos_all) - matmul(grad_imag, sin_all)
    q_two = matmul(grad_real, sin_all) + matmul(grad_imag, cos_all)
    grad_block = matmul_tn(cos_own, q_one) - matmul_tn(sin_own, q_two)
    padded = with_halo(grad_block, (("tile", 1),), OV)
    from_below = padded[:, :OV]
    from_above = padded[:, M + OV :]
    middle = jnp.zeros((local_x, M - 2 * OV), jnp.float32)
    grad_block = grad_block + jnp.concatenate([from_below, middle, from_above], axis=1)
    return (grad_block[None], source_grad)


MESH = pl.DeviceIdType.MESH


def pair(values):
    high = values.astype(jnp.bfloat16)
    return high, (values - high.astype(jnp.float32)).astype(jnp.bfloat16)


def dot_pair(left_op, right_op, contract_right=0):
    dims = (((1,), (contract_right,)), ((), ()))

    def one(a, b):
        return lax.dot_general(a, b, dims, preferred_element_type=jnp.float32)

    (left_high, left_low), (right_high, right_low) = left_op, right_op
    return one(left_high, right_high) + (
        one(left_high, right_low) + one(left_low, right_high)
    )


def frequency_order(freqs):
    half = freqs // 2
    return np.concatenate([np.arange(half), [-half], -np.arange(1, half)])


def wave_constants(pixels, freqs, blocks, src_count, local_x, fold):
    half = freqs // 2
    spots = np.arange(pixels)

    def waves(index):
        angles = 2.0 * np.pi / pixels * (np.outer(index, spots) % pixels)
        return np.cos(angles), np.sin(angles)

    cos_x, sin_x = waves(np.arange(freqs) - half)
    order = frequency_order(freqs)
    cos_y, sin_y = waves(order)
    spectrum = np.concatenate([cos_x, -sin_x], axis=0)
    wave_y = np.block([[cos_y, sin_y], [-sin_y, cos_y]])
    real_rows = np.concatenate([cos_x.T, -sin_x.T], axis=1)
    imag_rows = np.concatenate([sin_x.T, cos_x.T], axis=1)
    wave_rows = np.stack(
        [one.reshape(blocks, local_x, 2 * freqs) for one in (real_rows, imag_rows)], axis=1
    )
    sets = []
    for own in range(blocks):
        src, row = own // 2, own % 2
        mate = (src + src_count // 2) % src_count * 2 + 1 - row
        rows = np.concatenate([np.arange(local_x) + one * local_x for one in (own, mate)])
        c, s = cos_x[:, rows], sin_x[:, rows]
        sets.append(np.block([[c, s], [-s, c]]))
    packed = np.concatenate([cos_y[:half], -sin_y[half:]], axis=0).T
    edges = []
    for start in (pixels - OV, 0):
        table = np.zeros((fold, 2 * freqs, fold, OV))
        for group in range(fold):
            table[group, :freqs, group] = packed[start : start + OV].T
            table[group, freqs + half, group] = cos_y[half, start : start + OV]
        edges.append(table.reshape(fold * 2 * freqs, freqs))
    move = np.zeros((freqs, freqs))
    move[order + half, np.arange(freqs)] = 1.0
    return (
        split_constant(packed),
        split_constant(spectrum),
        split_constant(wave_y),
        split_constant(wave_rows),
        split_constant(np.stack(sets), 1),
        split_constant(np.stack(edges), 1),
        move.astype(jnp.bfloat16),
    )


def split_constant(values, axis=0):
    values = values.astype(np.float32)
    high = values.astype(jnp.bfloat16)
    low = (values - high.astype(np.float32)).astype(jnp.bfloat16)
    return np.stack([high, low], axis=axis)


def sine_cosine(phase):
    quarter = 0.25 * phase
    square = quarter * quarter
    sine = 1.0 / 362880.0
    for term in (-1.0 / 5040.0, 1.0 / 120.0, -1.0 / 6.0, 1.0):
        sine = sine * square + term
    sine = sine * quarter
    fall = -1.0 / 40320.0
    for term in (1.0 / 720.0, -1.0 / 24.0, 0.5):
        fall = fall * square + term
    cosine = 1.0 - fall * square
    twice = 2.0 * sine
    sine, cosine = twice * cosine, 1.0 - twice * sine
    twice = 2.0 * sine
    return twice * cosine, 1.0 - twice * sine


def dot_exact(left_op, right_op, dims=(((1,), (0,)), ((), ()))):
    high, low = pair(left_op)

    def one(a):
        return lax.dot_general(a, right_op, dims, preferred_element_type=jnp.float32)

    return one(high) + one(low)


def kernel(
    src_count,
    tile_count,
    wm_hbm,
    wf_hbm,
    wy_hbm,
    wb_hbm,
    wx_hbm,
    we_hbm,
    move_hbm,
    mask_hbm,
    goal_hbm,
    band_hbm,
    phase_hbm,
    weight_hbm,
    out_ref,
    terms_ref,
    wm_ref,
    wf_ref,
    wy_ref,
    wb_ref,
    wx_ref,
    we_ref,
    move_ref,
    mask_ref,
    goal_ref,
    band_ref,
    phase_ref,
    weight_ref,
    load_sems,
    mbuf,
    pupil_ref,
    fbuf,
    ubuf,
    meta_ref,
    goals_ref,
    part_send,
    part_recv,
    tsend,
    trecv,
    csend,
    crecv,
    gsend,
    grecv,
    hsend,
    hrecv,
    mask_ss,
    mask_rs,
    fwd_ss,
    fwd_rs,
    meta_ss,
    meta_rs,
    phase_ss,
    phase_rs,
    pfwd_ss,
    pfwd_rs,
    goal_ss,
    goal_rs,
    part_ss,
    part_rs,
    core_ss,
    core_rs,
    grad_ss,
    grad_rs,
    halo_ss,
    halo_rs,
    ready_sem,
    token_sem,
):
    part = lax.axis_index("parts")
    src = lax.axis_index("src")
    tile = lax.axis_index("tile")
    row = lax.axis_index("row")
    local_x, pixels = mask_ref.shape[1:]
    per_device, half, freqs = phase_ref.shape[1], phase_ref.shape[3], phase_ref.shape[4]
    sources = per_device * src_count
    field_scale = 1.0 / (pixels * freqs)
    fold = freqs // OV
    depth = local_x // fold
    other_row = 1 - row
    other_tile = 1 - tile
    last = src_count - 1
    own_slot = src * 2 + row
    mate_src = lax.rem(src + src_count // 2, src_count)
    mate_slot = mate_src * 2 + other_row
    pool_src = src + 1 - 2 * lax.rem(src, 2)

    side = lax.div(src, 2)
    far_first = [last * (1 - side), 2 - side, pool_src]
    near_first = far_first[::-1]

    def to(src_ref, dst_ref, ss, rs, src_at=src, tile_at=tile, row_at=other_row):
        return pltpu.make_async_remote_copy(
            src_ref=src_ref,
            dst_ref=dst_ref,
            send_sem=ss,
            recv_sem=rs,
            device_id=(part, src_at, tile_at, row_at),
            device_id_type=MESH,
        )

    def tell(semaphore, src_at, row_at, tile_at=tile):
        pl.semaphore_signal(
            semaphore, inc=1, device_id=(part, src_at, tile_at, row_at), device_id_type=MESH
        )

    barrier = pltpu.get_barrier_semaphore()

    @pl.when(side == 0)
    def _():
        for peer in (last, last - 1):
            for core in (other_row, row):
                tell(barrier, peer, core)
        tell(barrier, pool_src, other_row)
        tell(barrier, src, other_row, other_tile)
        tell(barrier, src, other_row)

    @pl.when(src == last - 1)
    def _():
        for core in (other_row, row):
            tell(barrier, last, core)

    loads = {}
    for index, (name, source, target) in enumerate(
        [
            ("mask", mask_hbm, mask_ref),
            ("wm", wm_hbm, wm_ref),
            ("weight", weight_hbm, weight_ref),
            ("band", band_hbm, band_ref),
            ("phase", phase_hbm, phase_ref.at[0]),
            ("goal", goal_hbm, goal_ref),
            ("move", move_hbm, move_ref),
            ("wf", wf_hbm, wf_ref),
            ("wb", wb_hbm, wb_ref),
            ("wy", wy_hbm, wy_ref),
            ("wx", wx_hbm.at[own_slot], wx_ref),
            ("we", we_hbm.at[tile], we_ref),
        ]
    ):
        loads[name] = pltpu.make_async_copy(source, target, load_sems.at[index])
        loads[name].start()

    pl.semaphore_wait(barrier, 3 * (1 - side) + 2 * side * src)

    @pl.when(side == 1)
    def _():
        for peer in (0, 1):
            tell(ready_sem, peer, other_row)

    @pl.when(src == last)
    def _():
        for core in (other_row, row):
            tell(ready_sem, last - 1, core)

    lanes = lax.broadcasted_iota(jnp.int32, (local_x, freqs), 1)
    spots = lax.broadcasted_iota(jnp.int32, (8, pixels), 1)
    turn = spots - 4 * lax.div(spots, 4)
    quarter_wave = jnp.where(turn == 0, 1.0, jnp.where(turn == 2, -1.0, 0.0))
    first_row = lax.broadcasted_iota(jnp.int32, (8, pixels), 0) == 0

    loads["mask"].wait()
    loads["wm"].wait()
    wm = (wm_ref[0], wm_ref[1])
    mask = mask_ref[0]
    mbuf[own_slot, :local_x] = dot_pair(pair(mask), wm)
    quarter_row = jnp.where(first_row, quarter_wave, 0.0).astype(jnp.bfloat16)
    padded = jnp.concatenate([mask, jnp.zeros((freqs - local_x, pixels), jnp.float32)], axis=0)
    high, low = pair(padded)
    nt = (((1,), (1,)), ((), ()))
    mbuf[own_slot, local_x:] = lax.dot_general(
        quarter_row, high, nt, preferred_element_type=jnp.float32
    ) + lax.dot_general(quarter_row, low, nt, preferred_element_type=jnp.float32)
    loads["weight"].wait()
    loads["band"].wait()
    for one in range(per_device):
        meta_ref[0, one : one + 1, :] = jnp.full((1, freqs), weight_ref[one] / sources)
    meta_ref[0, 8:, :] = jnp.concatenate(
        [band_ref[one] for one in range(per_device)]
        + [jnp.zeros((8 - 2 * per_device, freqs), jnp.int32)],
        axis=0,
    ).astype(jnp.float32)
    loads["phase"].wait()
    loads["goal"].wait()
    copies = []

    def send(*args, **keys):
        copy = to(*args, **keys)
        copy.start()
        copies.append(copy)
        return copy

    own_block = mbuf.at[own_slot]
    far_copies = [
        to(own_block, own_block, mask_ss.at[peer], mask_rs.at[src], src_at=peer)
        for peer in far_first[:-1]
    ]
    pool_copies = [
        to(own_block, own_block, mask_ss.at[pool_src], mask_rs.at[src], src_at=pool_src),
        to(meta_ref.at[0], meta_ref.at[1], meta_ss, meta_rs, src_at=pool_src),
    ]
    for one in range(per_device):
        pool_copies.append(
            to(
                phase_ref.at[0, one, row],
                phase_ref.at[1, one, row],
                phase_ss.at[one],
                phase_rs.at[one],
                src_at=pool_src,
            )
        )
    copies += far_copies + pool_copies

    def start(group):
        for copy in group:
            copy.start()

    @pl.when(side == 1)
    def _():
        start(far_copies)

    @pl.when(src != last - 1)
    def _():
        start(pool_copies)

    loads["move"].wait()
    move = move_ref[...]
    columns = lax.broadcasted_iota(jnp.int32, (freqs, freqs), 1).astype(jnp.float32)

    def make_pupil(group, one):
        bands = meta_ref[group, 8:, :].T
        lower, upper = bands[:, 2 * one : 2 * one + 1], bands[:, 2 * one + 1 : 2 * one + 2]
        passing = (columns >= lower) & (columns < upper)
        sine, cosine = sine_cosine(phase_ref[group, one].reshape(freqs, freqs))
        moved = dot_exact(
            jnp.concatenate(
                [jnp.where(passing, cosine, 0.0), jnp.where(passing, sine, 0.0)], axis=0
            ),
            move,
        )
        pupil_ref[group, 2 * one] = moved[:freqs]
        pupil_ref[group, 2 * one + 1] = moved[freqs:]

    for one in range(per_device):
        make_pupil(0, one)

    @pl.when(src != last)
    def _():
        pl.semaphore_wait(ready_sem, 2)

    @pl.when(side == 0)
    def _():
        start(far_copies)

    @pl.when(src == last - 1)
    def _():
        start(pool_copies)

    for name in ("wf", "wb", "wy", "wx", "we"):
        loads[name].wait()

    for index, peer in enumerate(near_first):
        block = mbuf.at[peer * 2 + other_row]
        to(block, block, mask_ss.at[peer], mask_rs.at[peer], src_at=peer).wait_recv()
        send(block, block, fwd_ss.at[peer], fwd_rs.at[peer])
        if index == 0:
            send(own_block, own_block, fwd_ss.at[src], fwd_rs.at[src])
        if index == last - 1:
            send(goal_ref.at[0], goals_ref, goal_ss, goal_rs, src_at=mate_src)
    for one in range(per_device):
        half_block = phase_ref.at[1, one, other_row]
        to(
            half_block, half_block, phase_ss.at[one], phase_rs.at[one], src_at=pool_src
        ).wait_recv()
        send(half_block, half_block, pfwd_ss.at[one], pfwd_rs.at[one])
    for peer in near_first:
        block = mbuf.at[peer * 2 + row]
        to(block, block, fwd_ss.at[peer], fwd_rs.at[peer]).wait_recv()
    block = mbuf.at[src * 2 + other_row]
    to(block, block, fwd_ss.at[src], fwd_rs.at[src]).wait_recv()

    @pl.when(side == 0)
    def _():
        tell(token_sem, src, other_row, other_tile)

    blocks = pixels // local_x
    extra = jnp.concatenate([mbuf[one, local_x : local_x + 1] for one in range(blocks)], axis=0).T
    rows = []
    for one in range(blocks):
        straight = mbuf[one, :local_x]
        turned = pltpu.roll(straight, half, axis=1)
        real = jnp.where(lanes < half, straight, turned)
        real = jnp.where(lanes == half, extra[:local_x, one : one + 1], real)
        imag = jnp.where(lanes < half, -turned, straight)
        imag = jnp.where(lanes == 0, 0.0, imag)
        rows.append(jnp.concatenate([real, imag], axis=1))
    spectrum = dot_pair((wf_ref[0], wf_ref[1]), pair(jnp.concatenate(rows, axis=0)))
    spec_real = spectrum[:freqs, :freqs] - spectrum[freqs:, freqs:]
    spec_imag = spectrum[:freqs, freqs:] + spectrum[freqs:, :freqs]

    wxt = tuple(
        jnp.concatenate(
            [wb_ref[index, slot, side] for side in range(2) for slot in (own_slot, mate_slot)],
            axis=0,
        )
        for index in range(2)
    )
    wy = (wy_ref[0], wy_ref[1])

    def swept_rows(group):
        reals, imags = [], []
        for one in range(per_device):
            pr, pi = pupil_ref[group, 2 * one], pupil_ref[group, 2 * one + 1]
            reals.append(pr * spec_real - pi * spec_imag)
            imags.append(pi * spec_real + pr * spec_imag)
        amps = jnp.concatenate(
            [jnp.concatenate(reals, axis=1), jnp.concatenate(imags, axis=1)], axis=0
        )
        return dot_pair(wxt, pair(amps)) * field_scale

    to(meta_ref.at[0], meta_ref.at[1], meta_ss, meta_rs, src_at=pool_src).wait_recv()
    weights = [
        jnp.concatenate([meta_ref[group, one : one + 1, :]] * 2, axis=1)
        for group in range(2)
        for one in range(per_device)
    ]

    def light_of(group, swept, block):
        tops = swept[block * local_x : (block + 1) * local_x]
        ends = swept[(2 + block) * local_x : (3 + block) * local_x]
        rows = jnp.concatenate(
            [
                jnp.concatenate(
                    [
                        tops[:, one * freqs : (one + 1) * freqs],
                        ends[:, one * freqs : (one + 1) * freqs],
                    ],
                    axis=1,
                )
                for one in range(per_device)
            ],
            axis=0,
        )
        field = dot_pair(pair(rows), wy)
        fbuf[group, block] = field
        squares = field[:, :pixels] * field[:, :pixels] + field[:, pixels:] * field[:, pixels:]
        total = weights[group * per_device] * squares[:local_x]
        for one in range(1, per_device):
            total = total + (
                weights[group * per_device + one]
                * squares[one * local_x : (one + 1) * local_x]
            )
        return total

    swept = swept_rows(0)
    lights = [light_of(0, swept, block) for block in range(2)]
    for one in range(per_device):
        half_block = phase_ref.at[1, one, row]
        to(half_block, half_block, pfwd_ss.at[one], pfwd_rs.at[one]).wait_recv()
        make_pupil(1, one)
    swept = swept_rows(1)

    @pl.when(side == 0)
    def _():
        pl.semaphore_wait(token_sem, 1)

    for block in (1, 0):
        lights[block] = lights[block] + light_of(1, swept, block)
        part_send[block] = lights[block]
        send(
            part_send.at[block],
            part_recv.at[1 - block],
            part_ss.at[block],
            part_rs.at[1 - block],
            src_at=mate_src,
        )
    to(goal_ref.at[0], goals_ref, goal_ss, goal_rs, src_at=mate_src).wait_recv()

    terms = [jnp.zeros((1, pixels), jnp.float32)] * (2 * per_device)
    for block in (0, 1):
        to(
            part_send.at[1 - block],
            part_recv.at[block],
            part_ss.at[1 - block],
            part_rs.at[block],
            src_at=mate_src,
        ).wait_recv()
        intensity = lights[block] + part_recv[block]
        goal = goal_ref[0] if block == 0 else goals_ref[...]
        resist = 1.0 / (1.0 + jnp.exp(-STEEPNESS * (intensity - THRESHOLD)))
        cotangent = LOSS_SCALE * (resist - goal) * STEEPNESS * resist * (1.0 - resist)
        for group in range(2):
            backs = []
            for one in range(per_device):
                at = group * per_device + one
                field = fbuf[group, block, one * local_x : (one + 1) * local_x]
                real, imag = field[:, :pixels], field[:, pixels:]
                lit_real, lit_imag = cotangent * real, cotangent * imag
                scale = 2.0 * weights[at]
                backs.append(jnp.concatenate([scale * lit_real, scale * lit_imag], axis=1))
                terms[at] = terms[at] + jnp.sum(
                    lit_real * real + lit_imag * imag, axis=0, keepdims=True
                )
            adjoint = dot_pair(pair(jnp.concatenate(backs, axis=0)), wy, 1)
            for one in range(per_device):
                rows = slice(one * local_x, (one + 1) * local_x)
                at = group * per_device + one
                cols = slice(at * freqs, (at + 1) * freqs)
                ubuf[block, :, cols] = adjoint[rows, :freqs]
                ubuf[2 + block, :, cols] = adjoint[rows, freqs:]

    blank = jnp.zeros((1, freqs), jnp.float32)
    for group in range(2):
        tsend[group] = jnp.concatenate(
            [blank]
            + [
                terms[group * per_device + one][:, :freqs]
                + terms[group * per_device + one][:, freqs:]
                for one in range(per_device)
            ]
            + [blank] * (7 - per_device),
            axis=0,
        )
    term_copy = send(tsend, trecv, core_ss.at[src_count], core_rs.at[src_count])

    wx = (wx_ref[0], wx_ref[1])
    swept = ubuf[...].reshape(4 * local_x, 2 * per_device * freqs)
    swept = dot_pair(wx, pair(swept)) * field_scale
    grad_real = jnp.zeros((freqs, freqs), jnp.float32)
    grad_imag = grad_real
    for at in range(2 * per_device):
        group, one = at // per_device, at % per_device
        pr, pi = pupil_ref[group, 2 * one], pupil_ref[group, 2 * one + 1]
        cols = slice(at * freqs, (at + 1) * freqs)
        real, imag = swept[:freqs, cols], swept[freqs:, cols]
        grad_real = grad_real + pr * real + pi * imag
        grad_imag = grad_imag + pr * imag - pi * real

    lane = lax.broadcasted_iota(jnp.int32, (freqs, freqs), 1)
    turn_real = pltpu.roll(grad_real, half, axis=1)
    turn_imag = pltpu.roll(grad_imag, half, axis=1)
    sum_real = grad_real + jnp.where(lane == 0, 0.0, turn_real)
    sum_imag = grad_imag + jnp.where(lane == 0, 0.0, turn_imag)
    gap_real = jnp.where(lane == half, 0.0, turn_real) - grad_real
    gap_imag = jnp.where(lane == half, 0.0, turn_imag) - grad_imag
    upper = jnp.where(lane < half, sum_real, -gap_imag)
    lower = jnp.where(lane < half, sum_imag, gap_real)
    grads = pair(
        jnp.concatenate(
            [
                jnp.concatenate([upper, grad_real], axis=1),
                jnp.concatenate([lower, grad_imag], axis=1),
            ],
            axis=0,
        )
    )

    def rows_of(far_row, own_row):
        slots = [peer * 2 + far_row for peer in far_first] + [src * 2 + own_row]
        waves = tuple(
            jnp.concatenate([wb_ref[index, slot, 0] for slot in slots], axis=0)
            for index in range(2)
        )
        return dot_pair(waves, grads)

    theirs = rows_of(row, other_row)
    for index in range(src_count):
        csend[index] = theirs[index * local_x : (index + 1) * local_x]
        send(csend.at[index], crecv.at[index], core_ss.at[index], core_rs.at[index])
    mine = rows_of(other_row, row)
    strips = jnp.concatenate(
        [
            jnp.concatenate(
                [
                    blocks_of[
                        index * local_x + one * depth : index * local_x + (one + 1) * depth
                    ]
                    for one in range(fold)
                ],
                axis=1,
            )
            for blocks_of in (theirs, mine)
            for index in range(src_count)
        ],
        axis=0,
    )
    strips = dot_pair(pair(strips), (we_ref[0], we_ref[1]))
    for side, near_row, far_row in ((0, other_row, row), (1, row, other_row)):
        for index, peer in enumerate(far_first + [src]):
            at = side * src_count + index
            hsend[at, :depth] = strips[at * depth : (at + 1) * depth]
            tall = depth if index < last - 1 else depth + 8
            if index >= last - 1:
                hsend[at, depth:] = tsend[last - index]
            send(
                hsend.at[at, :tall],
                hrecv.at[own_slot, :tall],
                halo_ss.at[at],
                halo_rs.at[own_slot],
                src_at=peer,
                tile_at=other_tile,
                row_at=far_row if index < last else near_row,
            )
    term_copy.wait_recv()
    own_terms = tsend[0] + trecv[0]
    pool_terms = tsend[1] + trecv[1]
    for index in range(src_count):
        gsend[index, local_x:] = pool_terms if index < last else own_terms
    for index, peer in enumerate(far_first + [src]):
        to(csend.at[index], crecv.at[index], core_ss.at[index], core_rs.at[index]).wait_recv()
        both = mine[index * local_x : (index + 1) * local_x] + crecv[index]
        gsend[index, :local_x] = both[:, :freqs]
        gsend[index, local_x : local_x + 1, :local_x] = both[:, freqs:].T[half : half + 1]
        if index < last:
            send(
                gsend.at[index], grecv.at[src], grad_ss.at[index], grad_rs.at[src], src_at=peer
            )

    total = gsend[last]
    for peer in near_first:
        to(
            gsend.at[0], grecv.at[peer], grad_ss.at[0], grad_rs.at[peer], src_at=peer
        ).wait_recv()
        total = total + grecv[peer]
    grad_block = dot_pair(pair(total[:local_x]), wm, 1)
    grad_block = grad_block + total[local_x:].T[:local_x, :1] * quarter_wave[:1]
    low, high = grad_block[:, :freqs], grad_block[:, pixels - freqs :]

    packed = jnp.zeros((depth, freqs), jnp.float32)
    for index, peer in enumerate([src] + near_first):
        tall = depth if index > 1 else depth + 8
        for core in range(2):
            slot = peer * 2 + core
            to(
                hsend.at[0, :tall],
                hrecv.at[slot, :tall],
                halo_ss.at[0],
                halo_rs.at[slot],
                src_at=peer,
                tile_at=other_tile,
                row_at=core,
            ).wait_recv()
            packed = packed + hrecv[slot, :depth]
    strip = jnp.concatenate(
        [packed]
        + [pltpu.roll(packed, freqs - one * OV, axis=1) for one in range(1, fold)],
        axis=0,
    )
    from_below = jnp.where((lanes < OV) & (tile == 1), strip, 0.0)
    from_above = jnp.where(
        (lanes >= freqs - OV) & (tile == 0), pltpu.roll(strip, freqs - OV, axis=1), 0.0
    )
    out_ref[0, :, :freqs] = low + from_below
    out_ref[0, :, pixels - freqs :] = high + from_above
    terms = own_terms + grecv[pool_src, local_x:]
    for slot in (src * 2, src * 2 + 1, pool_src * 2, pool_src * 2 + 1):
        terms = terms + hrecv[slot, depth:]
    terms = terms / (sources * pixels * tile_count)
    terms_ref[...] = terms
    for copy in copies:
        copy.wait_send()


def finish_kernel(grads_ref, terms_ref, out_ref, sums_ref, held_ref, sems):
    copy = pltpu.make_async_copy(grads_ref, out_ref, sems.at[0])
    copy.start()
    for one in range(held_ref.shape[0]):
        held_ref[one] = jnp.sum(terms_ref[one + 1 : one + 2, :])
    other = pltpu.make_async_copy(held_ref, sums_ref, sems.at[1])
    other.start()
    copy.wait()
    other.wait()


def finish(grads, terms, shape):
    in_vmem = pl.BlockSpec(memory_space=pltpu.VMEM)
    in_hbm = pl.BlockSpec(memory_space=pltpu.HBM)
    return pl.pallas_call(
        finish_kernel,
        out_shape=(
            jax.ShapeDtypeStruct(grads.shape, grads.dtype),
            jax.ShapeDtypeStruct(shape, terms.dtype),
        ),
        in_specs=[in_vmem, in_vmem],
        out_specs=(in_hbm, in_hbm),
        scratch_shapes=[pltpu.SMEM(shape, terms.dtype), pltpu.SemaphoreType.DMA((2,))],
    )(*(pltpu.with_memory_space_constraint(one, pltpu.VMEM) for one in (grads, terms)))


def shards(mask_windows, target_windows, pupil_bands, pupil_phase, source_weight):
    src_count = lax.axis_size("src")
    tile_count = lax.axis_size("tile")
    row_count = lax.axis_size("row")
    local_x, pixels = mask_windows.shape[1:]
    per_device, freqs = pupil_phase.shape[:2]
    blocks = src_count * row_count
    fits = row_count == 2 and tile_count == 2 and src_count == 4 and 2 * per_device <= 8
    fits = fits and freqs == 128 and pixels == 2 * freqs and local_x == OV
    if not fits or local_x * blocks != pixels or OV * 4 != freqs:
        return shards_plain(
            mask_windows, target_windows, pupil_bands, pupil_phase, source_weight
        )
    half, fold = freqs // 2, freqs // OV
    tables = wave_constants(pixels, freqs, blocks, src_count, local_x, fold)
    bands = jnp.transpose(pupil_bands, (0, 2, 1))
    phases = pupil_phase.reshape(per_device, 2, half, freqs)
    in_vmem = pl.BlockSpec(memory_space=pltpu.VMEM)
    in_smem = pl.BlockSpec(memory_space=pltpu.SMEM)
    f32 = jnp.float32
    block = (local_x, pixels)
    dma = pltpu.SemaphoreType.DMA
    like = [pltpu.VMEM(one.shape, one.dtype) for one in tables]
    like[4] = pltpu.VMEM(tables[4].shape[1:], tables[4].dtype)
    like[5] = pltpu.VMEM(tables[5].shape[1:], tables[5].dtype)
    four = dma((src_count,))
    grads, terms = pl.pallas_call(
        functools.partial(kernel, src_count, tile_count),
        out_shape=(
            pltpu.VMEM(mask_windows.shape, f32),
            pltpu.VMEM((8, freqs), f32),
        ),
        in_specs=[pl.BlockSpec(memory_space=pltpu.HBM)] * 12,
        out_specs=(in_vmem, in_vmem),
        scratch_shapes=like
        + [
            pltpu.VMEM(mask_windows.shape, f32),
            pltpu.VMEM(target_windows.shape, f32),
            pltpu.VMEM(bands.shape, bands.dtype),
            pltpu.VMEM((2,) + phases.shape, f32),
            pltpu.SMEM(source_weight.shape, f32),
            dma((12,)),
            pltpu.VMEM((blocks, local_x + 8, freqs), f32),
            pltpu.VMEM((2, 2 * per_device, freqs, freqs), f32),
            pltpu.VMEM((2, 2, per_device * local_x, 2 * pixels), f32),
            pltpu.VMEM((4, local_x, 2 * per_device * freqs), f32),
            pltpu.VMEM((2, 16, freqs), f32),
            pltpu.VMEM(block, f32),
            pltpu.VMEM((2,) + block, f32),
            pltpu.VMEM((2,) + block, f32),
            pltpu.VMEM((2, 8, freqs), f32),
            pltpu.VMEM((2, 8, freqs), f32),
            pltpu.VMEM((src_count,) + block, f32),
            pltpu.VMEM((src_count,) + block, f32),
            pltpu.VMEM((src_count, local_x + 8, freqs), f32),
            pltpu.VMEM((src_count, local_x + 8, freqs), f32),
            pltpu.VMEM((blocks, 16, freqs), f32),
            pltpu.VMEM((blocks, 16, freqs), f32),
        ]
        + [four] * 4
        + [dma(())] * 2
        + [dma((per_device,))] * 4
        + [dma(())] * 2
        + [dma((2,))] * 2
        + [dma((src_count + 1,))] * 2
        + [four] * 2
        + [dma((blocks,))] * 2
        + [pltpu.SemaphoreType.REGULAR] * 2,
        compiler_params=pltpu.CompilerParams(
            collective_id=0, has_side_effects=True, vmem_limit_bytes=63 * 1024 * 1024
        ),
    )(*tables, mask_windows, target_windows, bands, phases, source_weight)
    return finish(grads, terms, source_weight.shape)


def solution(mesh):
    return jax.shard_map(
        shards,
        mesh=mesh,
        in_specs=(
            P(("parts", "tile"), ("src", "row"), None),
            P(("parts", "tile"), ("src", "row"), None),
            P(("parts", "src"), None, None),
            P(("parts", "src"), None, None),
            P(("parts", "src")),
        ),
        out_specs=(P(("parts", "tile"), ("src", "row"), None), P(("parts", "src"))),
        check_vma=False,
    )
```

```python
import functools
import math

import jax
import jax.numpy as jnp
import numpy as np
from jax import lax
from jax.experimental import pallas as pl
from jax.experimental.pallas import tpu as pltpu
from jax.sharding import PartitionSpec as P

M = 256
K = 128
OV = 32


STEEPNESS = 20.0
THRESHOLD = 0.15
LOSS_SCALE = 32.0


def with_halo(block, sides, width):
    for axis, dim in sides:
        count = lax.axis_size(axis)
        forward = [(i, i + 1) for i in range(count - 1)]
        backward = [(target, source) for source, target in forward]
        low = lax.ppermute(
            lax.slice_in_dim(block, block.shape[dim] - width, None, axis=dim), axis, forward
        )
        high = lax.ppermute(lax.slice_in_dim(block, 0, width, axis=dim), axis, backward)
        block = jnp.concatenate([low, block, high], axis=dim)
    return block


def matmul(left_op, right_op):
    return lax.dot_general(
        left_op,
        right_op,
        (((1,), (0,)), ((), ())),
        precision=lax.Precision.HIGHEST,
        preferred_element_type=jnp.float32,
    )


def matmul_tn(left_op, right_op):
    return lax.dot_general(
        left_op,
        right_op,
        (((0,), (0,)), ((), ())),
        precision=lax.Precision.HIGHEST,
        preferred_element_type=jnp.float32,
    )


def matmul_nt(left_op, right_op):
    return lax.dot_general(
        left_op,
        right_op,
        (((1,), (1,)), ((), ())),
        precision=lax.Precision.HIGHEST,
        preferred_element_type=jnp.float32,
    )


def wave_tables(positions):
    freq_index = jnp.arange(K, dtype=jnp.int32) - K // 2
    phase_index = freq_index[:, None] * positions[None, :] % M
    angles = 2.0 * math.pi / M * phase_index.astype(jnp.float32)
    return (jnp.cos(angles), jnp.sin(angles))


def shards_plain(mask_windows, target_windows, pupil_bands, pupil_phase, source_weight):
    src_count = lax.axis_size("src")
    tile_count = lax.axis_size("tile")
    row_count = lax.axis_size("row")
    local_x = mask_windows.shape[1]
    per_device = pupil_phase.shape[0]
    sources = per_device * src_count
    field_scale = 1.0 / (M * K)
    src_id = lax.axis_index("src")
    row_id = lax.axis_index("row")
    x_start = (src_id * row_count + row_id) * local_x
    block_starts = (jnp.arange(src_count, dtype=jnp.int32) * row_count + row_id) * local_x
    row_set = (block_starts[:, None] + jnp.arange(local_x, dtype=jnp.int32)[None, :]).reshape(
        src_count * local_x
    )
    cos_all, sin_all = wave_tables(jnp.arange(M, dtype=jnp.int32))
    cos_set, sin_set = wave_tables(row_set)
    cos_own, sin_own = wave_tables(x_start + jnp.arange(local_x, dtype=jnp.int32))
    window = mask_windows[0]
    goal_block = target_windows[0]
    zero_spec = jnp.zeros((K, K), jnp.float32)
    shard_rows = lax.all_gather(window, ("src", "row"), axis=0, tiled=True)
    part_real = matmul_nt(shard_rows, cos_all)
    part_imag = -matmul_nt(shard_rows, sin_all)
    spec_real = matmul(cos_all, part_real) + matmul(sin_all, part_imag)
    spec_imag = matmul(cos_all, part_imag) - matmul(sin_all, part_real)
    freq_cols = jnp.arange(K, dtype=jnp.int32)
    inside = (freq_cols[None, None, :] >= pupil_bands[:, :, 0:1]) & (
        freq_cols[None, None, :] < pupil_bands[:, :, 1:2]
    )
    passing = inside.astype(jnp.float32)
    pupil_real = passing * jnp.cos(pupil_phase)
    pupil_imag = passing * jnp.sin(pupil_phase)
    amp_real = (pupil_real * spec_real - pupil_imag * spec_imag).reshape(per_device * K, K)
    amp_imag = (pupil_imag * spec_real + pupil_real * spec_imag).reshape(per_device * K, K)
    half_real = (matmul(amp_real, cos_all) - matmul(amp_imag, sin_all)).reshape(per_device, K, M)
    half_imag = (matmul(amp_real, sin_all) + matmul(amp_imag, cos_all)).reshape(per_device, K, M)
    weights = source_weight / sources

    def fields(pair_in):
        one_real, one_imag = pair_in
        field_real = field_scale * (matmul_tn(cos_set, one_real) - matmul_tn(sin_set, one_imag))
        field_imag = field_scale * (matmul_tn(cos_set, one_imag) + matmul_tn(sin_set, one_real))
        return (field_real, field_imag)

    stack_real, stack_imag = lax.map(fields, (half_real, half_imag))
    part_real = stack_real
    part_imag = stack_imag
    intensity = lax.psum_scatter(
        jnp.sum(weights[:, None, None] * (part_real * part_real + part_imag * part_imag), axis=0),
        "src",
        scatter_dimension=0,
        tiled=True,
    )
    resist = jax.nn.sigmoid(STEEPNESS * (intensity - THRESHOLD))
    cotangent = LOSS_SCALE * (resist - goal_block) * STEEPNESS * resist * (1.0 - resist)
    cotangent_all = lax.all_gather(cotangent, "src", axis=0, tiled=True)
    source_ids = jnp.arange(per_device, dtype=jnp.int32)

    def add_back(source_id, totals):
        grad_real, grad_imag, source_terms = totals
        field_real = stack_real[source_id]
        field_imag = stack_imag[source_id]
        back_scale = 2.0 * weights[source_id] * cotangent_all
        back_real = back_scale * field_real
        back_imag = back_scale * field_imag
        adj_real = matmul(cos_set, back_real) + matmul(sin_set, back_imag)
        adj_imag = matmul(cos_set, back_imag) - matmul(sin_set, back_real)
        amp_grad_real = field_scale * (matmul_nt(adj_real, cos_all) + matmul_nt(adj_imag, sin_all))
        amp_grad_imag = field_scale * (matmul_nt(adj_imag, cos_all) - matmul_nt(adj_real, sin_all))
        pass_real = pupil_real[source_id]
        pass_imag = pupil_imag[source_id]
        grad_real = grad_real + pass_real * amp_grad_real + pass_imag * amp_grad_imag
        grad_imag = grad_imag + pass_real * amp_grad_imag - pass_imag * amp_grad_real
        term_value = jnp.sum(cotangent_all * (field_real * field_real + field_imag * field_imag))
        source_terms = source_terms + jnp.where(source_ids == source_id, term_value, 0.0)
        return (grad_real, grad_imag, source_terms)

    grad_real, grad_imag, source_terms = lax.fori_loop(
        0, per_device, add_back, (zero_spec, zero_spec, jnp.zeros((per_device,), jnp.float32))
    )
    grad_real, grad_imag = lax.psum((grad_real, grad_imag), ("src", "row"))
    source_sum = lax.psum(source_terms, ("tile", "row"))
    source_grad = source_sum / (sources * M * tile_count)
    q_one = matmul(grad_real, cos_all) - matmul(grad_imag, sin_all)
    q_two = matmul(grad_real, sin_all) + matmul(grad_imag, cos_all)
    grad_block = matmul_tn(cos_own, q_one) - matmul_tn(sin_own, q_two)
    padded = with_halo(grad_block, (("tile", 1),), OV)
    from_below = padded[:, :OV]
    from_above = padded[:, M + OV :]
    middle = jnp.zeros((local_x, M - 2 * OV), jnp.float32)
    grad_block = grad_block + jnp.concatenate([from_below, middle, from_above], axis=1)
    return (grad_block[None], source_grad)


MESH = pl.DeviceIdType.MESH


def pair(values):
    high = values.astype(jnp.bfloat16)
    return high, (values - high.astype(jnp.float32)).astype(jnp.bfloat16)


def dot_pair(left_op, right_op, contract_right=0):
    dims = (((1,), (contract_right,)), ((), ()))

    def one(a, b):
        return lax.dot_general(a, b, dims, preferred_element_type=jnp.float32)

    (left_high, left_low), (right_high, right_low) = left_op, right_op
    return one(left_high, right_high) + (
        one(left_high, right_low) + one(left_low, right_high)
    )


def frequency_order(freqs):
    half = freqs // 2
    return np.concatenate([np.arange(half), [-half], -np.arange(1, half)])


def wave_constants(pixels, freqs, blocks, src_count, local_x, fold):
    half = freqs // 2
    spots = np.arange(pixels)

    def waves(index):
        angles = 2.0 * np.pi / pixels * (np.outer(index, spots) % pixels)
        return np.cos(angles), np.sin(angles)

    cos_x, sin_x = waves(np.arange(freqs) - half)
    order = frequency_order(freqs)
    cos_y, sin_y = waves(order)
    spectrum = np.concatenate([cos_x, -sin_x], axis=0)
    wave_y = np.block([[cos_y, sin_y], [-sin_y, cos_y]])
    real_rows = np.concatenate([cos_x.T, -sin_x.T], axis=1)
    imag_rows = np.concatenate([sin_x.T, cos_x.T], axis=1)
    wave_rows = np.stack(
        [one.reshape(blocks, local_x, 2 * freqs) for one in (real_rows, imag_rows)], axis=1
    )
    sets = []
    for own in range(blocks):
        src, row = own // 2, own % 2
        mate = (src + src_count // 2) % src_count * 2 + 1 - row
        rows = np.concatenate([np.arange(local_x) + one * local_x for one in (own, mate)])
        c, s = cos_x[:, rows], sin_x[:, rows]
        sets.append(np.block([[c, s], [-s, c]]))
    packed = np.concatenate([cos_y[:half], -sin_y[half:]], axis=0).T
    edges = []
    for start in (pixels - OV, 0):
        table = np.zeros((fold, 2 * freqs, fold, OV))
        for group in range(fold):
            table[group, :freqs, group] = packed[start : start + OV].T
            table[group, freqs + half, group] = cos_y[half, start : start + OV]
        edges.append(table.reshape(fold * 2 * freqs, freqs))
    move = np.zeros((freqs, freqs))
    move[order + half, np.arange(freqs)] = 1.0
    return (
        split_constant(packed),
        split_constant(spectrum),
        split_constant(wave_y),
        split_constant(wave_rows),
        split_constant(np.stack(sets), 1),
        split_constant(np.stack(edges), 1),
        move.astype(jnp.bfloat16),
    )


def split_constant(values, axis=0):
    values = values.astype(np.float32)
    high = values.astype(jnp.bfloat16)
    low = (values - high.astype(np.float32)).astype(jnp.bfloat16)
    return np.stack([high, low], axis=axis)


def sine_cosine(phase):
    quarter = 0.25 * phase
    square = quarter * quarter
    sine = 1.0 / 362880.0
    for term in (-1.0 / 5040.0, 1.0 / 120.0, -1.0 / 6.0, 1.0):
        sine = sine * square + term
    sine = sine * quarter
    fall = -1.0 / 40320.0
    for term in (1.0 / 720.0, -1.0 / 24.0, 0.5):
        fall = fall * square + term
    cosine = 1.0 - fall * square
    twice = 2.0 * sine
    sine, cosine = twice * cosine, 1.0 - twice * sine
    twice = 2.0 * sine
    return twice * cosine, 1.0 - twice * sine


def dot_exact(left_op, right_op, dims=(((1,), (0,)), ((), ()))):
    high, low = pair(left_op)

    def one(a):
        return lax.dot_general(a, right_op, dims, preferred_element_type=jnp.float32)

    return one(high) + one(low)


def kernel(
    src_count,
    tile_count,
    wm_hbm,
    wf_hbm,
    wy_hbm,
    wb_hbm,
    wx_hbm,
    we_hbm,
    move_hbm,
    mask_hbm,
    goal_hbm,
    band_hbm,
    phase_hbm,
    weight_hbm,
    out_ref,
    terms_ref,
    wm_ref,
    wf_ref,
    wy_ref,
    wb_ref,
    wx_ref,
    we_ref,
    move_ref,
    mask_ref,
    goal_ref,
    band_ref,
    phase_ref,
    weight_ref,
    load_sems,
    mbuf,
    pupil_ref,
    fbuf,
    ubuf,
    meta_ref,
    goals_ref,
    part_send,
    part_recv,
    tsend,
    trecv,
    csend,
    crecv,
    gsend,
    grecv,
    hsend,
    hrecv,
    mask_ss,
    mask_rs,
    fwd_ss,
    fwd_rs,
    meta_ss,
    meta_rs,
    phase_ss,
    phase_rs,
    pfwd_ss,
    pfwd_rs,
    goal_ss,
    goal_rs,
    part_ss,
    part_rs,
    core_ss,
    core_rs,
    grad_ss,
    grad_rs,
    halo_ss,
    halo_rs,
    ready_sem,
    token_sem,
    band_rows,
):
    part = lax.axis_index("parts")
    src = lax.axis_index("src")
    tile = lax.axis_index("tile")
    row = lax.axis_index("row")
    local_x, pixels = mask_ref.shape[1:]
    per_device, half, freqs = phase_ref.shape[1], phase_ref.shape[3], phase_ref.shape[4]
    sources = per_device * src_count
    field_scale = 1.0 / (pixels * freqs)
    fold = freqs // OV
    depth = local_x // fold
    other_row = 1 - row
    other_tile = 1 - tile
    last = src_count - 1
    own_slot = src * 2 + row
    mate_src = lax.rem(src + src_count // 2, src_count)
    mate_slot = mate_src * 2 + other_row
    pool_src = src + 1 - 2 * lax.rem(src, 2)

    side = lax.div(src, 2)
    far_first = [last * (1 - side), 2 - side, pool_src]
    near_first = far_first[::-1]

    def to(src_ref, dst_ref, ss, rs, src_at=src, tile_at=tile, row_at=other_row):
        return pltpu.make_async_remote_copy(
            src_ref=src_ref,
            dst_ref=dst_ref,
            send_sem=ss,
            recv_sem=rs,
            device_id=(part, src_at, tile_at, row_at),
            device_id_type=MESH,
        )

    def tell(semaphore, src_at, row_at, tile_at=tile):
        pl.semaphore_signal(
            semaphore, inc=1, device_id=(part, src_at, tile_at, row_at), device_id_type=MESH
        )

    barrier = pltpu.get_barrier_semaphore()

    @pl.when(side == 0)
    def _():
        for peer in (last, last - 1):
            for core in (other_row, row):
                tell(barrier, peer, core)
        tell(barrier, pool_src, other_row)
        tell(barrier, src, other_row, other_tile)
        tell(barrier, src, other_row)

    @pl.when(src == last - 1)
    def _():
        for core in (other_row, row):
            tell(barrier, last, core)

    loads = {}
    for index, (name, source, target) in enumerate(
        [
            ("mask", mask_hbm, mask_ref),
            ("wm", wm_hbm, wm_ref),
            ("weight", weight_hbm, weight_ref),
            ("band", band_hbm, band_ref),
            ("phase", phase_hbm, phase_ref.at[0]),
            ("goal", goal_hbm, goal_ref),
            ("move", move_hbm, move_ref),
            ("wf", wf_hbm, wf_ref),
            ("wb", wb_hbm, wb_ref),
            ("wy", wy_hbm, wy_ref),
            ("wx", wx_hbm.at[own_slot], wx_ref),
            ("we", we_hbm.at[tile], we_ref),
        ]
    ):
        loads[name] = pltpu.make_async_copy(source, target, load_sems.at[index])
        loads[name].start()

    pl.semaphore_wait(barrier, 3 * (1 - side) + 2 * side * src)

    @pl.when(side == 1)
    def _():
        for peer in (0, 1):
            tell(ready_sem, peer, other_row)

    @pl.when(src == last)
    def _():
        for core in (other_row, row):
            tell(ready_sem, last - 1, core)

    lanes = lax.broadcasted_iota(jnp.int32, (local_x, freqs), 1)
    spots = lax.broadcasted_iota(jnp.int32, (8, pixels), 1)
    turn = spots - 4 * lax.div(spots, 4)
    quarter_wave = jnp.where(turn == 0, 1.0, jnp.where(turn == 2, -1.0, 0.0))
    first_row = lax.broadcasted_iota(jnp.int32, (8, pixels), 0) == 0

    loads["mask"].wait()
    loads["wm"].wait()
    wm = (wm_ref[0], wm_ref[1])
    mask = mask_ref[0]
    mbuf[own_slot, :local_x] = dot_pair(pair(mask), wm)
    quarter_row = jnp.where(first_row, quarter_wave, 0.0).astype(jnp.bfloat16)
    padded = jnp.concatenate([mask, jnp.zeros((freqs - local_x, pixels), jnp.float32)], axis=0)
    high, low = pair(padded)
    nt = (((1,), (1,)), ((), ()))
    mbuf[own_slot, local_x:] = lax.dot_general(
        quarter_row, high, nt, preferred_element_type=jnp.float32
    ) + lax.dot_general(quarter_row, low, nt, preferred_element_type=jnp.float32)
    loads["weight"].wait()
    loads["band"].wait()
    for one in range(per_device):
        meta_ref[0, one : one + 1, :] = jnp.full((1, freqs), weight_ref[one] / sources)
    meta_ref[0, 8:, :] = jnp.concatenate(
        [band_ref[one] for one in range(per_device)]
        + [jnp.zeros((8 - 2 * per_device, freqs), jnp.int32)],
        axis=0,
    ).astype(jnp.float32)
    loads["phase"].wait()
    loads["goal"].wait()
    copies = []

    def send(*args, **keys):
        copy = to(*args, **keys)
        copy.start()
        copies.append(copy)
        return copy

    own_block = mbuf.at[own_slot]
    far_copies = [
        to(own_block, own_block, mask_ss.at[peer], mask_rs.at[src], src_at=peer)
        for peer in far_first[:-1]
    ]
    pool_copies = [
        to(own_block, own_block, mask_ss.at[pool_src], mask_rs.at[src], src_at=pool_src),
        to(meta_ref.at[0], meta_ref.at[1], meta_ss, meta_rs, src_at=pool_src),
    ]
    for one in range(per_device):
        pool_copies.append(
            to(
                phase_ref.at[0, one, row],
                phase_ref.at[1, one, row],
                phase_ss.at[one],
                phase_rs.at[one],
                src_at=pool_src,
            )
        )
    copies += far_copies + pool_copies

    def start(group):
        for copy in group:
            copy.start()

    @pl.when(side == 1)
    def _():
        start(far_copies)

    @pl.when(src != last - 1)
    def _():
        start(pool_copies)

    loads["move"].wait()
    move = move_ref[...]
    columns = lax.broadcasted_iota(jnp.int32, (half, freqs), 1).astype(jnp.float32)

    def read_bands(group):
        band_rows[...] = meta_ref[group, 8:, :].T

    def make_pupil(group, one, part_of):
        rows = pl.ds(pl.multiple_of(part_of * half, half), half)
        lower = band_rows[rows, 2 * one : 2 * one + 1]
        upper = band_rows[rows, 2 * one + 1 : 2 * one + 2]
        passing = (columns >= lower) & (columns < upper)
        sine, cosine = sine_cosine(phase_ref[group, one, part_of])
        moved = dot_exact(
            jnp.concatenate(
                [jnp.where(passing, cosine, 0.0), jnp.where(passing, sine, 0.0)], axis=0
            ),
            move,
        )
        pupil_ref[group, 2 * one, rows] = moved[:half]
        pupil_ref[group, 2 * one + 1, rows] = moved[half:]

    read_bands(0)
    for one in range(per_device):
        for part_of in range(2):
            make_pupil(0, one, part_of)

    @pl.when(src != last)
    def _():
        pl.semaphore_wait(ready_sem, 2)

    @pl.when(side == 0)
    def _():
        start(far_copies)

    @pl.when(src == last - 1)
    def _():
        start(pool_copies)

    for name in ("wf", "wb", "wy", "wx", "we"):
        loads[name].wait()

    for index, peer in enumerate(near_first):
        block = mbuf.at[peer * 2 + other_row]
        to(block, block, mask_ss.at[peer], mask_rs.at[peer], src_at=peer).wait_recv()
        send(block, block, fwd_ss.at[peer], fwd_rs.at[peer])
        if index == 0:
            send(own_block, own_block, fwd_ss.at[src], fwd_rs.at[src])
        if index == last - 1:
            send(goal_ref.at[0], goals_ref, goal_ss, goal_rs, src_at=mate_src)
    for one in range(per_device):
        half_block = phase_ref.at[1, one, other_row]
        to(
            half_block, half_block, phase_ss.at[one], phase_rs.at[one], src_at=pool_src
        ).wait_recv()
        send(half_block, half_block, pfwd_ss.at[one], pfwd_rs.at[one])
    to(meta_ref.at[0], meta_ref.at[1], meta_ss, meta_rs, src_at=pool_src).wait_recv()
    read_bands(1)
    for one in range(per_device):
        make_pupil(1, one, other_row)
    for peer in near_first:
        block = mbuf.at[peer * 2 + row]
        to(block, block, fwd_ss.at[peer], fwd_rs.at[peer]).wait_recv()
    block = mbuf.at[src * 2 + other_row]
    to(block, block, fwd_ss.at[src], fwd_rs.at[src]).wait_recv()

    @pl.when(side == 0)
    def _():
        tell(token_sem, src, other_row, other_tile)

    for one in range(per_device):
        half_block = phase_ref.at[1, one, row]
        to(half_block, half_block, pfwd_ss.at[one], pfwd_rs.at[one]).wait_recv()
        make_pupil(1, one, row)
    blocks = pixels // local_x
    extra = jnp.concatenate([mbuf[one, local_x : local_x + 1] for one in range(blocks)], axis=0).T
    rows = []
    for one in range(blocks):
        straight = mbuf[one, :local_x]
        turned = pltpu.roll(straight, half, axis=1)
        real = jnp.where(lanes < half, straight, turned)
        real = jnp.where(lanes == half, extra[:local_x, one : one + 1], real)
        imag = jnp.where(lanes < half, -turned, straight)
        imag = jnp.where(lanes == 0, 0.0, imag)
        rows.append(jnp.concatenate([real, imag], axis=1))
    spectrum = dot_pair((wf_ref[0], wf_ref[1]), pair(jnp.concatenate(rows, axis=0)))
    spec_real = spectrum[:freqs, :freqs] - spectrum[freqs:, freqs:]
    spec_imag = spectrum[:freqs, freqs:] + spectrum[freqs:, :freqs]

    wxt = tuple(
        jnp.concatenate(
            [wb_ref[index, slot, side] for side in range(2) for slot in (own_slot, mate_slot)],
            axis=0,
        )
        for index in range(2)
    )
    wy = (wy_ref[0], wy_ref[1])

    def swept_rows(group):
        reals, imags = [], []
        for one in range(per_device):
            pr, pi = pupil_ref[group, 2 * one], pupil_ref[group, 2 * one + 1]
            reals.append(pr * spec_real - pi * spec_imag)
            imags.append(pi * spec_real + pr * spec_imag)
        amps = jnp.concatenate(
            [jnp.concatenate(reals, axis=1), jnp.concatenate(imags, axis=1)], axis=0
        )
        return dot_pair(wxt, pair(amps)) * field_scale

    weights = [
        jnp.concatenate([meta_ref[group, one : one + 1, :]] * 2, axis=1)
        for group in range(2)
        for one in range(per_device)
    ]

    def light_of(group, swept, block):
        tops = swept[block * local_x : (block + 1) * local_x]
        ends = swept[(2 + block) * local_x : (3 + block) * local_x]
        rows = jnp.concatenate(
            [
                jnp.concatenate(
                    [
                        tops[:, one * freqs : (one + 1) * freqs],
                        ends[:, one * freqs : (one + 1) * freqs],
                    ],
                    axis=1,
                )
                for one in range(per_device)
            ],
            axis=0,
        )
        field = dot_pair(pair(rows), wy)
        fbuf[group, block] = field
        squares = field[:, :pixels] * field[:, :pixels] + field[:, pixels:] * field[:, pixels:]
        total = weights[group * per_device] * squares[:local_x]
        for one in range(1, per_device):
            total = total + (
                weights[group * per_device + one]
                * squares[one * local_x : (one + 1) * local_x]
            )
        return total

    swept = [swept_rows(group) for group in range(2)]
    lights = [None, None]
    @pl.when(side == 0)
    def _():
        pl.semaphore_wait(token_sem, 1)

    for block in (1, 0):
        lights[block] = light_of(0, swept[0], block) + light_of(1, swept[1], block)
        part_send[block] = lights[block]
        send(
            part_send.at[block],
            part_recv.at[1 - block],
            part_ss.at[block],
            part_rs.at[1 - block],
            src_at=mate_src,
        )
    to(goal_ref.at[0], goals_ref, goal_ss, goal_rs, src_at=mate_src).wait_recv()

    terms = [jnp.zeros((1, pixels), jnp.float32)] * (2 * per_device)
    for block in (0, 1):
        to(
            part_send.at[1 - block],
            part_recv.at[block],
            part_ss.at[1 - block],
            part_rs.at[block],
            src_at=mate_src,
        ).wait_recv()
        intensity = lights[block] + part_recv[block]
        goal = goal_ref[0] if block == 0 else goals_ref[...]
        resist = 1.0 / (1.0 + jnp.exp(-STEEPNESS * (intensity - THRESHOLD)))
        cotangent = LOSS_SCALE * (resist - goal) * STEEPNESS * resist * (1.0 - resist)
        for group in range(2):
            backs = []
            for one in range(per_device):
                at = group * per_device + one
                field = fbuf[group, block, one * local_x : (one + 1) * local_x]
                real, imag = field[:, :pixels], field[:, pixels:]
                lit_real, lit_imag = cotangent * real, cotangent * imag
                scale = 2.0 * weights[at]
                backs.append(jnp.concatenate([scale * lit_real, scale * lit_imag], axis=1))
                terms[at] = terms[at] + jnp.sum(
                    lit_real * real + lit_imag * imag, axis=0, keepdims=True
                )
            adjoint = dot_pair(pair(jnp.concatenate(backs, axis=0)), wy, 1)
            for one in range(per_device):
                rows = slice(one * local_x, (one + 1) * local_x)
                at = group * per_device + one
                cols = slice(at * freqs, (at + 1) * freqs)
                ubuf[block, :, cols] = adjoint[rows, :freqs]
                ubuf[2 + block, :, cols] = adjoint[rows, freqs:]

    blank = jnp.zeros((1, freqs), jnp.float32)
    for group in range(2):
        tsend[group] = jnp.concatenate(
            [blank]
            + [
                terms[group * per_device + one][:, :freqs]
                + terms[group * per_device + one][:, freqs:]
                for one in range(per_device)
            ]
            + [blank] * (7 - per_device),
            axis=0,
        )
    term_copy = send(tsend, trecv, core_ss.at[src_count], core_rs.at[src_count])

    wx = (wx_ref[0], wx_ref[1])
    swept = ubuf[...].reshape(4 * local_x, 2 * per_device * freqs)
    swept = dot_pair(wx, pair(swept)) * field_scale
    grad_real = jnp.zeros((freqs, freqs), jnp.float32)
    grad_imag = grad_real
    for at in range(2 * per_device):
        group, one = at // per_device, at % per_device
        pr, pi = pupil_ref[group, 2 * one], pupil_ref[group, 2 * one + 1]
        cols = slice(at * freqs, (at + 1) * freqs)
        real, imag = swept[:freqs, cols], swept[freqs:, cols]
        grad_real = grad_real + pr * real + pi * imag
        grad_imag = grad_imag + pr * imag - pi * real

    lane = lax.broadcasted_iota(jnp.int32, (freqs, freqs), 1)
    turn_real = pltpu.roll(grad_real, half, axis=1)
    turn_imag = pltpu.roll(grad_imag, half, axis=1)
    sum_real = grad_real + jnp.where(lane == 0, 0.0, turn_real)
    sum_imag = grad_imag + jnp.where(lane == 0, 0.0, turn_imag)
    gap_real = jnp.where(lane == half, 0.0, turn_real) - grad_real
    gap_imag = jnp.where(lane == half, 0.0, turn_imag) - grad_imag
    upper = jnp.where(lane < half, sum_real, -gap_imag)
    lower = jnp.where(lane < half, sum_imag, gap_real)
    grads = pair(
        jnp.concatenate(
            [
                jnp.concatenate([upper, grad_real], axis=1),
                jnp.concatenate([lower, grad_imag], axis=1),
            ],
            axis=0,
        )
    )

    def rows_of(far_row, own_row):
        slots = [peer * 2 + far_row for peer in far_first] + [src * 2 + own_row]
        waves = tuple(
            jnp.concatenate([wb_ref[index, slot, 0] for slot in slots], axis=0)
            for index in range(2)
        )
        return dot_pair(waves, grads)

    theirs = rows_of(row, other_row)
    for index in range(src_count):
        csend[index] = theirs[index * local_x : (index + 1) * local_x]
        send(csend.at[index], crecv.at[index], core_ss.at[index], core_rs.at[index])
    mine = rows_of(other_row, row)
    strips = jnp.concatenate(
        [
            jnp.concatenate(
                [
                    blocks_of[
                        index * local_x + one * depth : index * local_x + (one + 1) * depth
                    ]
                    for one in range(fold)
                ],
                axis=1,
            )
            for blocks_of in (theirs, mine)
            for index in range(src_count)
        ],
        axis=0,
    )
    strips = dot_pair(pair(strips), (we_ref[0], we_ref[1]))
    for side, near_row, far_row in ((0, other_row, row), (1, row, other_row)):
        for index, peer in enumerate(far_first + [src]):
            at = side * src_count + index
            hsend[at, :depth] = strips[at * depth : (at + 1) * depth]
            tall = depth if index < last - 1 else depth + 8
            if index >= last - 1:
                hsend[at, depth:] = tsend[last - index]
            send(
                hsend.at[at, :tall],
                hrecv.at[own_slot, :tall],
                halo_ss.at[at],
                halo_rs.at[own_slot],
                src_at=peer,
                tile_at=other_tile,
                row_at=far_row if index < last else near_row,
            )
    term_copy.wait_recv()
    own_terms = tsend[0] + trecv[0]
    pool_terms = tsend[1] + trecv[1]
    for index in range(src_count):
        gsend[index, local_x:] = pool_terms if index < last else own_terms
    for index, peer in enumerate(far_first + [src]):
        to(csend.at[index], crecv.at[index], core_ss.at[index], core_rs.at[index]).wait_recv()
        both = mine[index * local_x : (index + 1) * local_x] + crecv[index]
        gsend[index, :local_x] = both[:, :freqs]
        gsend[index, local_x : local_x + 1, :local_x] = both[:, freqs:].T[half : half + 1]
        if index < last:
            send(
                gsend.at[index], grecv.at[src], grad_ss.at[index], grad_rs.at[src], src_at=peer
            )

    total = gsend[last]
    for peer in near_first:
        to(
            gsend.at[0], grecv.at[peer], grad_ss.at[0], grad_rs.at[peer], src_at=peer
        ).wait_recv()
        total = total + grecv[peer]
    grad_block = dot_pair(pair(total[:local_x]), wm, 1)
    grad_block = grad_block + total[local_x:].T[:local_x, :1] * quarter_wave[:1]
    low, high = grad_block[:, :freqs], grad_block[:, pixels - freqs :]

    packed = jnp.zeros((depth, freqs), jnp.float32)
    for index, peer in enumerate([src] + near_first):
        tall = depth if index > 1 else depth + 8
        for core in range(2):
            slot = peer * 2 + core
            to(
                hsend.at[0, :tall],
                hrecv.at[slot, :tall],
                halo_ss.at[0],
                halo_rs.at[slot],
                src_at=peer,
                tile_at=other_tile,
                row_at=core,
            ).wait_recv()
            packed = packed + hrecv[slot, :depth]
    strip = jnp.concatenate(
        [packed]
        + [pltpu.roll(packed, freqs - one * OV, axis=1) for one in range(1, fold)],
        axis=0,
    )
    from_below = jnp.where((lanes < OV) & (tile == 1), strip, 0.0)
    from_above = jnp.where(
        (lanes >= freqs - OV) & (tile == 0), pltpu.roll(strip, freqs - OV, axis=1), 0.0
    )
    out_ref[0, :, :freqs] = low + from_below
    out_ref[0, :, pixels - freqs :] = high + from_above
    terms = own_terms + grecv[pool_src, local_x:]
    for slot in (src * 2, src * 2 + 1, pool_src * 2, pool_src * 2 + 1):
        terms = terms + hrecv[slot, depth:]
    terms = terms / (sources * pixels * tile_count)
    terms_ref[...] = terms
    for copy in copies:
        copy.wait_send()


def finish_kernel(grads_ref, terms_ref, out_ref, sums_ref, held_ref, sems):
    copy = pltpu.make_async_copy(grads_ref, out_ref, sems.at[0])
    copy.start()
    for one in range(held_ref.shape[0]):
        held_ref[one] = jnp.sum(terms_ref[one + 1 : one + 2, :])
    other = pltpu.make_async_copy(held_ref, sums_ref, sems.at[1])
    other.start()
    copy.wait()
    other.wait()


def finish(grads, terms, shape):
    in_vmem = pl.BlockSpec(memory_space=pltpu.VMEM)
    in_hbm = pl.BlockSpec(memory_space=pltpu.HBM)
    return pl.pallas_call(
        finish_kernel,
        out_shape=(
            jax.ShapeDtypeStruct(grads.shape, grads.dtype),
            jax.ShapeDtypeStruct(shape, terms.dtype),
        ),
        in_specs=[in_vmem, in_vmem],
        out_specs=(in_hbm, in_hbm),
        scratch_shapes=[pltpu.SMEM(shape, terms.dtype), pltpu.SemaphoreType.DMA((2,))],
    )(*(pltpu.with_memory_space_constraint(one, pltpu.VMEM) for one in (grads, terms)))


def shards(mask_windows, target_windows, pupil_bands, pupil_phase, source_weight):
    src_count = lax.axis_size("src")
    tile_count = lax.axis_size("tile")
    row_count = lax.axis_size("row")
    local_x, pixels = mask_windows.shape[1:]
    per_device, freqs = pupil_phase.shape[:2]
    blocks = src_count * row_count
    fits = row_count == 2 and tile_count == 2 and src_count == 4 and 2 * per_device <= 8
    fits = fits and freqs == 128 and pixels == 2 * freqs and local_x == OV
    if not fits or local_x * blocks != pixels or OV * 4 != freqs:
        return shards_plain(
            mask_windows, target_windows, pupil_bands, pupil_phase, source_weight
        )
    half, fold = freqs // 2, freqs // OV
    tables = wave_constants(pixels, freqs, blocks, src_count, local_x, fold)
    bands = jnp.transpose(pupil_bands, (0, 2, 1))
    phases = pupil_phase.reshape(per_device, 2, half, freqs)
    in_vmem = pl.BlockSpec(memory_space=pltpu.VMEM)
    in_smem = pl.BlockSpec(memory_space=pltpu.SMEM)
    f32 = jnp.float32
    block = (local_x, pixels)
    dma = pltpu.SemaphoreType.DMA
    like = [pltpu.VMEM(one.shape, one.dtype) for one in tables]
    like[4] = pltpu.VMEM(tables[4].shape[1:], tables[4].dtype)
    like[5] = pltpu.VMEM(tables[5].shape[1:], tables[5].dtype)
    four = dma((src_count,))
    grads, terms = pl.pallas_call(
        functools.partial(kernel, src_count, tile_count),
        out_shape=(
            pltpu.VMEM(mask_windows.shape, f32),
            pltpu.VMEM((8, freqs), f32),
        ),
        in_specs=[pl.BlockSpec(memory_space=pltpu.HBM)] * 12,
        out_specs=(in_vmem, in_vmem),
        scratch_shapes=like
        + [
            pltpu.VMEM(mask_windows.shape, f32),
            pltpu.VMEM(target_windows.shape, f32),
            pltpu.VMEM(bands.shape, bands.dtype),
            pltpu.VMEM((2,) + phases.shape, f32),
            pltpu.SMEM(source_weight.shape, f32),
            dma((12,)),
            pltpu.VMEM((blocks, local_x + 8, freqs), f32),
            pltpu.VMEM((2, 2 * per_device, freqs, freqs), f32),
            pltpu.VMEM((2, 2, per_device * local_x, 2 * pixels), f32),
            pltpu.VMEM((4, local_x, 2 * per_device * freqs), f32),
            pltpu.VMEM((2, 16, freqs), f32),
            pltpu.VMEM(block, f32),
            pltpu.VMEM((2,) + block, f32),
            pltpu.VMEM((2,) + block, f32),
            pltpu.VMEM((2, 8, freqs), f32),
            pltpu.VMEM((2, 8, freqs), f32),
            pltpu.VMEM((src_count,) + block, f32),
            pltpu.VMEM((src_count,) + block, f32),
            pltpu.VMEM((src_count, local_x + 8, freqs), f32),
            pltpu.VMEM((src_count, local_x + 8, freqs), f32),
            pltpu.VMEM((blocks, 16, freqs), f32),
            pltpu.VMEM((blocks, 16, freqs), f32),
        ]
        + [four] * 4
        + [dma(())] * 2
        + [dma((per_device,))] * 4
        + [dma(())] * 2
        + [dma((2,))] * 2
        + [dma((src_count + 1,))] * 2
        + [four] * 2
        + [dma((blocks,))] * 2
        + [pltpu.SemaphoreType.REGULAR] * 2
        + [pltpu.VMEM((freqs, 8), f32)],
        compiler_params=pltpu.CompilerParams(
            collective_id=0, has_side_effects=True, vmem_limit_bytes=63 * 1024 * 1024
        ),
    )(*tables, mask_windows, target_windows, bands, phases, source_weight)
    return finish(grads, terms, source_weight.shape)


def solution(mesh):
    return jax.shard_map(
        shards,
        mesh=mesh,
        in_specs=(
            P(("parts", "tile"), ("src", "row"), None),
            P(("parts", "tile"), ("src", "row"), None),
            P(("parts", "src"), None, None),
            P(("parts", "src"), None, None),
            P(("parts", "src")),
        ),
        out_specs=(P(("parts", "tile"), ("src", "row"), None), P(("parts", "src"))),
        check_vma=False,
    )
```

```python
import functools
import math

import jax
import jax.numpy as jnp
import numpy as np
from jax import lax
from jax.experimental import pallas as pl
from jax.experimental.pallas import tpu as pltpu
from jax.sharding import PartitionSpec as P

M = 256
K = 128
OV = 32


STEEPNESS = 20.0
THRESHOLD = 0.15
LOSS_SCALE = 32.0


def with_halo(block, sides, width):
    for axis, dim in sides:
        count = lax.axis_size(axis)
        forward = [(i, i + 1) for i in range(count - 1)]
        backward = [(target, source) for source, target in forward]
        low = lax.ppermute(
            lax.slice_in_dim(block, block.shape[dim] - width, None, axis=dim), axis, forward
        )
        high = lax.ppermute(lax.slice_in_dim(block, 0, width, axis=dim), axis, backward)
        block = jnp.concatenate([low, block, high], axis=dim)
    return block


def matmul(left_op, right_op):
    return lax.dot_general(
        left_op,
        right_op,
        (((1,), (0,)), ((), ())),
        precision=lax.Precision.HIGHEST,
        preferred_element_type=jnp.float32,
    )


def matmul_tn(left_op, right_op):
    return lax.dot_general(
        left_op,
        right_op,
        (((0,), (0,)), ((), ())),
        precision=lax.Precision.HIGHEST,
        preferred_element_type=jnp.float32,
    )


def matmul_nt(left_op, right_op):
    return lax.dot_general(
        left_op,
        right_op,
        (((1,), (1,)), ((), ())),
        precision=lax.Precision.HIGHEST,
        preferred_element_type=jnp.float32,
    )


def wave_tables(positions):
    freq_index = jnp.arange(K, dtype=jnp.int32) - K // 2
    phase_index = freq_index[:, None] * positions[None, :] % M
    angles = 2.0 * math.pi / M * phase_index.astype(jnp.float32)
    return (jnp.cos(angles), jnp.sin(angles))


def shards_plain(mask_windows, target_windows, pupil_bands, pupil_phase, source_weight):
    src_count = lax.axis_size("src")
    tile_count = lax.axis_size("tile")
    row_count = lax.axis_size("row")
    local_x = mask_windows.shape[1]
    per_device = pupil_phase.shape[0]
    sources = per_device * src_count
    field_scale = 1.0 / (M * K)
    src_id = lax.axis_index("src")
    row_id = lax.axis_index("row")
    x_start = (src_id * row_count + row_id) * local_x
    block_starts = (jnp.arange(src_count, dtype=jnp.int32) * row_count + row_id) * local_x
    row_set = (block_starts[:, None] + jnp.arange(local_x, dtype=jnp.int32)[None, :]).reshape(
        src_count * local_x
    )
    cos_all, sin_all = wave_tables(jnp.arange(M, dtype=jnp.int32))
    cos_set, sin_set = wave_tables(row_set)
    cos_own, sin_own = wave_tables(x_start + jnp.arange(local_x, dtype=jnp.int32))
    window = mask_windows[0]
    goal_block = target_windows[0]
    zero_spec = jnp.zeros((K, K), jnp.float32)
    shard_rows = lax.all_gather(window, ("src", "row"), axis=0, tiled=True)
    part_real = matmul_nt(shard_rows, cos_all)
    part_imag = -matmul_nt(shard_rows, sin_all)
    spec_real = matmul(cos_all, part_real) + matmul(sin_all, part_imag)
    spec_imag = matmul(cos_all, part_imag) - matmul(sin_all, part_real)
    freq_cols = jnp.arange(K, dtype=jnp.int32)
    inside = (freq_cols[None, None, :] >= pupil_bands[:, :, 0:1]) & (
        freq_cols[None, None, :] < pupil_bands[:, :, 1:2]
    )
    passing = inside.astype(jnp.float32)
    pupil_real = passing * jnp.cos(pupil_phase)
    pupil_imag = passing * jnp.sin(pupil_phase)
    amp_real = (pupil_real * spec_real - pupil_imag * spec_imag).reshape(per_device * K, K)
    amp_imag = (pupil_imag * spec_real + pupil_real * spec_imag).reshape(per_device * K, K)
    half_real = (matmul(amp_real, cos_all) - matmul(amp_imag, sin_all)).reshape(per_device, K, M)
    half_imag = (matmul(amp_real, sin_all) + matmul(amp_imag, cos_all)).reshape(per_device, K, M)
    weights = source_weight / sources

    def fields(pair_in):
        one_real, one_imag = pair_in
        field_real = field_scale * (matmul_tn(cos_set, one_real) - matmul_tn(sin_set, one_imag))
        field_imag = field_scale * (matmul_tn(cos_set, one_imag) + matmul_tn(sin_set, one_real))
        return (field_real, field_imag)

    stack_real, stack_imag = lax.map(fields, (half_real, half_imag))
    part_real = stack_real
    part_imag = stack_imag
    intensity = lax.psum_scatter(
        jnp.sum(weights[:, None, None] * (part_real * part_real + part_imag * part_imag), axis=0),
        "src",
        scatter_dimension=0,
        tiled=True,
    )
    resist = jax.nn.sigmoid(STEEPNESS * (intensity - THRESHOLD))
    cotangent = LOSS_SCALE * (resist - goal_block) * STEEPNESS * resist * (1.0 - resist)
    cotangent_all = lax.all_gather(cotangent, "src", axis=0, tiled=True)
    source_ids = jnp.arange(per_device, dtype=jnp.int32)

    def add_back(source_id, totals):
        grad_real, grad_imag, source_terms = totals
        field_real = stack_real[source_id]
        field_imag = stack_imag[source_id]
        back_scale = 2.0 * weights[source_id] * cotangent_all
        back_real = back_scale * field_real
        back_imag = back_scale * field_imag
        adj_real = matmul(cos_set, back_real) + matmul(sin_set, back_imag)
        adj_imag = matmul(cos_set, back_imag) - matmul(sin_set, back_real)
        amp_grad_real = field_scale * (matmul_nt(adj_real, cos_all) + matmul_nt(adj_imag, sin_all))
        amp_grad_imag = field_scale * (matmul_nt(adj_imag, cos_all) - matmul_nt(adj_real, sin_all))
        pass_real = pupil_real[source_id]
        pass_imag = pupil_imag[source_id]
        grad_real = grad_real + pass_real * amp_grad_real + pass_imag * amp_grad_imag
        grad_imag = grad_imag + pass_real * amp_grad_imag - pass_imag * amp_grad_real
        term_value = jnp.sum(cotangent_all * (field_real * field_real + field_imag * field_imag))
        source_terms = source_terms + jnp.where(source_ids == source_id, term_value, 0.0)
        return (grad_real, grad_imag, source_terms)

    grad_real, grad_imag, source_terms = lax.fori_loop(
        0, per_device, add_back, (zero_spec, zero_spec, jnp.zeros((per_device,), jnp.float32))
    )
    grad_real, grad_imag = lax.psum((grad_real, grad_imag), ("src", "row"))
    source_sum = lax.psum(source_terms, ("tile", "row"))
    source_grad = source_sum / (sources * M * tile_count)
    q_one = matmul(grad_real, cos_all) - matmul(grad_imag, sin_all)
    q_two = matmul(grad_real, sin_all) + matmul(grad_imag, cos_all)
    grad_block = matmul_tn(cos_own, q_one) - matmul_tn(sin_own, q_two)
    padded = with_halo(grad_block, (("tile", 1),), OV)
    from_below = padded[:, :OV]
    from_above = padded[:, M + OV :]
    middle = jnp.zeros((local_x, M - 2 * OV), jnp.float32)
    grad_block = grad_block + jnp.concatenate([from_below, middle, from_above], axis=1)
    return (grad_block[None], source_grad)


MESH = pl.DeviceIdType.MESH


def pair(values):
    high = values.astype(jnp.bfloat16)
    return high, (values - high.astype(jnp.float32)).astype(jnp.bfloat16)


def dot_pair(left_op, right_op, contract_right=0):
    dims = (((1,), (contract_right,)), ((), ()))

    def one(a, b):
        return lax.dot_general(a, b, dims, preferred_element_type=jnp.float32)

    (left_high, left_low), (right_high, right_low) = left_op, right_op
    both = one(jnp.concatenate([left_high, left_low], axis=0), right_high)
    count = left_high.shape[0]
    return both[:count] + (both[count:] + one(left_high, right_low))


def frequency_order(freqs):
    half = freqs // 2
    return np.concatenate([np.arange(half), [-half], -np.arange(1, half)])


def wave_constants(pixels, freqs, blocks, src_count, local_x, fold):
    half = freqs // 2
    spots = np.arange(pixels)

    def waves(index):
        angles = 2.0 * np.pi / pixels * (np.outer(index, spots) % pixels)
        return np.cos(angles), np.sin(angles)

    cos_x, sin_x = waves(np.arange(freqs) - half)
    order = frequency_order(freqs)
    cos_y, sin_y = waves(order)
    spectrum = np.concatenate([cos_x, -sin_x], axis=0)
    wave_y = np.block([[cos_y, sin_y], [-sin_y, cos_y]])
    real_rows = np.concatenate([cos_x.T, -sin_x.T], axis=1)
    imag_rows = np.concatenate([sin_x.T, cos_x.T], axis=1)
    wave_rows = np.stack(
        [one.reshape(blocks, local_x, 2 * freqs) for one in (real_rows, imag_rows)], axis=1
    )
    sets = []
    for own in range(blocks):
        src, row = own // 2, own % 2
        mate = (src + src_count // 2) % src_count * 2 + 1 - row
        rows = np.concatenate([np.arange(local_x) + one * local_x for one in (own, mate)])
        c, s = cos_x[:, rows], sin_x[:, rows]
        pieces = []
        for one in range(2):
            cols = slice(one * local_x, (one + 1) * local_x)
            high, low = split_constant(np.block([[c[:, cols], s[:, cols]], [-s[:, cols], c[:, cols]]]))
            pieces.append(np.concatenate([high, high, low], axis=1))
        sets.append(np.stack(pieces))
    packed = np.concatenate([cos_y[:half], -sin_y[half:]], axis=0).T
    edges = []
    for start in (pixels - OV, 0):
        table = np.zeros((fold, 2 * freqs, fold, OV))
        for group in range(fold):
            table[group, :freqs, group] = packed[start : start + OV].T
            table[group, freqs + half, group] = cos_y[half, start : start + OV]
        edges.append(table.reshape(fold * 2 * freqs, freqs))
    move = np.zeros((freqs, freqs))
    move[order + half, np.arange(freqs)] = 1.0
    return (
        split_constant(packed),
        split_constant(spectrum),
        split_constant(wave_y),
        split_constant(wave_rows),
        np.stack(sets),
        split_constant(np.stack(edges), 1),
        move.astype(jnp.bfloat16),
    )


def split_constant(values, axis=0):
    values = values.astype(np.float32)
    high = values.astype(jnp.bfloat16)
    low = (values - high.astype(np.float32)).astype(jnp.bfloat16)
    return np.stack([high, low], axis=axis)


def sine_cosine(phase):
    quarter = 0.25 * phase
    square = quarter * quarter
    sine = 1.0 / 362880.0
    for term in (-1.0 / 5040.0, 1.0 / 120.0, -1.0 / 6.0, 1.0):
        sine = sine * square + term
    sine = sine * quarter
    fall = -1.0 / 40320.0
    for term in (1.0 / 720.0, -1.0 / 24.0, 0.5):
        fall = fall * square + term
    cosine = 1.0 - fall * square
    twice = 2.0 * sine
    sine, cosine = twice * cosine, 1.0 - twice * sine
    twice = 2.0 * sine
    return twice * cosine, 1.0 - twice * sine


def dot_exact(left_op, right_op, dims=(((1,), (0,)), ((), ()))):
    high, low = pair(left_op)

    def one(a):
        return lax.dot_general(a, right_op, dims, preferred_element_type=jnp.float32)

    return one(high) + one(low)


def kernel(
    src_count,
    tile_count,
    wm_hbm,
    wf_hbm,
    wy_hbm,
    wb_hbm,
    wx_hbm,
    we_hbm,
    move_hbm,
    mask_hbm,
    goal_hbm,
    band_hbm,
    phase_hbm,
    weight_hbm,
    out_ref,
    terms_ref,
    wm_ref,
    wf_ref,
    wy_ref,
    wb_ref,
    wx_ref,
    we_ref,
    move_ref,
    mask_ref,
    goal_ref,
    band_ref,
    phase_ref,
    weight_ref,
    load_sems,
    mbuf,
    pupil_ref,
    fbuf,
    ubuf,
    meta_ref,
    goals_ref,
    part_send,
    part_recv,
    tsend,
    trecv,
    csend,
    crecv,
    gsend,
    grecv,
    hsend,
    hrecv,
    mask_ss,
    mask_rs,
    fwd_ss,
    fwd_rs,
    meta_ss,
    meta_rs,
    phase_ss,
    phase_rs,
    pfwd_ss,
    pfwd_rs,
    goal_ss,
    goal_rs,
    part_ss,
    part_rs,
    core_ss,
    core_rs,
    grad_ss,
    grad_rs,
    halo_ss,
    halo_rs,
    ready_sem,
    token_sem,
    band_rows,
):
    part = lax.axis_index("parts")
    src = lax.axis_index("src")
    tile = lax.axis_index("tile")
    row = lax.axis_index("row")
    local_x, pixels = mask_ref.shape[1:]
    per_device, half, freqs = phase_ref.shape[1], phase_ref.shape[3], phase_ref.shape[4]
    sources = per_device * src_count
    field_scale = 1.0 / (pixels * freqs)
    fold = freqs // OV
    depth = local_x // fold
    other_row = 1 - row
    other_tile = 1 - tile
    last = src_count - 1
    own_slot = src * 2 + row
    mate_src = lax.rem(src + src_count // 2, src_count)
    mate_slot = mate_src * 2 + other_row
    pool_src = src + 1 - 2 * lax.rem(src, 2)

    side = lax.div(src, 2)
    far_first = [last * (1 - side), 2 - side, pool_src]
    near_first = far_first[::-1]

    def to(src_ref, dst_ref, ss, rs, src_at=src, tile_at=tile, row_at=other_row):
        return pltpu.make_async_remote_copy(
            src_ref=src_ref,
            dst_ref=dst_ref,
            send_sem=ss,
            recv_sem=rs,
            device_id=(part, src_at, tile_at, row_at),
            device_id_type=MESH,
        )

    def tell(semaphore, src_at, row_at, tile_at=tile):
        pl.semaphore_signal(
            semaphore, inc=1, device_id=(part, src_at, tile_at, row_at), device_id_type=MESH
        )

    barrier = pltpu.get_barrier_semaphore()

    @pl.when(side == 0)
    def _():
        for peer in (last, last - 1):
            for core in (other_row, row):
                tell(barrier, peer, core)
        tell(barrier, pool_src, other_row)
        tell(barrier, src, other_row, other_tile)
        tell(barrier, src, other_row)

    @pl.when(src == last - 1)
    def _():
        for core in (other_row, row):
            tell(barrier, last, core)

    loads = {}
    for index, (name, source, target) in enumerate(
        [
            ("mask", mask_hbm, mask_ref),
            ("wm", wm_hbm, wm_ref),
            ("weight", weight_hbm, weight_ref),
            ("band", band_hbm, band_ref),
            ("phase", phase_hbm, phase_ref.at[0]),
            ("goal", goal_hbm, goal_ref),
            ("move", move_hbm, move_ref),
            ("wf", wf_hbm, wf_ref),
            ("wb", wb_hbm, wb_ref),
            ("wy", wy_hbm, wy_ref),
            ("wx", wx_hbm.at[own_slot], wx_ref),
            ("we", we_hbm.at[tile], we_ref),
        ]
    ):
        loads[name] = pltpu.make_async_copy(source, target, load_sems.at[index])
        loads[name].start()

    pl.semaphore_wait(barrier, 3 * (1 - side) + 2 * side * src)

    @pl.when(side == 1)
    def _():
        for peer in (0, 1):
            tell(ready_sem, peer, other_row)

    @pl.when(src == last)
    def _():
        for core in (other_row, row):
            tell(ready_sem, last - 1, core)

    lanes = lax.broadcasted_iota(jnp.int32, (local_x, freqs), 1)
    spots = lax.broadcasted_iota(jnp.int32, (8, pixels), 1)
    turn = spots - 4 * lax.div(spots, 4)
    quarter_wave = jnp.where(turn == 0, 1.0, jnp.where(turn == 2, -1.0, 0.0))
    first_row = lax.broadcasted_iota(jnp.int32, (8, pixels), 0) == 0

    loads["mask"].wait()
    loads["wm"].wait()
    wm = (wm_ref[0], wm_ref[1])
    mask = mask_ref[0]
    mbuf[own_slot, :local_x] = dot_pair(pair(mask), wm)
    quarter_row = jnp.where(first_row, quarter_wave, 0.0).astype(jnp.bfloat16)
    padded = jnp.concatenate([mask, jnp.zeros((freqs - local_x, pixels), jnp.float32)], axis=0)
    high, low = pair(padded)
    nt = (((1,), (1,)), ((), ()))
    mbuf[own_slot, local_x:] = lax.dot_general(
        quarter_row, high, nt, preferred_element_type=jnp.float32
    ) + lax.dot_general(quarter_row, low, nt, preferred_element_type=jnp.float32)
    loads["weight"].wait()
    loads["band"].wait()
    for one in range(per_device):
        meta_ref[0, one : one + 1, :] = jnp.full((1, freqs), weight_ref[one] / sources)
    meta_ref[0, 8:, :] = jnp.concatenate(
        [band_ref[one] for one in range(per_device)]
        + [jnp.zeros((8 - 2 * per_device, freqs), jnp.int32)],
        axis=0,
    ).astype(jnp.float32)
    loads["phase"].wait()
    loads["goal"].wait()
    copies = []

    def send(*args, **keys):
        copy = to(*args, **keys)
        copy.start()
        copies.append(copy)
        return copy

    own_block = mbuf.at[own_slot]
    far_copies = [
        to(own_block, own_block, mask_ss.at[peer], mask_rs.at[src], src_at=peer)
        for peer in far_first[:-1]
    ]
    pool_copies = [
        to(own_block, own_block, mask_ss.at[pool_src], mask_rs.at[src], src_at=pool_src),
        to(meta_ref.at[0], meta_ref.at[1], meta_ss, meta_rs, src_at=pool_src),
    ]
    for one in range(per_device):
        pool_copies.append(
            to(
                phase_ref.at[0, one, row],
                phase_ref.at[1, one, row],
                phase_ss.at[one],
                phase_rs.at[one],
                src_at=pool_src,
            )
        )
    copies += far_copies + pool_copies

    def start(group):
        for copy in group:
            copy.start()

    @pl.when(side == 1)
    def _():
        start(far_copies)

    @pl.when(src != last - 1)
    def _():
        start(pool_copies)

    loads["move"].wait()
    move = move_ref[...]
    columns = lax.broadcasted_iota(jnp.int32, (half, freqs), 1).astype(jnp.float32)

    def read_bands(group):
        band_rows[...] = meta_ref[group, 8:, :].T

    def make_pupil(group, one, part_of):
        rows = pl.ds(pl.multiple_of(part_of * half, half), half)
        lower = band_rows[rows, 2 * one : 2 * one + 1]
        upper = band_rows[rows, 2 * one + 1 : 2 * one + 2]
        passing = (columns >= lower) & (columns < upper)
        sine, cosine = sine_cosine(phase_ref[group, one, part_of])
        moved = dot_exact(
            jnp.concatenate(
                [jnp.where(passing, cosine, 0.0), jnp.where(passing, sine, 0.0)], axis=0
            ),
            move,
        )
        pupil_ref[group, 2 * one, rows] = moved[:half]
        pupil_ref[group, 2 * one + 1, rows] = moved[half:]

    read_bands(0)
    for one in range(per_device):
        for part_of in range(2):
            make_pupil(0, one, part_of)

    @pl.when(src != last)
    def _():
        pl.semaphore_wait(ready_sem, 2)

    @pl.when(side == 0)
    def _():
        start(far_copies)

    @pl.when(src == last - 1)
    def _():
        start(pool_copies)

    for name in ("wf", "wb", "wy", "wx", "we"):
        loads[name].wait()

    for index, peer in enumerate(near_first):
        block = mbuf.at[peer * 2 + other_row]
        to(block, block, mask_ss.at[peer], mask_rs.at[peer], src_at=peer).wait_recv()
        send(block, block, fwd_ss.at[peer], fwd_rs.at[peer])
        if index == 0:
            send(own_block, own_block, fwd_ss.at[src], fwd_rs.at[src])
        if index == last - 1:
            send(goal_ref.at[0], goals_ref, goal_ss, goal_rs, src_at=mate_src)
    for one in range(per_device):
        half_block = phase_ref.at[1, one, other_row]
        to(
            half_block, half_block, phase_ss.at[one], phase_rs.at[one], src_at=pool_src
        ).wait_recv()
        send(half_block, half_block, pfwd_ss.at[one], pfwd_rs.at[one])
    to(meta_ref.at[0], meta_ref.at[1], meta_ss, meta_rs, src_at=pool_src).wait_recv()
    read_bands(1)
    for one in range(per_device):
        make_pupil(1, one, other_row)
    for peer in near_first:
        block = mbuf.at[peer * 2 + row]
        to(block, block, fwd_ss.at[peer], fwd_rs.at[peer]).wait_recv()
    block = mbuf.at[src * 2 + other_row]
    to(block, block, fwd_ss.at[src], fwd_rs.at[src]).wait_recv()

    @pl.when(side == 0)
    def _():
        tell(token_sem, src, other_row, other_tile)

    for one in range(per_device):
        half_block = phase_ref.at[1, one, row]
        to(half_block, half_block, pfwd_ss.at[one], pfwd_rs.at[one]).wait_recv()
    blocks = pixels // local_x
    extra = jnp.concatenate([mbuf[one, local_x : local_x + 1] for one in range(blocks)], axis=0).T
    rows = []
    for one in range(blocks):
        straight = mbuf[one, :local_x]
        turned = pltpu.roll(straight, half, axis=1)
        real = jnp.where(lanes < half, straight, turned)
        real = jnp.where(lanes == half, extra[:local_x, one : one + 1], real)
        imag = jnp.where(lanes < half, -turned, straight)
        imag = jnp.where(lanes == 0, 0.0, imag)
        rows.append(jnp.concatenate([real, imag], axis=1))
    spectrum = dot_pair((wf_ref[0], wf_ref[1]), pair(jnp.concatenate(rows, axis=0)))
    spec_real = spectrum[:freqs, :freqs] - spectrum[freqs:, freqs:]
    spec_imag = spectrum[:freqs, freqs:] + spectrum[freqs:, :freqs]

    wxt = tuple(
        jnp.concatenate(
            [wb_ref[index, slot, side] for side in range(2) for slot in (own_slot, mate_slot)],
            axis=0,
        )
        for index in range(2)
    )
    wy = (wy_ref[0], wy_ref[1])

    def swept_rows(group):
        reals, imags = [], []
        for one in range(per_device):
            pr, pi = pupil_ref[group, 2 * one], pupil_ref[group, 2 * one + 1]
            reals.append(pr * spec_real - pi * spec_imag)
            imags.append(pi * spec_real + pr * spec_imag)
        amps = jnp.concatenate(
            [jnp.concatenate(reals, axis=1), jnp.concatenate(imags, axis=1)], axis=0
        )
        return dot_pair(wxt, pair(amps)) * field_scale

    weights = [
        jnp.concatenate([meta_ref[group, one : one + 1, :]] * 2, axis=1)
        for group in range(2)
        for one in range(per_device)
    ]

    def light_of(swept, block):
        rows = []
        for group in range(2):
            tops = swept[group][block * local_x : (block + 1) * local_x]
            ends = swept[group][(2 + block) * local_x : (3 + block) * local_x]
            for one in range(per_device):
                cols = slice(one * freqs, (one + 1) * freqs)
                rows.append(jnp.concatenate([tops[:, cols], ends[:, cols]], axis=1))
        field = dot_pair(pair(jnp.concatenate(rows, axis=0)), wy)
        fbuf[block] = field
        squares = field[:, :pixels] * field[:, :pixels] + field[:, pixels:] * field[:, pixels:]
        total = weights[0] * squares[:local_x]
        for at in range(1, 2 * per_device):
            total = total + weights[at] * squares[at * local_x : (at + 1) * local_x]
        return total

    for one in range(per_device):
        make_pupil(1, one, row)
    swept = [swept_rows(group) for group in range(2)]
    lights = [None, None]
    @pl.when(side == 0)
    def _():
        pl.semaphore_wait(token_sem, 1)

    for block in (1, 0):
        lights[block] = light_of(swept, block)
        part_send[block] = lights[block]
        send(
            part_send.at[block],
            part_recv.at[1 - block],
            part_ss.at[block],
            part_rs.at[1 - block],
            src_at=mate_src,
        )
    to(goal_ref.at[0], goals_ref, goal_ss, goal_rs, src_at=mate_src).wait_recv()

    terms = [jnp.zeros((1, pixels), jnp.float32)] * (2 * per_device)
    spread = []
    for block in (0, 1):
        to(
            part_send.at[1 - block],
            part_recv.at[block],
            part_ss.at[1 - block],
            part_rs.at[block],
            src_at=mate_src,
        ).wait_recv()
        intensity = lights[block] + part_recv[block]
        goal = goal_ref[0] if block == 0 else goals_ref[...]
        resist = 1.0 / (1.0 + jnp.exp(-STEEPNESS * (intensity - THRESHOLD)))
        cotangent = LOSS_SCALE * (resist - goal) * STEEPNESS * resist * (1.0 - resist)
        backs = []
        for at in range(2 * per_device):
            field = fbuf[block, at * local_x : (at + 1) * local_x]
            real, imag = field[:, :pixels], field[:, pixels:]
            lit_real, lit_imag = cotangent * real, cotangent * imag
            scale = 2.0 * weights[at]
            backs.append(jnp.concatenate([scale * lit_real, scale * lit_imag], axis=1))
            terms[at] = terms[at] + jnp.sum(
                lit_real * real + lit_imag * imag, axis=0, keepdims=True
            )
        adjoint = dot_pair(pair(jnp.concatenate(backs, axis=0)), wy, 1)
        for at in range(2 * per_device):
            rows = slice(at * local_x, (at + 1) * local_x)
            cols = slice(at * freqs, (at + 1) * freqs)
            ubuf[0, :, cols] = adjoint[rows, :freqs]
            ubuf[1, :, cols] = adjoint[rows, freqs:]
        high, low = pair(ubuf[...].reshape(2 * local_x, 2 * per_device * freqs))
        spread.append(
            jnp.dot(
                wx_ref[block],
                jnp.concatenate([high, low, high], axis=0),
                preferred_element_type=jnp.float32,
            )
        )

    blank = jnp.zeros((1, freqs), jnp.float32)
    for group in range(2):
        tsend[group] = jnp.concatenate(
            [blank]
            + [
                terms[group * per_device + one][:, :freqs]
                + terms[group * per_device + one][:, freqs:]
                for one in range(per_device)
            ]
            + [blank] * (7 - per_device),
            axis=0,
        )
    term_copy = send(tsend, trecv, core_ss.at[src_count], core_rs.at[src_count])

    swept = (spread[0] + spread[1]) * field_scale
    grad_real = jnp.zeros((freqs, freqs), jnp.float32)
    grad_imag = grad_real
    for at in range(2 * per_device):
        group, one = at // per_device, at % per_device
        pr, pi = pupil_ref[group, 2 * one], pupil_ref[group, 2 * one + 1]
        cols = slice(at * freqs, (at + 1) * freqs)
        real, imag = swept[:freqs, cols], swept[freqs:, cols]
        grad_real = grad_real + pr * real + pi * imag
        grad_imag = grad_imag + pr * imag - pi * real

    lane = lax.broadcasted_iota(jnp.int32, (freqs, freqs), 1)
    turn_real = pltpu.roll(grad_real, half, axis=1)
    turn_imag = pltpu.roll(grad_imag, half, axis=1)
    sum_real = grad_real + jnp.where(lane == 0, 0.0, turn_real)
    sum_imag = grad_imag + jnp.where(lane == 0, 0.0, turn_imag)
    gap_real = jnp.where(lane == half, 0.0, turn_real) - grad_real
    gap_imag = jnp.where(lane == half, 0.0, turn_imag) - grad_imag
    upper = jnp.where(lane < half, sum_real, -gap_imag)
    lower = jnp.where(lane < half, sum_imag, gap_real)
    grads = pair(
        jnp.concatenate(
            [
                jnp.concatenate([upper, grad_real], axis=1),
                jnp.concatenate([lower, grad_imag], axis=1),
            ],
            axis=0,
        )
    )

    def rows_of(far_row, own_row):
        slots = [peer * 2 + far_row for peer in far_first] + [src * 2 + own_row]
        waves = tuple(
            jnp.concatenate([wb_ref[index, slot, 0] for slot in slots], axis=0)
            for index in range(2)
        )
        return dot_pair(waves, grads)

    theirs = rows_of(row, other_row)
    for index in range(src_count):
        csend[index] = theirs[index * local_x : (index + 1) * local_x]
        send(csend.at[index], crecv.at[index], core_ss.at[index], core_rs.at[index])
    mine = rows_of(other_row, row)
    strips = jnp.concatenate(
        [
            jnp.concatenate(
                [
                    blocks_of[
                        index * local_x + one * depth : index * local_x + (one + 1) * depth
                    ]
                    for one in range(fold)
                ],
                axis=1,
            )
            for blocks_of in (theirs, mine)
            for index in range(src_count)
        ],
        axis=0,
    )
    strips = dot_pair(pair(strips), (we_ref[0], we_ref[1]))
    for side, near_row, far_row in ((0, other_row, row), (1, row, other_row)):
        for index, peer in enumerate(far_first + [src]):
            at = side * src_count + index
            hsend[at, :depth] = strips[at * depth : (at + 1) * depth]
            tall = depth if index < last - 1 else depth + 8
            if index >= last - 1:
                hsend[at, depth:] = tsend[last - index]
            send(
                hsend.at[at, :tall],
                hrecv.at[own_slot, :tall],
                halo_ss.at[at],
                halo_rs.at[own_slot],
                src_at=peer,
                tile_at=other_tile,
                row_at=far_row if index < last else near_row,
            )
    term_copy.wait_recv()
    own_terms = tsend[0] + trecv[0]
    pool_terms = tsend[1] + trecv[1]
    for index in range(src_count):
        gsend[index, local_x:] = pool_terms if index < last else own_terms
    for index, peer in enumerate(far_first + [src]):
        to(csend.at[index], crecv.at[index], core_ss.at[index], core_rs.at[index]).wait_recv()
        both = mine[index * local_x : (index + 1) * local_x] + crecv[index]
        gsend[index, :local_x] = both[:, :freqs]
        gsend[index, local_x : local_x + 1, :local_x] = both[:, freqs:].T[half : half + 1]
        if index < last:
            send(
                gsend.at[index], grecv.at[src], grad_ss.at[index], grad_rs.at[src], src_at=peer
            )

    total = gsend[last]
    for peer in near_first:
        to(
            gsend.at[0], grecv.at[peer], grad_ss.at[0], grad_rs.at[peer], src_at=peer
        ).wait_recv()
        total = total + grecv[peer]
    grad_block = dot_pair(pair(total[:local_x]), wm, 1)
    grad_block = grad_block + total[local_x:].T[:local_x, :1] * quarter_wave[:1]
    low, high = grad_block[:, :freqs], grad_block[:, pixels - freqs :]

    packed = jnp.zeros((depth, freqs), jnp.float32)
    for index, peer in enumerate([src] + near_first):
        tall = depth if index > 1 else depth + 8
        for core in range(2):
            slot = peer * 2 + core
            to(
                hsend.at[0, :tall],
                hrecv.at[slot, :tall],
                halo_ss.at[0],
                halo_rs.at[slot],
                src_at=peer,
                tile_at=other_tile,
                row_at=core,
            ).wait_recv()
            packed = packed + hrecv[slot, :depth]
    strip = jnp.concatenate(
        [packed]
        + [pltpu.roll(packed, freqs - one * OV, axis=1) for one in range(1, fold)],
        axis=0,
    )
    from_below = jnp.where((lanes < OV) & (tile == 1), strip, 0.0)
    from_above = jnp.where(
        (lanes >= freqs - OV) & (tile == 0), pltpu.roll(strip, freqs - OV, axis=1), 0.0
    )
    out_ref[0, :, :freqs] = low + from_below
    out_ref[0, :, pixels - freqs :] = high + from_above
    terms = own_terms + grecv[pool_src, local_x:]
    for slot in (src * 2, src * 2 + 1, pool_src * 2, pool_src * 2 + 1):
        terms = terms + hrecv[slot, depth:]
    terms = terms / (sources * pixels * tile_count)
    terms_ref[...] = terms
    for copy in copies:
        copy.wait_send()


def finish_kernel(grads_ref, terms_ref, out_ref, sums_ref, held_ref, sems):
    copy = pltpu.make_async_copy(grads_ref, out_ref, sems.at[0])
    copy.start()
    for one in range(held_ref.shape[0]):
        held_ref[one] = jnp.sum(terms_ref[one + 1 : one + 2, :])
    other = pltpu.make_async_copy(held_ref, sums_ref, sems.at[1])
    other.start()
    copy.wait()
    other.wait()


def finish(grads, terms, shape):
    in_vmem = pl.BlockSpec(memory_space=pltpu.VMEM)
    in_hbm = pl.BlockSpec(memory_space=pltpu.HBM)
    return pl.pallas_call(
        finish_kernel,
        out_shape=(
            jax.ShapeDtypeStruct(grads.shape, grads.dtype),
            jax.ShapeDtypeStruct(shape, terms.dtype),
        ),
        in_specs=[in_vmem, in_vmem],
        out_specs=(in_hbm, in_hbm),
        scratch_shapes=[pltpu.SMEM(shape, terms.dtype), pltpu.SemaphoreType.DMA((2,))],
    )(*(pltpu.with_memory_space_constraint(one, pltpu.VMEM) for one in (grads, terms)))


def shards(mask_windows, target_windows, pupil_bands, pupil_phase, source_weight):
    src_count = lax.axis_size("src")
    tile_count = lax.axis_size("tile")
    row_count = lax.axis_size("row")
    local_x, pixels = mask_windows.shape[1:]
    per_device, freqs = pupil_phase.shape[:2]
    blocks = src_count * row_count
    fits = row_count == 2 and tile_count == 2 and src_count == 4 and 2 * per_device <= 8
    fits = fits and freqs == 128 and pixels == 2 * freqs and local_x == OV
    if not fits or local_x * blocks != pixels or OV * 4 != freqs:
        return shards_plain(
            mask_windows, target_windows, pupil_bands, pupil_phase, source_weight
        )
    half, fold = freqs // 2, freqs // OV
    tables = wave_constants(pixels, freqs, blocks, src_count, local_x, fold)
    bands = jnp.transpose(pupil_bands, (0, 2, 1))
    phases = pupil_phase.reshape(per_device, 2, half, freqs)
    in_vmem = pl.BlockSpec(memory_space=pltpu.VMEM)
    in_smem = pl.BlockSpec(memory_space=pltpu.SMEM)
    f32 = jnp.float32
    block = (local_x, pixels)
    dma = pltpu.SemaphoreType.DMA
    like = [pltpu.VMEM(one.shape, one.dtype) for one in tables]
    like[4] = pltpu.VMEM(tables[4].shape[1:], tables[4].dtype)
    like[5] = pltpu.VMEM(tables[5].shape[1:], tables[5].dtype)
    four = dma((src_count,))
    grads, terms = pl.pallas_call(
        functools.partial(kernel, src_count, tile_count),
        out_shape=(
            pltpu.VMEM(mask_windows.shape, f32),
            pltpu.VMEM((8, freqs), f32),
        ),
        in_specs=[pl.BlockSpec(memory_space=pltpu.HBM)] * 12,
        out_specs=(in_vmem, in_vmem),
        scratch_shapes=like
        + [
            pltpu.VMEM(mask_windows.shape, f32),
            pltpu.VMEM(target_windows.shape, f32),
            pltpu.VMEM(bands.shape, bands.dtype),
            pltpu.VMEM((2,) + phases.shape, f32),
            pltpu.SMEM(source_weight.shape, f32),
            dma((12,)),
            pltpu.VMEM((blocks, local_x + 8, freqs), f32),
            pltpu.VMEM((2, 2 * per_device, freqs, freqs), f32),
            pltpu.VMEM((2, 2 * per_device * local_x, 2 * pixels), f32),
            pltpu.VMEM((2, local_x, 2 * per_device * freqs), f32),
            pltpu.VMEM((2, 16, freqs), f32),
            pltpu.VMEM(block, f32),
            pltpu.VMEM((2,) + block, f32),
            pltpu.VMEM((2,) + block, f32),
            pltpu.VMEM((2, 8, freqs), f32),
            pltpu.VMEM((2, 8, freqs), f32),
            pltpu.VMEM((src_count,) + block, f32),
            pltpu.VMEM((src_count,) + block, f32),
            pltpu.VMEM((src_count, local_x + 8, freqs), f32),
            pltpu.VMEM((src_count, local_x + 8, freqs), f32),
            pltpu.VMEM((blocks, 16, freqs), f32),
            pltpu.VMEM((blocks, 16, freqs), f32),
        ]
        + [four] * 4
        + [dma(())] * 2
        + [dma((per_device,))] * 4
        + [dma(())] * 2
        + [dma((2,))] * 2
        + [dma((src_count + 1,))] * 2
        + [four] * 2
        + [dma((blocks,))] * 2
        + [pltpu.SemaphoreType.REGULAR] * 2
        + [pltpu.VMEM((freqs, 8), f32)],
        compiler_params=pltpu.CompilerParams(
            collective_id=0, has_side_effects=True, vmem_limit_bytes=63 * 1024 * 1024
        ),
    )(*tables, mask_windows, target_windows, bands, phases, source_weight)
    return finish(grads, terms, source_weight.shape)


def solution(mesh):
    return jax.shard_map(
        shards,
        mesh=mesh,
        in_specs=(
            P(("parts", "tile"), ("src", "row"), None),
            P(("parts", "tile"), ("src", "row"), None),
            P(("parts", "src"), None, None),
            P(("parts", "src"), None, None),
            P(("parts", "src")),
        ),
        out_specs=(P(("parts", "tile"), ("src", "row"), None), P(("parts", "src"))),
        check_vma=False,
    )
```

```python
import functools
import math

import jax
import jax.numpy as jnp
import numpy as np
from jax import lax
from jax.experimental import pallas as pl
from jax.experimental.pallas import tpu as pltpu
from jax.sharding import PartitionSpec as P

M = 256
K = 128
OV = 32


STEEPNESS = 20.0
THRESHOLD = 0.15
LOSS_SCALE = 32.0


def with_halo(block, sides, width):
    for axis, dim in sides:
        count = lax.axis_size(axis)
        forward = [(i, i + 1) for i in range(count - 1)]
        backward = [(target, source) for source, target in forward]
        low = lax.ppermute(
            lax.slice_in_dim(block, block.shape[dim] - width, None, axis=dim), axis, forward
        )
        high = lax.ppermute(lax.slice_in_dim(block, 0, width, axis=dim), axis, backward)
        block = jnp.concatenate([low, block, high], axis=dim)
    return block


def matmul(left_op, right_op):
    return lax.dot_general(
        left_op,
        right_op,
        (((1,), (0,)), ((), ())),
        precision=lax.Precision.HIGHEST,
        preferred_element_type=jnp.float32,
    )


def matmul_tn(left_op, right_op):
    return lax.dot_general(
        left_op,
        right_op,
        (((0,), (0,)), ((), ())),
        precision=lax.Precision.HIGHEST,
        preferred_element_type=jnp.float32,
    )


def matmul_nt(left_op, right_op):
    return lax.dot_general(
        left_op,
        right_op,
        (((1,), (1,)), ((), ())),
        precision=lax.Precision.HIGHEST,
        preferred_element_type=jnp.float32,
    )


def wave_tables(positions):
    freq_index = jnp.arange(K, dtype=jnp.int32) - K // 2
    phase_index = freq_index[:, None] * positions[None, :] % M
    angles = 2.0 * math.pi / M * phase_index.astype(jnp.float32)
    return (jnp.cos(angles), jnp.sin(angles))


def shards_plain(mask_windows, target_windows, pupil_bands, pupil_phase, source_weight):
    src_count = lax.axis_size("src")
    tile_count = lax.axis_size("tile")
    row_count = lax.axis_size("row")
    local_x = mask_windows.shape[1]
    per_device = pupil_phase.shape[0]
    sources = per_device * src_count
    field_scale = 1.0 / (M * K)
    src_id = lax.axis_index("src")
    row_id = lax.axis_index("row")
    x_start = (src_id * row_count + row_id) * local_x
    block_starts = (jnp.arange(src_count, dtype=jnp.int32) * row_count + row_id) * local_x
    row_set = (block_starts[:, None] + jnp.arange(local_x, dtype=jnp.int32)[None, :]).reshape(
        src_count * local_x
    )
    cos_all, sin_all = wave_tables(jnp.arange(M, dtype=jnp.int32))
    cos_set, sin_set = wave_tables(row_set)
    cos_own, sin_own = wave_tables(x_start + jnp.arange(local_x, dtype=jnp.int32))
    window = mask_windows[0]
    goal_block = target_windows[0]
    zero_spec = jnp.zeros((K, K), jnp.float32)
    shard_rows = lax.all_gather(window, ("src", "row"), axis=0, tiled=True)
    part_real = matmul_nt(shard_rows, cos_all)
    part_imag = -matmul_nt(shard_rows, sin_all)
    spec_real = matmul(cos_all, part_real) + matmul(sin_all, part_imag)
    spec_imag = matmul(cos_all, part_imag) - matmul(sin_all, part_real)
    freq_cols = jnp.arange(K, dtype=jnp.int32)
    inside = (freq_cols[None, None, :] >= pupil_bands[:, :, 0:1]) & (
        freq_cols[None, None, :] < pupil_bands[:, :, 1:2]
    )
    passing = inside.astype(jnp.float32)
    pupil_real = passing * jnp.cos(pupil_phase)
    pupil_imag = passing * jnp.sin(pupil_phase)
    amp_real = (pupil_real * spec_real - pupil_imag * spec_imag).reshape(per_device * K, K)
    amp_imag = (pupil_imag * spec_real + pupil_real * spec_imag).reshape(per_device * K, K)
    half_real = (matmul(amp_real, cos_all) - matmul(amp_imag, sin_all)).reshape(per_device, K, M)
    half_imag = (matmul(amp_real, sin_all) + matmul(amp_imag, cos_all)).reshape(per_device, K, M)
    weights = source_weight / sources

    def fields(pair_in):
        one_real, one_imag = pair_in
        field_real = field_scale * (matmul_tn(cos_set, one_real) - matmul_tn(sin_set, one_imag))
        field_imag = field_scale * (matmul_tn(cos_set, one_imag) + matmul_tn(sin_set, one_real))
        return (field_real, field_imag)

    stack_real, stack_imag = lax.map(fields, (half_real, half_imag))
    part_real = stack_real
    part_imag = stack_imag
    intensity = lax.psum_scatter(
        jnp.sum(weights[:, None, None] * (part_real * part_real + part_imag * part_imag), axis=0),
        "src",
        scatter_dimension=0,
        tiled=True,
    )
    resist = jax.nn.sigmoid(STEEPNESS * (intensity - THRESHOLD))
    cotangent = LOSS_SCALE * (resist - goal_block) * STEEPNESS * resist * (1.0 - resist)
    cotangent_all = lax.all_gather(cotangent, "src", axis=0, tiled=True)
    source_ids = jnp.arange(per_device, dtype=jnp.int32)

    def add_back(source_id, totals):
        grad_real, grad_imag, source_terms = totals
        field_real = stack_real[source_id]
        field_imag = stack_imag[source_id]
        back_scale = 2.0 * weights[source_id] * cotangent_all
        back_real = back_scale * field_real
        back_imag = back_scale * field_imag
        adj_real = matmul(cos_set, back_real) + matmul(sin_set, back_imag)
        adj_imag = matmul(cos_set, back_imag) - matmul(sin_set, back_real)
        amp_grad_real = field_scale * (matmul_nt(adj_real, cos_all) + matmul_nt(adj_imag, sin_all))
        amp_grad_imag = field_scale * (matmul_nt(adj_imag, cos_all) - matmul_nt(adj_real, sin_all))
        pass_real = pupil_real[source_id]
        pass_imag = pupil_imag[source_id]
        grad_real = grad_real + pass_real * amp_grad_real + pass_imag * amp_grad_imag
        grad_imag = grad_imag + pass_real * amp_grad_imag - pass_imag * amp_grad_real
        term_value = jnp.sum(cotangent_all * (field_real * field_real + field_imag * field_imag))
        source_terms = source_terms + jnp.where(source_ids == source_id, term_value, 0.0)
        return (grad_real, grad_imag, source_terms)

    grad_real, grad_imag, source_terms = lax.fori_loop(
        0, per_device, add_back, (zero_spec, zero_spec, jnp.zeros((per_device,), jnp.float32))
    )
    grad_real, grad_imag = lax.psum((grad_real, grad_imag), ("src", "row"))
    source_sum = lax.psum(source_terms, ("tile", "row"))
    source_grad = source_sum / (sources * M * tile_count)
    q_one = matmul(grad_real, cos_all) - matmul(grad_imag, sin_all)
    q_two = matmul(grad_real, sin_all) + matmul(grad_imag, cos_all)
    grad_block = matmul_tn(cos_own, q_one) - matmul_tn(sin_own, q_two)
    padded = with_halo(grad_block, (("tile", 1),), OV)
    from_below = padded[:, :OV]
    from_above = padded[:, M + OV :]
    middle = jnp.zeros((local_x, M - 2 * OV), jnp.float32)
    grad_block = grad_block + jnp.concatenate([from_below, middle, from_above], axis=1)
    return (grad_block[None], source_grad)


MESH = pl.DeviceIdType.MESH


def pair(values):
    high = values.astype(jnp.bfloat16)
    return high, (values - high.astype(jnp.float32)).astype(jnp.bfloat16)


def dot_pair(left_op, right_op, contract_right=0):
    dims = (((1,), (contract_right,)), ((), ()))

    def one(a, b):
        return lax.dot_general(a, b, dims, preferred_element_type=jnp.float32)

    (left_high, left_low), (right_high, right_low) = left_op, right_op
    both = one(jnp.concatenate([left_high, left_low], axis=0), right_high)
    count = left_high.shape[0]
    return both[:count] + (both[count:] + one(left_high, right_low))


def frequency_order(freqs):
    half = freqs // 2
    return np.concatenate([np.arange(half), [-half], -np.arange(1, half)])


def wave_constants(pixels, freqs, blocks, src_count, local_x, fold):
    half = freqs // 2
    spots = np.arange(pixels)

    def waves(index):
        angles = 2.0 * np.pi / pixels * (np.outer(index, spots) % pixels)
        return np.cos(angles), np.sin(angles)

    cos_x, sin_x = waves(np.arange(freqs) - half)
    order = frequency_order(freqs)
    cos_y, sin_y = waves(order)
    spectrum = np.concatenate([cos_x, -sin_x], axis=0)
    wave_y = np.block([[cos_y, sin_y], [-sin_y, cos_y]])
    real_rows = np.concatenate([cos_x.T, -sin_x.T], axis=1)
    imag_rows = np.concatenate([sin_x.T, cos_x.T], axis=1)
    wave_rows = np.stack(
        [one.reshape(blocks, local_x, 2 * freqs) for one in (real_rows, imag_rows)], axis=1
    )
    sets = []
    for own in range(blocks):
        src, row = own // 2, own % 2
        mate = (src + src_count // 2) % src_count * 2 + 1 - row
        rows = np.concatenate([np.arange(local_x) + one * local_x for one in (own, mate)])
        c, s = cos_x[:, rows], sin_x[:, rows]
        pieces = []
        for one in range(2):
            cols = slice(one * local_x, (one + 1) * local_x)
            high, low = split_constant(np.block([[c[:, cols], s[:, cols]], [-s[:, cols], c[:, cols]]]))
            pieces.append(np.concatenate([high, high, low], axis=1))
        sets.append(np.stack(pieces))
    packed = np.concatenate([cos_y[:half], -sin_y[half:]], axis=0).T
    edges = []
    for start in (pixels - OV, 0):
        table = np.zeros((fold, 2 * freqs, fold, OV))
        for group in range(fold):
            table[group, :freqs, group] = packed[start : start + OV].T
            table[group, freqs + half, group] = cos_y[half, start : start + OV]
        edges.append(table.reshape(fold * 2 * freqs, freqs))
    move = np.zeros((freqs, freqs))
    move[order + half, np.arange(freqs)] = 1.0
    return (
        split_constant(packed),
        split_constant(spectrum),
        split_constant(wave_y),
        split_constant(wave_rows),
        np.stack(sets),
        split_constant(np.stack(edges), 1),
        move.astype(jnp.bfloat16),
    )


def split_constant(values, axis=0):
    values = values.astype(np.float32)
    high = values.astype(jnp.bfloat16)
    low = (values - high.astype(np.float32)).astype(jnp.bfloat16)
    return np.stack([high, low], axis=axis)


def sine_cosine(phase):
    quarter = 0.25 * phase
    square = quarter * quarter
    sine = 1.0 / 362880.0
    for term in (-1.0 / 5040.0, 1.0 / 120.0, -1.0 / 6.0, 1.0):
        sine = sine * square + term
    sine = sine * quarter
    fall = -1.0 / 40320.0
    for term in (1.0 / 720.0, -1.0 / 24.0, 0.5):
        fall = fall * square + term
    cosine = 1.0 - fall * square
    twice = 2.0 * sine
    sine, cosine = twice * cosine, 1.0 - twice * sine
    twice = 2.0 * sine
    return twice * cosine, 1.0 - twice * sine


def dot_exact(left_op, right_op, dims=(((1,), (0,)), ((), ()))):
    high, low = pair(left_op)

    def one(a):
        return lax.dot_general(a, right_op, dims, preferred_element_type=jnp.float32)

    return one(high) + one(low)


def kernel(
    src_count,
    tile_count,
    wm_hbm,
    wf_hbm,
    wy_hbm,
    wb_hbm,
    wx_hbm,
    we_hbm,
    move_hbm,
    mask_hbm,
    goal_hbm,
    band_hbm,
    phase_hbm,
    weight_hbm,
    out_ref,
    terms_ref,
    wm_ref,
    wf_ref,
    wy_ref,
    wb_ref,
    wx_ref,
    we_ref,
    move_ref,
    mask_ref,
    goal_ref,
    band_ref,
    phase_ref,
    weight_ref,
    load_sems,
    mbuf,
    pupil_ref,
    fbuf,
    ubuf,
    meta_ref,
    goals_ref,
    part_send,
    part_recv,
    tsend,
    trecv,
    csend,
    crecv,
    gsend,
    grecv,
    hsend,
    hrecv,
    mask_ss,
    mask_rs,
    fwd_ss,
    fwd_rs,
    meta_ss,
    meta_rs,
    phase_ss,
    phase_rs,
    pfwd_ss,
    pfwd_rs,
    goal_ss,
    goal_rs,
    part_ss,
    part_rs,
    core_ss,
    core_rs,
    grad_ss,
    grad_rs,
    halo_ss,
    halo_rs,
    ready_sem,
    token_sem,
    band_rows,
):
    part = lax.axis_index("parts")
    src = lax.axis_index("src")
    tile = lax.axis_index("tile")
    row = lax.axis_index("row")
    local_x, pixels = mask_ref.shape[1:]
    per_device, half, freqs = phase_ref.shape[1], phase_ref.shape[3], phase_ref.shape[4]
    sources = per_device * src_count
    field_scale = 1.0 / (pixels * freqs)
    fold = freqs // OV
    depth = local_x // fold
    other_row = 1 - row
    other_tile = 1 - tile
    last = src_count - 1
    own_slot = src * 2 + row
    mate_src = lax.rem(src + src_count // 2, src_count)
    mate_slot = mate_src * 2 + other_row
    pool_src = src + 1 - 2 * lax.rem(src, 2)

    side = lax.div(src, 2)
    far_first = [last * (1 - side), 2 - side, pool_src]
    near_first = far_first[::-1]

    def to(src_ref, dst_ref, ss, rs, src_at=src, tile_at=tile, row_at=other_row):
        return pltpu.make_async_remote_copy(
            src_ref=src_ref,
            dst_ref=dst_ref,
            send_sem=ss,
            recv_sem=rs,
            device_id=(part, src_at, tile_at, row_at),
            device_id_type=MESH,
        )

    def tell(semaphore, src_at, row_at, tile_at=tile):
        pl.semaphore_signal(
            semaphore, inc=1, device_id=(part, src_at, tile_at, row_at), device_id_type=MESH
        )

    barrier = pltpu.get_barrier_semaphore()

    @pl.when(side == 0)
    def _():
        for peer in (last, last - 1):
            tell(barrier, peer, other_row)
        tell(barrier, pool_src, other_row)
        tell(barrier, src, other_row, other_tile)
        tell(barrier, src, other_row)

    @pl.when(src == last - 1)
    def _():
        for core in (other_row, row):
            tell(barrier, last, core)

    loads = {}
    for index, (name, source, target) in enumerate(
        [
            ("mask", mask_hbm, mask_ref),
            ("wm", wm_hbm, wm_ref),
            ("weight", weight_hbm, weight_ref),
            ("band", band_hbm, band_ref),
            ("phase", phase_hbm, phase_ref.at[0]),
            ("goal", goal_hbm, goal_ref),
            ("move", move_hbm, move_ref),
            ("wf", wf_hbm, wf_ref),
            ("wb", wb_hbm, wb_ref),
            ("wy", wy_hbm, wy_ref),
            ("wx", wx_hbm.at[own_slot], wx_ref),
            ("we", we_hbm.at[tile], we_ref),
        ]
    ):
        loads[name] = pltpu.make_async_copy(source, target, load_sems.at[index])
        loads[name].start()

    pl.semaphore_wait(barrier, 3 * (1 - side) + 2 * side * (src - 1))

    @pl.when(side == 1)
    def _():
        for peer in (0, 1):
            tell(ready_sem, peer, other_row)

    @pl.when(src == last)
    def _():
        for core in (other_row, row):
            tell(ready_sem, last - 1, core)

    lanes = lax.broadcasted_iota(jnp.int32, (local_x, freqs), 1)
    spots = lax.broadcasted_iota(jnp.int32, (8, pixels), 1)
    turn = spots - 4 * lax.div(spots, 4)
    quarter_wave = jnp.where(turn == 0, 1.0, jnp.where(turn == 2, -1.0, 0.0))
    first_row = lax.broadcasted_iota(jnp.int32, (8, pixels), 0) == 0

    loads["mask"].wait()
    loads["wm"].wait()
    wm = (wm_ref[0], wm_ref[1])
    mask = mask_ref[0]
    mbuf[own_slot, :local_x] = dot_pair(pair(mask), wm)
    quarter_row = jnp.where(first_row, quarter_wave, 0.0).astype(jnp.bfloat16)
    padded = jnp.concatenate([mask, jnp.zeros((freqs - local_x, pixels), jnp.float32)], axis=0)
    high, low = pair(padded)
    nt = (((1,), (1,)), ((), ()))
    mbuf[own_slot, local_x:] = lax.dot_general(
        quarter_row, high, nt, preferred_element_type=jnp.float32
    ) + lax.dot_general(quarter_row, low, nt, preferred_element_type=jnp.float32)
    loads["weight"].wait()
    loads["band"].wait()
    for one in range(per_device):
        meta_ref[0, one : one + 1, :] = jnp.full((1, freqs), weight_ref[one] / sources)
    meta_ref[0, 8:, :] = jnp.concatenate(
        [band_ref[one] for one in range(per_device)]
        + [jnp.zeros((8 - 2 * per_device, freqs), jnp.int32)],
        axis=0,
    ).astype(jnp.float32)
    loads["phase"].wait()
    loads["goal"].wait()
    copies = []

    def send(*args, **keys):
        copy = to(*args, **keys)
        copy.start()
        copies.append(copy)
        return copy

    own_block = mbuf.at[own_slot, : local_x + 1]
    far_copies = [
        to(own_block, own_block, mask_ss.at[peer], mask_rs.at[src], src_at=peer)
        for peer in far_first[:-1]
    ]
    pool_copies = [
        to(own_block, own_block, mask_ss.at[pool_src], mask_rs.at[src], src_at=pool_src),
        to(meta_ref.at[0], meta_ref.at[1], meta_ss, meta_rs, src_at=pool_src),
    ]
    for one in range(per_device):
        pool_copies.append(
            to(
                phase_ref.at[0, one, row],
                phase_ref.at[1, one, row],
                phase_ss.at[one],
                phase_rs.at[one],
                src_at=pool_src,
            )
        )
    goal_copy = to(goal_ref.at[0], goals_ref, goal_ss, goal_rs, src_at=mate_src)
    copies += far_copies + pool_copies + [goal_copy]

    def start(group):
        for copy in group:
            copy.start()

    @pl.when(side == 1)
    def _():
        start(far_copies)

    @pl.when(src != last - 1)
    def _():
        start(pool_copies)

    loads["move"].wait()
    move = move_ref[...]
    columns = lax.broadcasted_iota(jnp.int32, (half, freqs), 1).astype(jnp.float32)

    def read_bands(group):
        band_rows[...] = meta_ref[group, 8:, :].T

    def make_pupil(group, one, part_of):
        rows = pl.ds(pl.multiple_of(part_of * half, half), half)
        lower = band_rows[rows, 2 * one : 2 * one + 1]
        upper = band_rows[rows, 2 * one + 1 : 2 * one + 2]
        passing = (columns >= lower) & (columns < upper)
        sine, cosine = sine_cosine(phase_ref[group, one, part_of])
        moved = dot_exact(
            jnp.concatenate(
                [jnp.where(passing, cosine, 0.0), jnp.where(passing, sine, 0.0)], axis=0
            ),
            move,
        )
        pupil_ref[group, 2 * one, rows] = moved[:half]
        pupil_ref[group, 2 * one + 1, rows] = moved[half:]

    read_bands(0)
    for one in range(per_device):
        for part_of in range(2):
            make_pupil(0, one, part_of)

    @pl.when(src != last)
    def _():
        pl.semaphore_wait(ready_sem, 2)

    @pl.when(side == 0)
    def _():
        start(far_copies)

    @pl.when(src == last - 1)
    def _():
        start(pool_copies)

    @pl.when(side == 1)
    def _():
        goal_copy.start()

    for name in ("wf", "wb", "wy", "wx", "we"):
        loads[name].wait()

    for index, peer in enumerate(near_first):
        block = mbuf.at[peer * 2 + other_row, : local_x + 1]
        to(block, block, mask_ss.at[peer], mask_rs.at[peer], src_at=peer).wait_recv()
        send(block, block, fwd_ss.at[peer], fwd_rs.at[peer])
        if index == 0:
            send(own_block, own_block, fwd_ss.at[src], fwd_rs.at[src])
        if index == last - 1:
            pl.when(side == 0)(goal_copy.start)
    for one in range(per_device):
        half_block = phase_ref.at[1, one, other_row]
        to(
            half_block, half_block, phase_ss.at[one], phase_rs.at[one], src_at=pool_src
        ).wait_recv()
        send(half_block, half_block, pfwd_ss.at[one], pfwd_rs.at[one])
    to(meta_ref.at[0], meta_ref.at[1], meta_ss, meta_rs, src_at=pool_src).wait_recv()
    read_bands(1)
    for one in range(per_device):
        make_pupil(1, one, other_row)
    for peer in near_first:
        block = mbuf.at[peer * 2 + row, : local_x + 1]
        to(block, block, fwd_ss.at[peer], fwd_rs.at[peer]).wait_recv()
    block = mbuf.at[src * 2 + other_row, : local_x + 1]
    to(block, block, fwd_ss.at[src], fwd_rs.at[src]).wait_recv()

    @pl.when(side == 0)
    def _():
        tell(token_sem, src, other_row, other_tile)

    for one in range(per_device):
        half_block = phase_ref.at[1, one, row]
        to(half_block, half_block, pfwd_ss.at[one], pfwd_rs.at[one]).wait_recv()
    blocks = pixels // local_x
    extra = jnp.concatenate([mbuf[one, local_x : local_x + 1] for one in range(blocks)], axis=0).T
    rows = []
    for one in range(blocks):
        straight = mbuf[one, :local_x]
        turned = pltpu.roll(straight, half, axis=1)
        real = jnp.where(lanes < half, straight, turned)
        real = jnp.where(lanes == half, extra[:local_x, one : one + 1], real)
        imag = jnp.where(lanes < half, -turned, straight)
        imag = jnp.where(lanes == 0, 0.0, imag)
        rows.append(jnp.concatenate([real, imag], axis=1))
    spectrum = dot_pair((wf_ref[0], wf_ref[1]), pair(jnp.concatenate(rows, axis=0)))
    spec_real = spectrum[:freqs, :freqs] - spectrum[freqs:, freqs:]
    spec_imag = spectrum[:freqs, freqs:] + spectrum[freqs:, :freqs]

    wxt = tuple(
        jnp.concatenate(
            [wb_ref[index, slot, side] for side in range(2) for slot in (own_slot, mate_slot)],
            axis=0,
        )
        for index in range(2)
    )
    wy = (wy_ref[0], wy_ref[1])

    def swept_rows(group):
        reals, imags = [], []
        for one in range(per_device):
            pr, pi = pupil_ref[group, 2 * one], pupil_ref[group, 2 * one + 1]
            reals.append(pr * spec_real - pi * spec_imag)
            imags.append(pi * spec_real + pr * spec_imag)
        amps = jnp.concatenate(
            [jnp.concatenate(reals, axis=1), jnp.concatenate(imags, axis=1)], axis=0
        )
        return dot_pair(wxt, pair(amps)) * field_scale

    weights = [
        jnp.concatenate([meta_ref[group, one : one + 1, :]] * 2, axis=1)
        for group in range(2)
        for one in range(per_device)
    ]

    def light_of(swept, block):
        rows = []
        for group in range(2):
            tops = swept[group][block * local_x : (block + 1) * local_x]
            ends = swept[group][(2 + block) * local_x : (3 + block) * local_x]
            for one in range(per_device):
                cols = slice(one * freqs, (one + 1) * freqs)
                rows.append(jnp.concatenate([tops[:, cols], ends[:, cols]], axis=1))
        field = dot_pair(pair(jnp.concatenate(rows, axis=0)), wy)
        fbuf[block] = field
        squares = field[:, :pixels] * field[:, :pixels] + field[:, pixels:] * field[:, pixels:]
        total = weights[0] * squares[:local_x]
        for at in range(1, 2 * per_device):
            total = total + weights[at] * squares[at * local_x : (at + 1) * local_x]
        return total

    for one in range(per_device):
        make_pupil(1, one, row)
    swept = [swept_rows(group) for group in range(2)]
    lights = [None, None]
    @pl.when(side == 0)
    def _():
        pl.semaphore_wait(token_sem, 1)

    for block in (1, 0):
        lights[block] = light_of(swept, block)
        part_send[block] = lights[block]
        send(
            part_send.at[block],
            part_recv.at[1 - block],
            part_ss.at[block],
            part_rs.at[1 - block],
            src_at=mate_src,
        )
    to(goal_ref.at[0], goals_ref, goal_ss, goal_rs, src_at=mate_src).wait_recv()

    terms = [jnp.zeros((1, pixels), jnp.float32)] * (2 * per_device)
    spread = []
    for block in (0, 1):
        to(
            part_send.at[1 - block],
            part_recv.at[block],
            part_ss.at[1 - block],
            part_rs.at[block],
            src_at=mate_src,
        ).wait_recv()
        intensity = lights[block] + part_recv[block]
        goal = goal_ref[0] if block == 0 else goals_ref[...]
        resist = 1.0 / (1.0 + jnp.exp(-STEEPNESS * (intensity - THRESHOLD)))
        cotangent = LOSS_SCALE * (resist - goal) * STEEPNESS * resist * (1.0 - resist)
        backs = []
        for at in range(2 * per_device):
            field = fbuf[block, at * local_x : (at + 1) * local_x]
            real, imag = field[:, :pixels], field[:, pixels:]
            lit_real, lit_imag = cotangent * real, cotangent * imag
            scale = 2.0 * weights[at]
            backs.append(jnp.concatenate([scale * lit_real, scale * lit_imag], axis=1))
            terms[at] = terms[at] + jnp.sum(
                lit_real * real + lit_imag * imag, axis=0, keepdims=True
            )
        adjoint = dot_pair(pair(jnp.concatenate(backs, axis=0)), wy, 1)
        for at in range(2 * per_device):
            rows = slice(at * local_x, (at + 1) * local_x)
            cols = slice(at * freqs, (at + 1) * freqs)
            ubuf[0, :, cols] = adjoint[rows, :freqs]
            ubuf[1, :, cols] = adjoint[rows, freqs:]
        high, low = pair(ubuf[...].reshape(2 * local_x, 2 * per_device * freqs))
        spread.append(
            jnp.dot(
                wx_ref[block],
                jnp.concatenate([high, low, high], axis=0),
                preferred_element_type=jnp.float32,
            )
        )

    blank = jnp.zeros((1, freqs), jnp.float32)
    for group in range(2):
        tsend[group] = jnp.concatenate(
            [blank]
            + [
                terms[group * per_device + one][:, :freqs]
                + terms[group * per_device + one][:, freqs:]
                for one in range(per_device)
            ]
            + [blank] * (7 - per_device),
            axis=0,
        )
    term_copy = send(tsend, trecv, core_ss.at[src_count], core_rs.at[src_count])

    swept = (spread[0] + spread[1]) * field_scale
    grad_real = jnp.zeros((freqs, freqs), jnp.float32)
    grad_imag = grad_real
    for at in range(2 * per_device):
        group, one = at // per_device, at % per_device
        pr, pi = pupil_ref[group, 2 * one], pupil_ref[group, 2 * one + 1]
        cols = slice(at * freqs, (at + 1) * freqs)
        real, imag = swept[:freqs, cols], swept[freqs:, cols]
        grad_real = grad_real + pr * real + pi * imag
        grad_imag = grad_imag + pr * imag - pi * real

    lane = lax.broadcasted_iota(jnp.int32, (freqs, freqs), 1)
    turn_real = pltpu.roll(grad_real, half, axis=1)
    turn_imag = pltpu.roll(grad_imag, half, axis=1)
    sum_real = grad_real + jnp.where(lane == 0, 0.0, turn_real)
    sum_imag = grad_imag + jnp.where(lane == 0, 0.0, turn_imag)
    gap_real = jnp.where(lane == half, 0.0, turn_real) - grad_real
    gap_imag = jnp.where(lane == half, 0.0, turn_imag) - grad_imag
    upper = jnp.where(lane < half, sum_real, -gap_imag)
    lower = jnp.where(lane < half, sum_imag, gap_real)
    grads = pair(
        jnp.concatenate(
            [
                jnp.concatenate([upper, grad_real], axis=1),
                jnp.concatenate([lower, grad_imag], axis=1),
            ],
            axis=0,
        )
    )

    def rows_of(far_row, own_row):
        slots = [peer * 2 + far_row for peer in far_first] + [src * 2 + own_row]
        waves = tuple(
            jnp.concatenate([wb_ref[index, slot, 0] for slot in slots], axis=0)
            for index in range(2)
        )
        return dot_pair(waves, grads)

    theirs = rows_of(row, other_row)
    for index in range(src_count):
        csend[index] = theirs[index * local_x : (index + 1) * local_x]
        send(csend.at[index], crecv.at[index], core_ss.at[index], core_rs.at[index])
    mine = rows_of(other_row, row)
    strips = jnp.concatenate(
        [
            jnp.concatenate(
                [
                    blocks_of[
                        index * local_x + one * depth : index * local_x + (one + 1) * depth
                    ]
                    for one in range(fold)
                ],
                axis=1,
            )
            for blocks_of in (theirs, mine)
            for index in range(src_count)
        ],
        axis=0,
    )
    strips = dot_pair(pair(strips), (we_ref[0], we_ref[1]))
    for side, near_row, far_row in ((0, other_row, row), (1, row, other_row)):
        for index, peer in enumerate(far_first + [src]):
            at = side * src_count + index
            hsend[at, :depth] = strips[at * depth : (at + 1) * depth]
            tall = depth if index < last - 1 else depth + 8
            if index >= last - 1:
                hsend[at, depth:] = tsend[last - index]
            send(
                hsend.at[at, :tall],
                hrecv.at[own_slot, :tall],
                halo_ss.at[at],
                halo_rs.at[own_slot],
                src_at=peer,
                tile_at=other_tile,
                row_at=far_row if index < last else near_row,
            )
    term_copy.wait_recv()
    own_terms = tsend[0] + trecv[0]
    pool_terms = tsend[1] + trecv[1]
    for index in range(src_count):
        gsend[index, local_x:] = pool_terms if index < last else own_terms
    for index, peer in enumerate(far_first + [src]):
        to(csend.at[index], crecv.at[index], core_ss.at[index], core_rs.at[index]).wait_recv()
        both = mine[index * local_x : (index + 1) * local_x] + crecv[index]
        gsend[index, :local_x] = both[:, :freqs]
        gsend[index, local_x : local_x + 1, :local_x] = both[:, freqs:].T[half : half + 1]
        if index < last:
            tall = local_x + (1 if index < last - 1 else 8)
            send(
                gsend.at[index, :tall],
                grecv.at[src, :tall],
                grad_ss.at[index],
                grad_rs.at[src],
                src_at=peer,
            )

    total = gsend[last]
    tail = total[local_x : local_x + 1]
    total = total[:local_x]
    for index, peer in enumerate(near_first):
        tall = local_x + (1 if index > 0 else 8)
        to(
            gsend.at[0, :tall],
            grecv.at[peer, :tall],
            grad_ss.at[0],
            grad_rs.at[peer],
            src_at=peer,
        ).wait_recv()
        total = total + grecv[peer, :local_x]
        tail = tail + grecv[peer, local_x : local_x + 1]
    tail = jnp.concatenate([tail, jnp.zeros((7, freqs), jnp.float32)], axis=0)
    grad_block = dot_pair(pair(total), wm, 1)
    grad_block = grad_block + tail.T[:local_x, :1] * quarter_wave[:1]
    low, high = grad_block[:, :freqs], grad_block[:, pixels - freqs :]

    packed = jnp.zeros((depth, freqs), jnp.float32)
    for index, peer in enumerate([src] + near_first):
        tall = depth if index > 1 else depth + 8
        for core in range(2):
            slot = peer * 2 + core
            to(
                hsend.at[0, :tall],
                hrecv.at[slot, :tall],
                halo_ss.at[0],
                halo_rs.at[slot],
                src_at=peer,
                tile_at=other_tile,
                row_at=core,
            ).wait_recv()
            packed = packed + hrecv[slot, :depth]
    strip = jnp.concatenate(
        [packed]
        + [pltpu.roll(packed, freqs - one * OV, axis=1) for one in range(1, fold)],
        axis=0,
    )
    from_below = jnp.where((lanes < OV) & (tile == 1), strip, 0.0)
    from_above = jnp.where(
        (lanes >= freqs - OV) & (tile == 0), pltpu.roll(strip, freqs - OV, axis=1), 0.0
    )
    out_ref[0, :, :freqs] = low + from_below
    out_ref[0, :, pixels - freqs :] = high + from_above
    terms = own_terms + grecv[pool_src, local_x:]
    for slot in (src * 2, src * 2 + 1, pool_src * 2, pool_src * 2 + 1):
        terms = terms + hrecv[slot, depth:]
    terms = terms / (sources * pixels * tile_count)
    terms_ref[...] = terms
    for copy in copies:
        copy.wait_send()


def finish_kernel(grads_ref, terms_ref, out_ref, sums_ref, held_ref, sems):
    copy = pltpu.make_async_copy(grads_ref, out_ref, sems.at[0])
    copy.start()
    for one in range(held_ref.shape[0]):
        held_ref[one] = jnp.sum(terms_ref[one + 1 : one + 2, :])
    other = pltpu.make_async_copy(held_ref, sums_ref, sems.at[1])
    other.start()
    copy.wait()
    other.wait()


def finish(grads, terms, shape):
    in_vmem = pl.BlockSpec(memory_space=pltpu.VMEM)
    in_hbm = pl.BlockSpec(memory_space=pltpu.HBM)
    return pl.pallas_call(
        finish_kernel,
        out_shape=(
            jax.ShapeDtypeStruct(grads.shape, grads.dtype),
            jax.ShapeDtypeStruct(shape, terms.dtype),
        ),
        in_specs=[in_vmem, in_vmem],
        out_specs=(in_hbm, in_hbm),
        scratch_shapes=[pltpu.SMEM(shape, terms.dtype), pltpu.SemaphoreType.DMA((2,))],
    )(*(pltpu.with_memory_space_constraint(one, pltpu.VMEM) for one in (grads, terms)))


def shards(mask_windows, target_windows, pupil_bands, pupil_phase, source_weight):
    src_count = lax.axis_size("src")
    tile_count = lax.axis_size("tile")
    row_count = lax.axis_size("row")
    local_x, pixels = mask_windows.shape[1:]
    per_device, freqs = pupil_phase.shape[:2]
    blocks = src_count * row_count
    fits = row_count == 2 and tile_count == 2 and src_count == 4 and 2 * per_device <= 8
    fits = fits and freqs == 128 and pixels == 2 * freqs and local_x == OV
    if not fits or local_x * blocks != pixels or OV * 4 != freqs:
        return shards_plain(
            mask_windows, target_windows, pupil_bands, pupil_phase, source_weight
        )
    half, fold = freqs // 2, freqs // OV
    tables = wave_constants(pixels, freqs, blocks, src_count, local_x, fold)
    bands = jnp.transpose(pupil_bands, (0, 2, 1))
    phases = pupil_phase.reshape(per_device, 2, half, freqs)
    in_vmem = pl.BlockSpec(memory_space=pltpu.VMEM)
    in_smem = pl.BlockSpec(memory_space=pltpu.SMEM)
    f32 = jnp.float32
    block = (local_x, pixels)
    dma = pltpu.SemaphoreType.DMA
    like = [pltpu.VMEM(one.shape, one.dtype) for one in tables]
    like[4] = pltpu.VMEM(tables[4].shape[1:], tables[4].dtype)
    like[5] = pltpu.VMEM(tables[5].shape[1:], tables[5].dtype)
    four = dma((src_count,))
    grads, terms = pl.pallas_call(
        functools.partial(kernel, src_count, tile_count),
        out_shape=(
            pltpu.VMEM(mask_windows.shape, f32),
            pltpu.VMEM((8, freqs), f32),
        ),
        in_specs=[pl.BlockSpec(memory_space=pltpu.HBM)] * 12,
        out_specs=(in_vmem, in_vmem),
        scratch_shapes=like
        + [
            pltpu.VMEM(mask_windows.shape, f32),
            pltpu.VMEM(target_windows.shape, f32),
            pltpu.VMEM(bands.shape, bands.dtype),
            pltpu.VMEM((2,) + phases.shape, f32),
            pltpu.SMEM(source_weight.shape, f32),
            dma((12,)),
            pltpu.VMEM((blocks, local_x + 8, freqs), f32),
            pltpu.VMEM((2, 2 * per_device, freqs, freqs), f32),
            pltpu.VMEM((2, 2 * per_device * local_x, 2 * pixels), f32),
            pltpu.VMEM((2, local_x, 2 * per_device * freqs), f32),
            pltpu.VMEM((2, 16, freqs), f32),
            pltpu.VMEM(block, f32),
            pltpu.VMEM((2,) + block, f32),
            pltpu.VMEM((2,) + block, f32),
            pltpu.VMEM((2, 8, freqs), f32),
            pltpu.VMEM((2, 8, freqs), f32),
            pltpu.VMEM((src_count,) + block, f32),
            pltpu.VMEM((src_count,) + block, f32),
            pltpu.VMEM((src_count, local_x + 8, freqs), f32),
            pltpu.VMEM((src_count, local_x + 8, freqs), f32),
            pltpu.VMEM((blocks, 16, freqs), f32),
            pltpu.VMEM((blocks, 16, freqs), f32),
        ]
        + [four] * 4
        + [dma(())] * 2
        + [dma((per_device,))] * 4
        + [dma(())] * 2
        + [dma((2,))] * 2
        + [dma((src_count + 1,))] * 2
        + [four] * 2
        + [dma((blocks,))] * 2
        + [pltpu.SemaphoreType.REGULAR] * 2
        + [pltpu.VMEM((freqs, 8), f32)],
        compiler_params=pltpu.CompilerParams(
            collective_id=0, has_side_effects=True, vmem_limit_bytes=63 * 1024 * 1024
        ),
    )(*tables, mask_windows, target_windows, bands, phases, source_weight)
    return finish(grads, terms, source_weight.shape)


def solution(mesh):
    return jax.shard_map(
        shards,
        mesh=mesh,
        in_specs=(
            P(("parts", "tile"), ("src", "row"), None),
            P(("parts", "tile"), ("src", "row"), None),
            P(("parts", "src"), None, None),
            P(("parts", "src"), None, None),
            P(("parts", "src")),
        ),
        out_specs=(P(("parts", "tile"), ("src", "row"), None), P(("parts", "src"))),
        check_vma=False,
    )
```

```python
import functools
import math

import jax
import jax.numpy as jnp
import numpy as np
from jax import lax
from jax.experimental import pallas as pl
from jax.experimental.pallas import tpu as pltpu
from jax.sharding import PartitionSpec as P

M = 256
K = 128
OV = 32


STEEPNESS = 20.0
THRESHOLD = 0.15
LOSS_SCALE = 32.0


def with_halo(block, sides, width):
    for axis, dim in sides:
        count = lax.axis_size(axis)
        forward = [(i, i + 1) for i in range(count - 1)]
        backward = [(target, source) for source, target in forward]
        low = lax.ppermute(
            lax.slice_in_dim(block, block.shape[dim] - width, None, axis=dim), axis, forward
        )
        high = lax.ppermute(lax.slice_in_dim(block, 0, width, axis=dim), axis, backward)
        block = jnp.concatenate([low, block, high], axis=dim)
    return block


def matmul(left_op, right_op):
    return lax.dot_general(
        left_op,
        right_op,
        (((1,), (0,)), ((), ())),
        precision=lax.Precision.HIGHEST,
        preferred_element_type=jnp.float32,
    )


def matmul_tn(left_op, right_op):
    return lax.dot_general(
        left_op,
        right_op,
        (((0,), (0,)), ((), ())),
        precision=lax.Precision.HIGHEST,
        preferred_element_type=jnp.float32,
    )


def matmul_nt(left_op, right_op):
    return lax.dot_general(
        left_op,
        right_op,
        (((1,), (1,)), ((), ())),
        precision=lax.Precision.HIGHEST,
        preferred_element_type=jnp.float32,
    )


def wave_tables(positions):
    freq_index = jnp.arange(K, dtype=jnp.int32) - K // 2
    phase_index = freq_index[:, None] * positions[None, :] % M
    angles = 2.0 * math.pi / M * phase_index.astype(jnp.float32)
    return (jnp.cos(angles), jnp.sin(angles))


def shards_plain(mask_windows, target_windows, pupil_bands, pupil_phase, source_weight):
    src_count = lax.axis_size("src")
    tile_count = lax.axis_size("tile")
    row_count = lax.axis_size("row")
    local_x = mask_windows.shape[1]
    per_device = pupil_phase.shape[0]
    sources = per_device * src_count
    field_scale = 1.0 / (M * K)
    src_id = lax.axis_index("src")
    row_id = lax.axis_index("row")
    x_start = (src_id * row_count + row_id) * local_x
    block_starts = (jnp.arange(src_count, dtype=jnp.int32) * row_count + row_id) * local_x
    row_set = (block_starts[:, None] + jnp.arange(local_x, dtype=jnp.int32)[None, :]).reshape(
        src_count * local_x
    )
    cos_all, sin_all = wave_tables(jnp.arange(M, dtype=jnp.int32))
    cos_set, sin_set = wave_tables(row_set)
    cos_own, sin_own = wave_tables(x_start + jnp.arange(local_x, dtype=jnp.int32))
    window = mask_windows[0]
    goal_block = target_windows[0]
    zero_spec = jnp.zeros((K, K), jnp.float32)
    shard_rows = lax.all_gather(window, ("src", "row"), axis=0, tiled=True)
    part_real = matmul_nt(shard_rows, cos_all)
    part_imag = -matmul_nt(shard_rows, sin_all)
    spec_real = matmul(cos_all, part_real) + matmul(sin_all, part_imag)
    spec_imag = matmul(cos_all, part_imag) - matmul(sin_all, part_real)
    freq_cols = jnp.arange(K, dtype=jnp.int32)
    inside = (freq_cols[None, None, :] >= pupil_bands[:, :, 0:1]) & (
        freq_cols[None, None, :] < pupil_bands[:, :, 1:2]
    )
    passing = inside.astype(jnp.float32)
    pupil_real = passing * jnp.cos(pupil_phase)
    pupil_imag = passing * jnp.sin(pupil_phase)
    amp_real = (pupil_real * spec_real - pupil_imag * spec_imag).reshape(per_device * K, K)
    amp_imag = (pupil_imag * spec_real + pupil_real * spec_imag).reshape(per_device * K, K)
    half_real = (matmul(amp_real, cos_all) - matmul(amp_imag, sin_all)).reshape(per_device, K, M)
    half_imag = (matmul(amp_real, sin_all) + matmul(amp_imag, cos_all)).reshape(per_device, K, M)
    weights = source_weight / sources

    def fields(pair_in):
        one_real, one_imag = pair_in
        field_real = field_scale * (matmul_tn(cos_set, one_real) - matmul_tn(sin_set, one_imag))
        field_imag = field_scale * (matmul_tn(cos_set, one_imag) + matmul_tn(sin_set, one_real))
        return (field_real, field_imag)

    stack_real, stack_imag = lax.map(fields, (half_real, half_imag))
    part_real = stack_real
    part_imag = stack_imag
    intensity = lax.psum_scatter(
        jnp.sum(weights[:, None, None] * (part_real * part_real + part_imag * part_imag), axis=0),
        "src",
        scatter_dimension=0,
        tiled=True,
    )
    resist = jax.nn.sigmoid(STEEPNESS * (intensity - THRESHOLD))
    cotangent = LOSS_SCALE * (resist - goal_block) * STEEPNESS * resist * (1.0 - resist)
    cotangent_all = lax.all_gather(cotangent, "src", axis=0, tiled=True)
    source_ids = jnp.arange(per_device, dtype=jnp.int32)

    def add_back(source_id, totals):
        grad_real, grad_imag, source_terms = totals
        field_real = stack_real[source_id]
        field_imag = stack_imag[source_id]
        back_scale = 2.0 * weights[source_id] * cotangent_all
        back_real = back_scale * field_real
        back_imag = back_scale * field_imag
        adj_real = matmul(cos_set, back_real) + matmul(sin_set, back_imag)
        adj_imag = matmul(cos_set, back_imag) - matmul(sin_set, back_real)
        amp_grad_real = field_scale * (matmul_nt(adj_real, cos_all) + matmul_nt(adj_imag, sin_all))
        amp_grad_imag = field_scale * (matmul_nt(adj_imag, cos_all) - matmul_nt(adj_real, sin_all))
        pass_real = pupil_real[source_id]
        pass_imag = pupil_imag[source_id]
        grad_real = grad_real + pass_real * amp_grad_real + pass_imag * amp_grad_imag
        grad_imag = grad_imag + pass_real * amp_grad_imag - pass_imag * amp_grad_real
        term_value = jnp.sum(cotangent_all * (field_real * field_real + field_imag * field_imag))
        source_terms = source_terms + jnp.where(source_ids == source_id, term_value, 0.0)
        return (grad_real, grad_imag, source_terms)

    grad_real, grad_imag, source_terms = lax.fori_loop(
        0, per_device, add_back, (zero_spec, zero_spec, jnp.zeros((per_device,), jnp.float32))
    )
    grad_real, grad_imag = lax.psum((grad_real, grad_imag), ("src", "row"))
    source_sum = lax.psum(source_terms, ("tile", "row"))
    source_grad = source_sum / (sources * M * tile_count)
    q_one = matmul(grad_real, cos_all) - matmul(grad_imag, sin_all)
    q_two = matmul(grad_real, sin_all) + matmul(grad_imag, cos_all)
    grad_block = matmul_tn(cos_own, q_one) - matmul_tn(sin_own, q_two)
    padded = with_halo(grad_block, (("tile", 1),), OV)
    from_below = padded[:, :OV]
    from_above = padded[:, M + OV :]
    middle = jnp.zeros((local_x, M - 2 * OV), jnp.float32)
    grad_block = grad_block + jnp.concatenate([from_below, middle, from_above], axis=1)
    return (grad_block[None], source_grad)


MESH = pl.DeviceIdType.MESH


def pair(values):
    high = values.astype(jnp.bfloat16)
    return high, (values - high.astype(jnp.float32)).astype(jnp.bfloat16)


def dot_pair(left_op, right_op, contract_right=0):
    dims = (((1,), (contract_right,)), ((), ()))

    def one(a, b):
        return lax.dot_general(a, b, dims, preferred_element_type=jnp.float32)

    (left_high, left_low), (right_high, right_low) = left_op, right_op
    both = one(jnp.concatenate([left_high, left_low], axis=0), right_high)
    count = left_high.shape[0]
    return both[:count] + (both[count:] + one(left_high, right_low))


def frequency_order(freqs):
    half = freqs // 2
    return np.concatenate([np.arange(half), [-half], -np.arange(1, half)])


def wave_constants(pixels, freqs, blocks, src_count, local_x, fold):
    half = freqs // 2
    spots = np.arange(pixels)

    def waves(index):
        angles = 2.0 * np.pi / pixels * (np.outer(index, spots) % pixels)
        return np.cos(angles), np.sin(angles)

    cos_x, sin_x = waves(np.arange(freqs) - half)
    order = frequency_order(freqs)
    cos_y, sin_y = waves(order)
    spectrum = np.concatenate([cos_x, -sin_x], axis=0)
    wave_y = np.block([[cos_y, sin_y], [-sin_y, cos_y]])
    real_rows = np.concatenate([cos_x.T, -sin_x.T], axis=1)
    imag_rows = np.concatenate([sin_x.T, cos_x.T], axis=1)
    wave_rows = np.stack(
        [one.reshape(blocks, local_x, 2 * freqs) for one in (real_rows, imag_rows)], axis=1
    )
    sets = []
    for own in range(blocks):
        src, row = own // 2, own % 2
        mate = (src + src_count // 2) % src_count * 2 + 1 - row
        rows = np.concatenate([np.arange(local_x) + one * local_x for one in (own, mate)])
        c, s = cos_x[:, rows], sin_x[:, rows]
        pieces = []
        for one in range(2):
            cols = slice(one * local_x, (one + 1) * local_x)
            high, low = split_constant(np.block([[c[:, cols], s[:, cols]], [-s[:, cols], c[:, cols]]]))
            pieces.append(np.concatenate([high, high, low], axis=1))
        sets.append(np.stack(pieces))
    packed = np.concatenate([cos_y[:half], -sin_y[half:]], axis=0).T
    edges = []
    for start in (pixels - OV, 0):
        table = np.zeros((fold, 2 * freqs, fold, OV))
        for group in range(fold):
            table[group, :freqs, group] = packed[start : start + OV].T
            table[group, freqs + half, group] = cos_y[half, start : start + OV]
        edges.append(table.reshape(fold * 2 * freqs, freqs))
    move = np.zeros((freqs, freqs))
    move[order + half, np.arange(freqs)] = 1.0
    return (
        split_constant(packed),
        split_constant(spectrum),
        split_constant(wave_y),
        split_constant(wave_rows),
        np.stack(sets),
        split_constant(np.stack(edges), 1),
        move.astype(jnp.bfloat16),
    )


def split_constant(values, axis=0):
    values = values.astype(np.float32)
    high = values.astype(jnp.bfloat16)
    low = (values - high.astype(np.float32)).astype(jnp.bfloat16)
    return np.stack([high, low], axis=axis)


def sine_cosine(phase):
    quarter = 0.25 * phase
    square = quarter * quarter
    sine = 1.0 / 362880.0
    for term in (-1.0 / 5040.0, 1.0 / 120.0, -1.0 / 6.0, 1.0):
        sine = sine * square + term
    sine = sine * quarter
    fall = -1.0 / 40320.0
    for term in (1.0 / 720.0, -1.0 / 24.0, 0.5):
        fall = fall * square + term
    cosine = 1.0 - fall * square
    twice = 2.0 * sine
    sine, cosine = twice * cosine, 1.0 - twice * sine
    twice = 2.0 * sine
    return twice * cosine, 1.0 - twice * sine


def dot_exact(left_op, right_op, dims=(((1,), (0,)), ((), ()))):
    high, low = pair(left_op)

    def one(a):
        return lax.dot_general(a, right_op, dims, preferred_element_type=jnp.float32)

    return one(high) + one(low)


def kernel(
    src_count,
    tile_count,
    wm_hbm,
    wf_hbm,
    wy_hbm,
    wb_hbm,
    wx_hbm,
    we_hbm,
    move_hbm,
    mask_hbm,
    goal_hbm,
    band_hbm,
    phase_hbm,
    weight_hbm,
    out_ref,
    terms_ref,
    wm_ref,
    wf_ref,
    wy_ref,
    wb_ref,
    wx_ref,
    we_ref,
    move_ref,
    mask_ref,
    goal_ref,
    band_ref,
    phase_ref,
    weight_ref,
    load_sems,
    mbuf,
    pupil_ref,
    fbuf,
    ubuf,
    meta_ref,
    goals_ref,
    part_send,
    part_recv,
    tsend,
    trecv,
    csend,
    crecv,
    gsend,
    grecv,
    hsend,
    hrecv,
    mask_ss,
    mask_rs,
    fwd_ss,
    fwd_rs,
    meta_ss,
    meta_rs,
    phase_ss,
    phase_rs,
    pfwd_ss,
    pfwd_rs,
    goal_ss,
    goal_rs,
    part_ss,
    part_rs,
    core_ss,
    core_rs,
    grad_ss,
    grad_rs,
    halo_ss,
    halo_rs,
    ready_sem,
    token_sem,
    band_rows,
):
    part = lax.axis_index("parts")
    src = lax.axis_index("src")
    tile = lax.axis_index("tile")
    row = lax.axis_index("row")
    local_x, pixels = mask_ref.shape[1:]
    per_device, half, freqs = phase_ref.shape[1], phase_ref.shape[3], phase_ref.shape[4]
    sources = per_device * src_count
    field_scale = 1.0 / (pixels * freqs)
    fold = freqs // OV
    depth = local_x // fold
    other_row = 1 - row
    other_tile = 1 - tile
    last = src_count - 1
    own_slot = src * 2 + row
    mate_src = lax.rem(src + src_count // 2, src_count)
    mate_slot = mate_src * 2 + other_row
    pool_src = src + 1 - 2 * lax.rem(src, 2)

    side = lax.div(src, 2)
    far_first = [last * (1 - side), 2 - side, pool_src]
    near_first = far_first[::-1]

    def to(src_ref, dst_ref, ss, rs, src_at=src, tile_at=tile, row_at=other_row):
        return pltpu.make_async_remote_copy(
            src_ref=src_ref,
            dst_ref=dst_ref,
            send_sem=ss,
            recv_sem=rs,
            device_id=(part, src_at, tile_at, row_at),
            device_id_type=MESH,
        )

    def tell(semaphore, src_at, row_at, tile_at=tile):
        pl.semaphore_signal(
            semaphore, inc=1, device_id=(part, src_at, tile_at, row_at), device_id_type=MESH
        )

    barrier = pltpu.get_barrier_semaphore()

    @pl.when(side == 0)
    def _():
        for peer in (last, last - 1):
            tell(barrier, peer, other_row)
        tell(barrier, pool_src, other_row)
        tell(barrier, src, other_row, other_tile)
        tell(barrier, src, other_row)

    @pl.when(src == last - 1)
    def _():
        for core in (other_row, row):
            tell(barrier, last, core)

    loads = {}
    for index, (name, source, target) in enumerate(
        [
            ("mask", mask_hbm, mask_ref),
            ("wm", wm_hbm, wm_ref),
            ("weight", weight_hbm, weight_ref),
            ("band", band_hbm, band_ref),
            ("phase", phase_hbm, phase_ref.at[0]),
            ("goal", goal_hbm, goal_ref),
            ("move", move_hbm, move_ref),
            ("wf", wf_hbm, wf_ref),
            ("wb", wb_hbm, wb_ref),
            ("wy", wy_hbm, wy_ref),
            ("wx", wx_hbm.at[own_slot], wx_ref),
            ("we", we_hbm.at[tile], we_ref),
        ]
    ):
        loads[name] = pltpu.make_async_copy(source, target, load_sems.at[index])
        loads[name].start()

    pl.semaphore_wait(barrier, 3 * (1 - side) + 2 * side * (src - 1))

    @pl.when(side == 1)
    def _():
        for peer in (0, 1):
            tell(ready_sem, peer, other_row)

    @pl.when(src == last)
    def _():
        for core in (other_row, row):
            tell(ready_sem, last - 1, core)

    lanes = lax.broadcasted_iota(jnp.int32, (local_x, freqs), 1)
    spots = lax.broadcasted_iota(jnp.int32, (8, pixels), 1)
    turn = spots - 4 * lax.div(spots, 4)
    quarter_wave = jnp.where(turn == 0, 1.0, jnp.where(turn == 2, -1.0, 0.0))
    first_row = lax.broadcasted_iota(jnp.int32, (8, pixels), 0) == 0

    loads["mask"].wait()
    loads["wm"].wait()
    wm = (wm_ref[0], wm_ref[1])
    mask = mask_ref[0]
    mbuf[own_slot, :local_x] = dot_pair(pair(mask), wm)
    quarter_row = jnp.where(first_row, quarter_wave, 0.0).astype(jnp.bfloat16)
    padded = jnp.concatenate([mask, jnp.zeros((freqs - local_x, pixels), jnp.float32)], axis=0)
    high, low = pair(padded)
    nt = (((1,), (1,)), ((), ()))
    mbuf[own_slot, local_x:] = lax.dot_general(
        quarter_row, high, nt, preferred_element_type=jnp.float32
    ) + lax.dot_general(quarter_row, low, nt, preferred_element_type=jnp.float32)
    loads["weight"].wait()
    loads["band"].wait()
    for one in range(per_device):
        meta_ref[0, one : one + 1, :] = jnp.full((1, freqs), weight_ref[one] / sources)
    meta_ref[0, 8:, :] = jnp.concatenate(
        [band_ref[one] for one in range(per_device)]
        + [jnp.zeros((8 - 2 * per_device, freqs), jnp.int32)],
        axis=0,
    ).astype(jnp.float32)
    loads["phase"].wait()
    loads["goal"].wait()
    copies = []

    def send(*args, **keys):
        copy = to(*args, **keys)
        copy.start()
        copies.append(copy)
        return copy

    own_block = mbuf.at[own_slot, : local_x + 1]
    far_copies = [
        to(own_block, own_block, mask_ss.at[peer], mask_rs.at[src], src_at=peer)
        for peer in far_first[:-1]
    ]
    pool_copies = [
        to(own_block, own_block, mask_ss.at[pool_src], mask_rs.at[src], src_at=pool_src),
        to(meta_ref.at[0], meta_ref.at[1], meta_ss, meta_rs, src_at=pool_src),
    ]
    for one in range(per_device):
        pool_copies.append(
            to(
                phase_ref.at[0, one, row],
                phase_ref.at[1, one, row],
                phase_ss.at[one],
                phase_rs.at[one],
                src_at=pool_src,
            )
        )
    goal_copy = to(goal_ref.at[0], goals_ref, goal_ss, goal_rs, src_at=mate_src)
    copies += far_copies + pool_copies + [goal_copy]

    def start(group):
        for copy in group:
            copy.start()

    @pl.when(side == 1)
    def _():
        start(far_copies)

    @pl.when(src != last - 1)
    def _():
        start(pool_copies)

    loads["move"].wait()
    move = move_ref[...]
    columns = lax.broadcasted_iota(jnp.int32, (half, freqs), 1).astype(jnp.float32)

    def read_bands(group):
        band_rows[...] = meta_ref[group, 8:, :].T

    def make_pupil(group, one, part_of):
        rows = pl.ds(pl.multiple_of(part_of * half, half), half)
        lower = band_rows[rows, 2 * one : 2 * one + 1]
        upper = band_rows[rows, 2 * one + 1 : 2 * one + 2]
        passing = (columns >= lower) & (columns < upper)
        sine, cosine = sine_cosine(phase_ref[group, one, part_of])
        moved = dot_exact(
            jnp.concatenate(
                [jnp.where(passing, cosine, 0.0), jnp.where(passing, sine, 0.0)], axis=0
            ),
            move,
        )
        pupil_ref[group, 2 * one, rows] = moved[:half]
        pupil_ref[group, 2 * one + 1, rows] = moved[half:]

    read_bands(0)
    for one in range(per_device):
        for part_of in range(2):
            make_pupil(0, one, part_of)

    @pl.when(src != last)
    def _():
        pl.semaphore_wait(ready_sem, 2)

    @pl.when(side == 0)
    def _():
        start(far_copies)

    @pl.when(src == last - 1)
    def _():
        start(pool_copies)

    @pl.when(side == 1)
    def _():
        goal_copy.start()

    for name in ("wf", "wb", "wy", "wx", "we"):
        loads[name].wait()

    for index, peer in enumerate(near_first):
        block = mbuf.at[peer * 2 + other_row, : local_x + 1]
        to(block, block, mask_ss.at[peer], mask_rs.at[peer], src_at=peer).wait_recv()
        send(block, block, fwd_ss.at[peer], fwd_rs.at[peer])
        if index == 0:
            send(own_block, own_block, fwd_ss.at[src], fwd_rs.at[src])
        if index == last - 1:
            pl.when(side == 0)(goal_copy.start)
    for one in range(per_device):
        half_block = phase_ref.at[1, one, other_row]
        to(
            half_block, half_block, phase_ss.at[one], phase_rs.at[one], src_at=pool_src
        ).wait_recv()
        send(half_block, half_block, pfwd_ss.at[one], pfwd_rs.at[one])
    to(meta_ref.at[0], meta_ref.at[1], meta_ss, meta_rs, src_at=pool_src).wait_recv()
    read_bands(1)
    for one in range(per_device):
        make_pupil(1, one, other_row)
    for peer in near_first:
        block = mbuf.at[peer * 2 + row, : local_x + 1]
        to(block, block, fwd_ss.at[peer], fwd_rs.at[peer]).wait_recv()
    block = mbuf.at[src * 2 + other_row, : local_x + 1]
    to(block, block, fwd_ss.at[src], fwd_rs.at[src]).wait_recv()

    @pl.when(side == 0)
    def _():
        tell(token_sem, src, other_row, other_tile)

    for one in range(per_device):
        half_block = phase_ref.at[1, one, row]
        to(half_block, half_block, pfwd_ss.at[one], pfwd_rs.at[one]).wait_recv()
    blocks = pixels // local_x
    extra = jnp.concatenate([mbuf[one, local_x : local_x + 1] for one in range(blocks)], axis=0).T
    rows = []
    for one in range(blocks):
        straight = mbuf[one, :local_x]
        turned = pltpu.roll(straight, half, axis=1)
        real = jnp.where(lanes < half, straight, turned)
        real = jnp.where(lanes == half, extra[:local_x, one : one + 1], real)
        imag = jnp.where(lanes < half, -turned, straight)
        imag = jnp.where(lanes == 0, 0.0, imag)
        rows.append(jnp.concatenate([real, imag], axis=1))
    spectrum = dot_pair((wf_ref[0], wf_ref[1]), pair(jnp.concatenate(rows, axis=0)))
    spec_real = field_scale * (spectrum[:freqs, :freqs] - spectrum[freqs:, freqs:])
    spec_imag = field_scale * (spectrum[:freqs, freqs:] + spectrum[freqs:, :freqs])

    wxt = tuple(
        jnp.concatenate(
            [wb_ref[index, slot, side] for side in range(2) for slot in (own_slot, mate_slot)],
            axis=0,
        )
        for index in range(2)
    )
    wy = (wy_ref[0], wy_ref[1])

    def swept_rows(group):
        reals, imags = [], []
        for one in range(per_device):
            pr, pi = pupil_ref[group, 2 * one], pupil_ref[group, 2 * one + 1]
            reals.append(pr * spec_real - pi * spec_imag)
            imags.append(pi * spec_real + pr * spec_imag)
        amps = jnp.concatenate(
            [jnp.concatenate(reals, axis=1), jnp.concatenate(imags, axis=1)], axis=0
        )
        return dot_pair(wxt, pair(amps))

    weights = [
        jnp.concatenate([meta_ref[group, one : one + 1, :]] * 2, axis=1)
        for group in range(2)
        for one in range(per_device)
    ]

    def light_of(swept, block):
        rows = []
        for group in range(2):
            tops = swept[group][block * local_x : (block + 1) * local_x]
            ends = swept[group][(2 + block) * local_x : (3 + block) * local_x]
            for one in range(per_device):
                cols = slice(one * freqs, (one + 1) * freqs)
                rows.append(jnp.concatenate([tops[:, cols], ends[:, cols]], axis=1))
        field = dot_pair(pair(jnp.concatenate(rows, axis=0)), wy)
        fbuf[block] = field
        squares = field[:, :pixels] * field[:, :pixels] + field[:, pixels:] * field[:, pixels:]
        total = weights[0] * squares[:local_x]
        for at in range(1, 2 * per_device):
            total = total + weights[at] * squares[at * local_x : (at + 1) * local_x]
        return total

    for one in range(per_device):
        make_pupil(1, one, row)
    swept = [swept_rows(group) for group in range(2)]
    lights = [None, None]
    @pl.when(side == 0)
    def _():
        pl.semaphore_wait(token_sem, 1)

    for block in (1, 0):
        lights[block] = light_of(swept, block)
        part_send[block] = lights[block]
        send(
            part_send.at[block],
            part_recv.at[1 - block],
            part_ss.at[block],
            part_rs.at[1 - block],
            src_at=mate_src,
        )
    to(goal_ref.at[0], goals_ref, goal_ss, goal_rs, src_at=mate_src).wait_recv()

    terms = [jnp.zeros((1, pixels), jnp.float32)] * (2 * per_device)
    grad_real = jnp.zeros((freqs, freqs), jnp.float32)
    grad_imag = grad_real
    for block in (0, 1):
        to(
            part_send.at[1 - block],
            part_recv.at[block],
            part_ss.at[1 - block],
            part_rs.at[block],
            src_at=mate_src,
        ).wait_recv()
        intensity = lights[block] + part_recv[block]
        goal = goal_ref[0] if block == 0 else goals_ref[...]
        resist = 1.0 / (1.0 + jnp.exp(-STEEPNESS * (intensity - THRESHOLD)))
        cotangent = LOSS_SCALE * (resist - goal) * STEEPNESS * resist * (1.0 - resist)
        backs = []
        for at in range(2 * per_device):
            field = fbuf[block, at * local_x : (at + 1) * local_x]
            real, imag = field[:, :pixels], field[:, pixels:]
            lit_real, lit_imag = cotangent * real, cotangent * imag
            scale = 2.0 * field_scale * weights[at]
            backs.append(jnp.concatenate([scale * lit_real, scale * lit_imag], axis=1))
            terms[at] = terms[at] + jnp.sum(
                lit_real * real + lit_imag * imag, axis=0, keepdims=True
            )
        adjoint = dot_pair(pair(jnp.concatenate(backs, axis=0)), wy, 1)
        for at in range(2 * per_device):
            rows = slice(at * local_x, (at + 1) * local_x)
            cols = slice(at * freqs, (at + 1) * freqs)
            ubuf[0, :, cols] = adjoint[rows, :freqs]
            ubuf[1, :, cols] = adjoint[rows, freqs:]
        high, low = pair(ubuf[...].reshape(2 * local_x, 2 * per_device * freqs))
        swept = jnp.dot(
            wx_ref[block],
            jnp.concatenate([high, low, high], axis=0),
            preferred_element_type=jnp.float32,
        )
        for at in range(2 * per_device):
            group, one = at // per_device, at % per_device
            pr, pi = pupil_ref[group, 2 * one], pupil_ref[group, 2 * one + 1]
            cols = slice(at * freqs, (at + 1) * freqs)
            real, imag = swept[:freqs, cols], swept[freqs:, cols]
            grad_real = grad_real + pr * real + pi * imag
            grad_imag = grad_imag + pr * imag - pi * real

    blank = jnp.zeros((1, freqs), jnp.float32)
    for group in range(2):
        tsend[group] = jnp.concatenate(
            [blank]
            + [
                terms[group * per_device + one][:, :freqs]
                + terms[group * per_device + one][:, freqs:]
                for one in range(per_device)
            ]
            + [blank] * (7 - per_device),
            axis=0,
        )
    term_copy = send(tsend, trecv, core_ss.at[src_count], core_rs.at[src_count])

    lane = lax.broadcasted_iota(jnp.int32, (freqs, freqs), 1)
    turn_real = pltpu.roll(grad_real, half, axis=1)
    turn_imag = pltpu.roll(grad_imag, half, axis=1)
    sum_real = grad_real + jnp.where(lane == 0, 0.0, turn_real)
    sum_imag = grad_imag + jnp.where(lane == 0, 0.0, turn_imag)
    gap_real = jnp.where(lane == half, 0.0, turn_real) - grad_real
    gap_imag = jnp.where(lane == half, 0.0, turn_imag) - grad_imag
    upper = jnp.where(lane < half, sum_real, -gap_imag)
    lower = jnp.where(lane < half, sum_imag, gap_real)
    grads = pair(
        jnp.concatenate(
            [
                jnp.concatenate([upper, grad_real], axis=1),
                jnp.concatenate([lower, grad_imag], axis=1),
            ],
            axis=0,
        )
    )

    def rows_of(far_row, own_row):
        slots = [peer * 2 + far_row for peer in far_first] + [src * 2 + own_row]
        waves = tuple(
            jnp.concatenate([wb_ref[index, slot, 0] for slot in slots], axis=0)
            for index in range(2)
        )
        return dot_pair(waves, grads)

    theirs = rows_of(row, other_row)
    for index in range(src_count):
        csend[index] = theirs[index * local_x : (index + 1) * local_x]
        send(csend.at[index], crecv.at[index], core_ss.at[index], core_rs.at[index])
    mine = rows_of(other_row, row)
    strips = jnp.concatenate(
        [
            jnp.concatenate(
                [
                    blocks_of[
                        index * local_x + one * depth : index * local_x + (one + 1) * depth
                    ]
                    for one in range(fold)
                ],
                axis=1,
            )
            for blocks_of in (theirs, mine)
            for index in range(src_count)
        ],
        axis=0,
    )
    strips = dot_pair(pair(strips), (we_ref[0], we_ref[1]))
    for side, near_row, far_row in ((0, other_row, row), (1, row, other_row)):
        for index, peer in enumerate(far_first + [src]):
            at = side * src_count + index
            hsend[at, :depth] = strips[at * depth : (at + 1) * depth]
            tall = depth if index < last - 1 else depth + 8
            if index >= last - 1:
                hsend[at, depth:] = tsend[last - index]
            send(
                hsend.at[at, :tall],
                hrecv.at[own_slot, :tall],
                halo_ss.at[at],
                halo_rs.at[own_slot],
                src_at=peer,
                tile_at=other_tile,
                row_at=far_row if index < last else near_row,
            )
    term_copy.wait_recv()
    own_terms = tsend[0] + trecv[0]
    pool_terms = tsend[1] + trecv[1]
    for index in range(src_count):
        gsend[index, local_x:] = pool_terms if index < last else own_terms
    for index, peer in enumerate(far_first + [src]):
        to(csend.at[index], crecv.at[index], core_ss.at[index], core_rs.at[index]).wait_recv()
        both = mine[index * local_x : (index + 1) * local_x] + crecv[index]
        gsend[index, :local_x] = both[:, :freqs]
        gsend[index, local_x : local_x + 1, :local_x] = both[:, freqs:].T[half : half + 1]
        if index < last:
            tall = local_x + (1 if index < last - 1 else 8)
            send(
                gsend.at[index, :tall],
                grecv.at[src, :tall],
                grad_ss.at[index],
                grad_rs.at[src],
                src_at=peer,
            )

    total = gsend[last]
    tail = total[local_x : local_x + 1]
    total = total[:local_x]
    for index, peer in enumerate(near_first):
        tall = local_x + (1 if index > 0 else 8)
        to(
            gsend.at[0, :tall],
            grecv.at[peer, :tall],
            grad_ss.at[0],
            grad_rs.at[peer],
            src_at=peer,
        ).wait_recv()
        total = total + grecv[peer, :local_x]
        tail = tail + grecv[peer, local_x : local_x + 1]
    tail = jnp.concatenate([tail, jnp.zeros((7, freqs), jnp.float32)], axis=0)
    grad_block = dot_pair(pair(total), wm, 1)
    grad_block = grad_block + tail.T[:local_x, :1] * quarter_wave[:1]
    low, high = grad_block[:, :freqs], grad_block[:, pixels - freqs :]

    packed = jnp.zeros((depth, freqs), jnp.float32)
    for index, peer in enumerate([src] + near_first):
        tall = depth if index > 1 else depth + 8
        for core in range(2):
            slot = peer * 2 + core
            to(
                hsend.at[0, :tall],
                hrecv.at[slot, :tall],
                halo_ss.at[0],
                halo_rs.at[slot],
                src_at=peer,
                tile_at=other_tile,
                row_at=core,
            ).wait_recv()
            packed = packed + hrecv[slot, :depth]
    strip = jnp.concatenate(
        [packed]
        + [pltpu.roll(packed, freqs - one * OV, axis=1) for one in range(1, fold)],
        axis=0,
    )
    from_below = jnp.where((lanes < OV) & (tile == 1), strip, 0.0)
    from_above = jnp.where(
        (lanes >= freqs - OV) & (tile == 0), pltpu.roll(strip, freqs - OV, axis=1), 0.0
    )
    out_ref[0, :, :freqs] = low + from_below
    out_ref[0, :, pixels - freqs :] = high + from_above
    terms = own_terms + grecv[pool_src, local_x:]
    for slot in (src * 2, src * 2 + 1, pool_src * 2, pool_src * 2 + 1):
        terms = terms + hrecv[slot, depth:]
    terms = terms / (sources * pixels * tile_count)
    terms_ref[...] = terms
    for copy in copies:
        copy.wait_send()


def finish_kernel(grads_ref, terms_ref, out_ref, sums_ref, held_ref, sems):
    copy = pltpu.make_async_copy(grads_ref, out_ref, sems.at[0])
    copy.start()
    for one in range(held_ref.shape[0]):
        held_ref[one] = jnp.sum(terms_ref[one + 1 : one + 2, :])
    other = pltpu.make_async_copy(held_ref, sums_ref, sems.at[1])
    other.start()
    copy.wait()
    other.wait()


def finish(grads, terms, shape):
    in_vmem = pl.BlockSpec(memory_space=pltpu.VMEM)
    in_hbm = pl.BlockSpec(memory_space=pltpu.HBM)
    return pl.pallas_call(
        finish_kernel,
        out_shape=(
            jax.ShapeDtypeStruct(grads.shape, grads.dtype),
            jax.ShapeDtypeStruct(shape, terms.dtype),
        ),
        in_specs=[in_vmem, in_vmem],
        out_specs=(in_hbm, in_hbm),
        scratch_shapes=[pltpu.SMEM(shape, terms.dtype), pltpu.SemaphoreType.DMA((2,))],
    )(*(pltpu.with_memory_space_constraint(one, pltpu.VMEM) for one in (grads, terms)))


def shards(mask_windows, target_windows, pupil_bands, pupil_phase, source_weight):
    src_count = lax.axis_size("src")
    tile_count = lax.axis_size("tile")
    row_count = lax.axis_size("row")
    local_x, pixels = mask_windows.shape[1:]
    per_device, freqs = pupil_phase.shape[:2]
    blocks = src_count * row_count
    fits = row_count == 2 and tile_count == 2 and src_count == 4 and 2 * per_device <= 8
    fits = fits and freqs == 128 and pixels == 2 * freqs and local_x == OV
    if not fits or local_x * blocks != pixels or OV * 4 != freqs:
        return shards_plain(
            mask_windows, target_windows, pupil_bands, pupil_phase, source_weight
        )
    half, fold = freqs // 2, freqs // OV
    tables = wave_constants(pixels, freqs, blocks, src_count, local_x, fold)
    bands = jnp.transpose(pupil_bands, (0, 2, 1))
    phases = pupil_phase.reshape(per_device, 2, half, freqs)
    in_vmem = pl.BlockSpec(memory_space=pltpu.VMEM)
    in_smem = pl.BlockSpec(memory_space=pltpu.SMEM)
    f32 = jnp.float32
    block = (local_x, pixels)
    dma = pltpu.SemaphoreType.DMA
    like = [pltpu.VMEM(one.shape, one.dtype) for one in tables]
    like[4] = pltpu.VMEM(tables[4].shape[1:], tables[4].dtype)
    like[5] = pltpu.VMEM(tables[5].shape[1:], tables[5].dtype)
    four = dma((src_count,))
    grads, terms = pl.pallas_call(
        functools.partial(kernel, src_count, tile_count),
        out_shape=(
            pltpu.VMEM(mask_windows.shape, f32),
            pltpu.VMEM((8, freqs), f32),
        ),
        in_specs=[pl.BlockSpec(memory_space=pltpu.HBM)] * 12,
        out_specs=(in_vmem, in_vmem),
        scratch_shapes=like
        + [
            pltpu.VMEM(mask_windows.shape, f32),
            pltpu.VMEM(target_windows.shape, f32),
            pltpu.VMEM(bands.shape, bands.dtype),
            pltpu.VMEM((2,) + phases.shape, f32),
            pltpu.SMEM(source_weight.shape, f32),
            dma((12,)),
            pltpu.VMEM((blocks, local_x + 8, freqs), f32),
            pltpu.VMEM((2, 2 * per_device, freqs, freqs), f32),
            pltpu.VMEM((2, 2 * per_device * local_x, 2 * pixels), f32),
            pltpu.VMEM((2, local_x, 2 * per_device * freqs), f32),
            pltpu.VMEM((2, 16, freqs), f32),
            pltpu.VMEM(block, f32),
            pltpu.VMEM((2,) + block, f32),
            pltpu.VMEM((2,) + block, f32),
            pltpu.VMEM((2, 8, freqs), f32),
            pltpu.VMEM((2, 8, freqs), f32),
            pltpu.VMEM((src_count,) + block, f32),
            pltpu.VMEM((src_count,) + block, f32),
            pltpu.VMEM((src_count, local_x + 8, freqs), f32),
            pltpu.VMEM((src_count, local_x + 8, freqs), f32),
            pltpu.VMEM((blocks, 16, freqs), f32),
            pltpu.VMEM((blocks, 16, freqs), f32),
        ]
        + [four] * 4
        + [dma(())] * 2
        + [dma((per_device,))] * 4
        + [dma(())] * 2
        + [dma((2,))] * 2
        + [dma((src_count + 1,))] * 2
        + [four] * 2
        + [dma((blocks,))] * 2
        + [pltpu.SemaphoreType.REGULAR] * 2
        + [pltpu.VMEM((freqs, 8), f32)],
        compiler_params=pltpu.CompilerParams(
            collective_id=0, has_side_effects=True, vmem_limit_bytes=63 * 1024 * 1024
        ),
    )(*tables, mask_windows, target_windows, bands, phases, source_weight)
    return finish(grads, terms, source_weight.shape)


def solution(mesh):
    return jax.shard_map(
        shards,
        mesh=mesh,
        in_specs=(
            P(("parts", "tile"), ("src", "row"), None),
            P(("parts", "tile"), ("src", "row"), None),
            P(("parts", "src"), None, None),
            P(("parts", "src"), None, None),
            P(("parts", "src")),
        ),
        out_specs=(P(("parts", "tile"), ("src", "row"), None), P(("parts", "src"))),
        check_vma=False,
    )
```
